32 devices in a mesh: dp: 8 (over z, x), ctx: 2 (over y), tp: 2 (over core).
Axes of the slice: x: 2, y: 2, z: 4, core: 2. Of those that a mesh axis runs over, the one named last changes fastest.
Arguments:
- inputs: bfloat16 [4096, 768], P(('dp', 'ctx')), may hold values from -6 to 6
- qkv_weight: bfloat16 [3, 768, 768], P(None, 'dp', 'tp'), may hold values from -0.21875 to 0.21875
- out_weight: bfloat16 [768, 768], P('tp', 'dp'), may hold values from -2.5 to 2.5
- up_weight: bfloat16 [768, 3072], P('dp', 'tp'), may hold values from -0.21875 to 0.21875
- down_weight: bfloat16 [3072, 768], P('tp', 'dp'), may hold values from -0.109375 to 0.109375
- norm_gains: bfloat16 [2, 768], P(None, 'dp'), may hold values from 0.099609375 to 1.8984375
- norm_biases: bfloat16 [2, 768], P(None, 'dp'), may hold values from -3 to 3
- lengths: int32 [8, 1], P('dp'), may hold values from 4 to 8, as said below
- random_blocks: int32 [64, 12, 3], P(('dp', 'ctx'), 'tp'), may hold values from 0 to 4095
- out_grad: bfloat16 [4096, 768], P(('dp', 'ctx')), may hold values from -6 to 6
Outputs:
- output: bfloat16 [4096, 768], P(('dp', 'ctx'))
- input_grad: bfloat16 [4096, 768], P(('dp', 'ctx'))
- qkv_grad: float32 [3, 768, 768], P(None, 'dp', 'tp')
- proj_grad: float32 [768, 768], P('tp', 'dp')
- up_grad: float32 [768, 3072], P('dp', 'tp')
- down_grad: float32 [3072, 768], P('tp', 'dp')
- gains_grad: float32 [2, 768], P(None, 'dp')
- biases_grad: float32 [2, 768], P(None, 'dp')
The draws below stay inside these ranges and needn't reach their ends.
Inputs may be any that keep to these rules, and one draw needn't show every extreme that they name: Each of a group's 1 sequence has 4 blocks or more, a group's lengths sum to 8, and the first group's first sequence has the most, 8 blocks.
All inputs are finite; a program needn't handle non-finite values.
Results may differ from the reference program's by a relative error of at most 0.02.
Values may be sent and summed in bfloat16 or wider, within the bound.
No kernel may reach another device: no remote copies, remote signals or barrier semaphores. Data moves between devices by JAX's collectives and lax.ppermute only.
A program may use at most 128 MiB of HBM per device.

```python
import math
import jax
import jax.numpy as jnp
from jax import lax

D = 768
HEADS = 12
HD = 64
FF = 3072
BLOCK = 64
RANDOM = 3
MIN_BLOCKS = 4
TOK_DEV = 256
TOKENS = 4096
GB = 8
SEQS = 1
NBLK = 64
GROUPS = 8
N_DP = 8
N_CTX = 2


def draw_lengths(key, part):
    weights_int = jax.random.randint(key, (GROUPS, SEQS), 1, 9)
    spare_blocks = GB - SEQS * MIN_BLOCKS
    shares = spare_blocks * weights_int // jnp.sum(weights_int, axis=1, keepdims=True)
    leftover = spare_blocks - jnp.sum(shares, axis=1)
    shares = shares.at[:, 0].add(leftover)
    drawn = MIN_BLOCKS + shares
    longest = jnp.full((SEQS,), MIN_BLOCKS, jnp.int32).at[0].set(GB - (SEQS - 1) * MIN_BLOCKS)
    drawn = drawn.at[0].set(longest)
    return drawn.astype(jnp.int32)


def place_ends(values, own_key, least, largest):
    index_at = [jax.random.randint(jax.random.fold_in(own_key, axis), (), 0, length) for axis, length in enumerate(values.shape)]
    main_axis = values.shape.index(max(values.shape))
    beside = index_at[:main_axis] + [(index_at[main_axis] + 1) % values.shape[main_axis]] + index_at[main_axis + 1:]
    return values.at[tuple(index_at)].set(least).at[tuple(beside)].set(largest)


def steps_of(own_key, dims, split, smallest, largest):
    loudness = 1.0
    for dim, parts in split:
        steps = jax.random.uniform(jax.random.fold_in(jax.random.fold_in(own_key, 6), dim), (parts,), jnp.float32, smallest / len(split), largest / len(split))
        loudness = loudness * jnp.repeat(jnp.exp(steps), dims[dim] // parts).reshape((-1,) + (1,) * (len(dims) - 1 - dim))
    return loudness


def gaussian(stream_key, dims, scale, reach, cuts=(), held_as=jnp.bfloat16):
    level = steps_of(stream_key, dims, cuts, -0.22, 0.18) if cuts else 1.0
    values = jax.random.normal(stream_key, dims, jnp.float32) * scale * level
    return jnp.minimum(jnp.maximum(values, -reach), reach).astype(held_as)


def setup_inputs(seed: int = 0) -> dict:
    streams_of = jax.random.split(jax.random.key(seed), 11)
    return {
        "inputs": gaussian(streams_of[0], (TOKENS, D), 1.0, 6.0, ((0, 16),)),
        "qkv_weight": gaussian(streams_of[1], (3, D, D), D ** -0.5, 0.21875, ((1, 8), (2, 2))),
        "out_weight": gaussian(streams_of[2], (D, D), (max(D // 128, 1)) ** -0.5, 2.5, ((0, 2), (1, 8))),
        "up_weight": gaussian(streams_of[3], (D, FF), D ** -0.5, 0.21875, ((0, 8), (1, 2))),
        "down_weight": gaussian(streams_of[4], (FF, D), FF ** -0.5, 0.109375, ((0, 2), (1, 8))),
        "norm_gains": jnp.clip(1.0 + 0.18 * jax.random.normal(streams_of[5], (2, D), jnp.float32), 0.099609375, 1.8984375).astype(jnp.bfloat16),
        "norm_biases": gaussian(streams_of[6], (2, D), 0.5, 3.0, ((1, 8),)),
        "lengths": draw_lengths(jax.random.fold_in(streams_of[10], 71), 0),
        "random_blocks": place_ends(jax.random.randint(streams_of[8], (NBLK, HEADS, RANDOM), 0, 4096), jax.random.fold_in(streams_of[8], 1), 0, 4095).astype(jnp.int32),
        "out_grad": gaussian(streams_of[9], (TOKENS, D), 1.0, 6.0, ((0, 16),)),
    }


@jax.custom_vjp
def low(v):
    return lax.optimization_barrier(v.astype(jnp.bfloat16)).astype(jnp.float32)

@jax.custom_vjp
def low_back(v):
    return v

def low_keep(v):
    return (low(v), None)

def low_pass(kept, grad):
    return (grad,)

def back_keep(v):
    return (v, None)

def back_low(kept, grad):
    return (low(grad),)
low.defvjp(low_keep, low_pass)
low_back.defvjp(back_keep, back_low)
eps = 1e-06

def both_round(values):
    return low(low_back(values))

def layer_norm(values, gain, shift):
    row_mean = lax.optimization_barrier(jnp.mean(values, axis=-1, keepdims=True))
    centred = values - row_mean
    spread = lax.optimization_barrier(jnp.mean(centred * centred, axis=-1, keepdims=True))
    return centred * lax.rsqrt(spread + eps) * gain + shift

def gelu_tanh(values):
    return jax.nn.gelu(values, approximate=True)

def exact_dot(left, right):
    return jnp.dot(left, right, precision=lax.Precision.HIGHEST)

def block_table(blocks, lengths_row, offsets):
    seq_ends = jnp.cumsum(lengths_row).astype(jnp.int32)
    starts = seq_ends - lengths_row
    inside = ((blocks[:, None] >= starts[None, :]) & (blocks[:, None] < seq_ends[None, :])).astype(jnp.int32)
    seq_first = lax.optimization_barrier(jnp.sum(inside * starts[None, :], axis=1)).astype(jnp.int32)
    seq_count = lax.optimization_barrier(jnp.sum(inside * lengths_row[None, :], axis=1)).astype(jnp.int32)
    position = blocks - seq_first
    has_before = position > 0
    has_behind = position < seq_count - 1
    before = jnp.where(has_before, blocks - 1, blocks)
    behind = jnp.where(has_behind, blocks + 1, blocks)
    fixed_ids = jnp.stack([before, blocks, behind, seq_first, seq_first + 1], axis=-1)
    random_ids = seq_first[:, None, None] + offsets % seq_count[:, None, None]
    head_count = offsets.shape[1]
    key_table = jnp.concatenate([jnp.broadcast_to(fixed_ids[:, None, :], (blocks.shape[0], head_count, 5)), random_ids], axis=-1).astype(jnp.int32)
    always = jnp.ones_like(has_before)
    usable = jnp.stack([has_before, always, has_behind, always, always] + [always] * offsets.shape[2], axis=-1)
    return (key_table, usable)

def group_forward(lengths_row, random_group):
    group_blocks = random_group.shape[0]
    blocks = jnp.arange(group_blocks, dtype=jnp.int32)
    key_table, usable = block_table(blocks, lengths_row.astype(jnp.int32), random_group.astype(jnp.int32))
    step = math.gcd(group_blocks, 8)
    head_pick = jnp.arange(HEADS, dtype=jnp.int32)[None, :, None]
    scale = 1.0 / math.sqrt(HD)
    slots = key_table.shape[2]

    def forward(x_float, w_qkv, w_out, w_up, w_down, gains, biases):
        query = both_round(exact_dot(x_float, w_qkv[0]))
        keys = both_round(exact_dot(x_float, w_qkv[1]))
        values = both_round(exact_dot(x_float, w_qkv[2]))
        key_blocks = keys.reshape(group_blocks, BLOCK, HEADS, HD)
        value_blocks = values.reshape(group_blocks, BLOCK, HEADS, HD)
        query_blocks = query.reshape(group_blocks // step, step, BLOCK, HEADS, HD)
        tables = key_table.reshape(group_blocks // step, step, HEADS, slots)
        usables = usable.reshape(group_blocks // step, step, slots)

        def attend(piece):
            query_part, table_part, usable_part = piece
            key_sel = key_blocks[table_part, :, head_pick, :]
            value_sel = value_blocks[table_part, :, head_pick, :]
            raw = jnp.einsum('bqhd,bhkcd->bhqkc', query_part, key_sel, precision=lax.Precision.HIGHEST)
            scores = jnp.where(usable_part[:, None, None, :, None], low_back(raw) * scale, -1e+30)
            top = lax.optimization_barrier(jnp.max(scores, axis=(3, 4), keepdims=True))
            log_total = top + jnp.log(lax.optimization_barrier(jnp.sum(jnp.exp(scores - top), axis=(3, 4), keepdims=True)))
            probs = jnp.exp(scores - log_total)
            return jnp.einsum('bhqkc,bhkcd->bqhd', low(probs), value_sel, precision=lax.Precision.HIGHEST)
        attended = lax.map(jax.checkpoint(attend), (query_blocks, tables, usables))
        attended = both_round(attended.reshape(group_blocks * BLOCK, HEADS * HD))
        attn_out = low_back(exact_dot(attended, w_out))
        normed = layer_norm(x_float + attn_out, gains[0], biases[0])
        hidden = low_back(exact_dot(low(normed), w_up))
        mlp_out = low_back(exact_dot(low(gelu_tanh(hidden)), w_down))
        return layer_norm(normed + mlp_out, gains[1], biases[1])
    return forward

def reference(inputs, qkv_weight, out_weight, up_weight, down_weight, norm_gains, norm_biases, lengths, random_blocks, out_grad):
    group_rows = TOK_DEV * N_CTX
    group_blocks = group_rows // BLOCK
    weights = tuple((weight.astype(jnp.float32) for weight in (qkv_weight, out_weight, up_weight, down_weight, norm_gains, norm_biases)))
    x_groups = inputs.astype(jnp.float32).reshape(N_DP, group_rows, D)
    grad_groups = out_grad.astype(jnp.float32).reshape(N_DP, group_rows, D)
    random_groups = random_blocks.reshape(N_DP, group_blocks, HEADS, RANDOM)

    def one_group(running, piece):
        x_part, grad_part, lengths_row, random_part = piece
        forward = group_forward(lengths_row, random_part)
        result, pull = jax.vjp(forward, x_part, *weights)
        fresh = pull(grad_part)
        running = tuple((summed + added for summed, added in zip(running, fresh[1:])))
        return (running, (result.astype(jnp.bfloat16), fresh[0].astype(jnp.bfloat16)))
    zeros = tuple((jnp.zeros(weight.shape, jnp.float32) for weight in weights))
    totals, outputs = lax.scan(one_group, zeros, (x_groups, grad_groups, lengths, random_groups))
    results, input_grads = outputs
    return (results.reshape(TOKENS, D), input_grads.reshape(TOKENS, D), totals[0], totals[1], totals[2], totals[3], totals[4], totals[5])
```

```python
import functools
import math

import jax
import jax.numpy as jnp
from jax import lax
from jax.sharding import PartitionSpec as P

HD = 64
BLOCK = 64


eps = 1e-06


def layer_norm(values, gain, shift):
    row_mean = jnp.mean(values, axis=-1, keepdims=True)
    centred = values - row_mean
    spread = jnp.mean(centred * centred, axis=-1, keepdims=True)
    return centred * lax.rsqrt(spread + eps) * gain + shift


def gelu_tanh(values):
    return jax.nn.gelu(values, approximate=True)


def contract(form, left, right):
    return jnp.einsum(form, left, right, preferred_element_type=jnp.float32)


def block_table(blocks, lengths_row, offsets):
    seq_ends = jnp.cumsum(lengths_row)
    starts = seq_ends - lengths_row
    inside = ((blocks[:, None] >= starts[None, :]) & (blocks[:, None] < seq_ends[None, :])).astype(
        jnp.int32
    )
    seq_first = jnp.sum(inside * starts[None, :], axis=1)
    seq_count = jnp.sum(inside * lengths_row[None, :], axis=1)
    position = blocks - seq_first
    has_before = position > 0
    has_behind = position < seq_count - 1
    before = jnp.where(has_before, blocks - 1, blocks)
    behind = jnp.where(has_behind, blocks + 1, blocks)
    fixed_ids = jnp.stack([before, blocks, behind, seq_first, seq_first + 1], axis=-1)
    random_ids = seq_first[:, None, None] + offsets % seq_count[:, None, None]
    head_count = offsets.shape[1]
    key_table = jnp.concatenate(
        [jnp.broadcast_to(fixed_ids[:, None, :], (blocks.shape[0], head_count, 5)), random_ids],
        axis=-1,
    )
    always = jnp.ones_like(has_before)
    usable = jnp.stack(
        [has_before, always, has_behind, always, always] + [always] * offsets.shape[2], axis=-1
    )
    return (key_table, usable)


def scores_of(query, key_sel, usable, scale):
    raw = contract("bqhd,bhkcd->bhqkc", query, key_sel)
    return jnp.where(usable[:, None, None, :, None], raw * scale, -1e30)


def per_device(
    inputs,
    qkv_weight,
    out_weight,
    up_weight,
    down_weight,
    norm_gains,
    norm_biases,
    lengths,
    random_blocks,
    out_grad,
):
    w_qkv, w_out, w_up, w_down, gains_low, biases_low = (
        lax.all_gather(qkv_weight, "dp", axis=1, tiled=True),
        lax.all_gather(out_weight, "dp", axis=1, tiled=True),
        lax.all_gather(up_weight, "dp", axis=0, tiled=True),
        lax.all_gather(down_weight, "dp", axis=1, tiled=True),
        lax.all_gather(norm_gains, "dp", axis=1, tiled=True),
        lax.all_gather(norm_biases, "dp", axis=1, tiled=True),
    )
    gains = gains_low.astype(jnp.float32)
    biases = biases_low.astype(jnp.float32)
    rows = inputs.shape[0]
    own_blocks = rows // BLOCK
    local_width = w_qkv.shape[2]
    local_heads = local_width // HD
    scale = 1.0 / math.sqrt(HD)
    x_float = inputs.astype(jnp.float32)
    projected = contract("td,kde->kte", inputs, w_qkv)
    q_low = projected[0].astype(jnp.bfloat16)
    k_low = projected[1].astype(jnp.bfloat16)
    v_low = projected[2].astype(jnp.bfloat16)
    key_all, value_all = (
        lax.all_gather(k_low, "ctx", axis=0, tiled=True),
        lax.all_gather(v_low, "ctx", axis=0, tiled=True),
    )
    group_blocks = key_all.shape[0] // BLOCK
    first_block = lax.axis_index("ctx") * own_blocks
    blocks = first_block + jnp.arange(own_blocks, dtype=jnp.int32)
    key_table, usable = block_table(blocks, lengths[0], random_blocks)
    head_pick = jnp.arange(local_heads, dtype=jnp.int32)[None, :, None]
    key_blocks = key_all.reshape(group_blocks, BLOCK, local_heads, HD)
    value_blocks = value_all.reshape(group_blocks, BLOCK, local_heads, HD)
    key_sel = key_blocks[key_table, :, head_pick, :]
    value_sel = value_blocks[key_table, :, head_pick, :]
    query = q_low.reshape(own_blocks, BLOCK, local_heads, HD)
    scores = scores_of(query, key_sel, usable, scale)
    top = jnp.max(scores, axis=(3, 4), keepdims=True)
    log_total = top + jnp.log(jnp.sum(jnp.exp(scores - top), axis=(3, 4), keepdims=True))
    probs = jnp.exp(scores - log_total)
    probs_low = probs.astype(jnp.bfloat16)
    attended = (
        contract("bhqkc,bhkcd->bqhd", probs_low, value_sel)
        .reshape(rows, local_width)
        .astype(jnp.bfloat16)
    )
    attn_sum = lax.psum(
        jnp.dot(attended, w_out, preferred_element_type=jnp.float32).astype(jnp.bfloat16), "tp"
    ).astype(jnp.float32)
    first_sum = x_float + attn_sum
    normed, norm_pull = jax.vjp(layer_norm, first_sum, gains[0], biases[0])
    normed_low = normed.astype(jnp.bfloat16)
    hidden = jnp.dot(normed_low, w_up, preferred_element_type=jnp.float32)
    activated, gelu_pull = jax.vjp(gelu_tanh, hidden)
    act_low = activated.astype(jnp.bfloat16)
    mlp_sum = lax.psum(
        jnp.dot(act_low, w_down, preferred_element_type=jnp.float32).astype(jnp.bfloat16), "tp"
    ).astype(jnp.float32)
    second_sum = normed + mlp_sum
    result, final_pull = jax.vjp(layer_norm, second_sum, gains[1], biases[1])
    d_second, d_gain_two, d_bias_two = final_pull(out_grad.astype(jnp.float32))
    d_mlp = d_second.astype(jnp.bfloat16)
    grad_down = contract("tf,td->fd", act_low, d_mlp)
    d_act = contract("td,fd->tf", d_mlp, w_down)
    d_hidden = gelu_pull(d_act)[0].astype(jnp.bfloat16)
    grad_up = contract("td,tf->df", normed_low, d_hidden)
    d_normed = d_second + lax.psum(
        contract("tf,df->td", d_hidden, w_up).astype(jnp.bfloat16), "tp"
    ).astype(jnp.float32)
    d_first, d_gain_one, d_bias_one = norm_pull(d_normed)
    d_attn = d_first.astype(jnp.bfloat16)
    grad_proj = contract("te,td->ed", attended, d_attn)
    d_attended = (
        contract("td,ed->te", d_attn, w_out)
        .astype(jnp.bfloat16)
        .reshape(own_blocks, BLOCK, local_heads, HD)
    )
    scores = scores_of(query, key_sel, usable, scale)
    probs = jnp.exp(scores - log_total)
    probs_low = probs.astype(jnp.bfloat16)
    d_probs = contract("bqhd,bhkcd->bhqkc", d_attended, value_sel)
    d_scores = probs * (d_probs - jnp.sum(probs * d_probs, axis=(3, 4), keepdims=True))
    d_raw = (d_scores * scale).astype(jnp.bfloat16)
    d_query = (
        contract("bhqkc,bhkcd->bqhd", d_raw, key_sel)
        .reshape(rows, local_width)
        .astype(jnp.bfloat16)
    )
    d_key_sel = contract("bhqkc,bqhd->bhkcd", d_raw, query)
    d_value_sel = contract("bhqkc,bqhd->bhkcd", probs_low, d_attended)
    empty = jnp.zeros((group_blocks, BLOCK, local_heads, HD), jnp.float32)
    d_key_all = (
        empty.at[key_table, :, head_pick, :]
        .add(d_key_sel)
        .reshape(group_blocks * BLOCK, local_width)
    )
    d_value_all = (
        empty.at[key_table, :, head_pick, :]
        .add(d_value_sel)
        .reshape(group_blocks * BLOCK, local_width)
    )
    d_key, d_value = (
        lax.psum_scatter(
            d_key_all.astype(jnp.bfloat16), "ctx", scatter_dimension=0, tiled=True
        ).astype(jnp.float32),
        lax.psum_scatter(
            d_value_all.astype(jnp.bfloat16), "ctx", scatter_dimension=0, tiled=True
        ).astype(jnp.float32),
    )
    d_projected = jnp.stack([d_query, d_key.astype(jnp.bfloat16), d_value.astype(jnp.bfloat16)])
    grad_qkv = contract("td,kte->kde", inputs, d_projected)
    d_inputs = d_first + lax.psum(
        contract("kte,kde->td", d_projected, w_qkv).astype(jnp.bfloat16), "tp"
    ).astype(jnp.float32)
    grad_gains = jnp.stack([d_gain_one, d_gain_two])
    grad_biases = jnp.stack([d_bias_one, d_bias_two])
    shared = (
        lax.psum_scatter(
            grad_qkv.astype(jnp.bfloat16), "dp", scatter_dimension=1, tiled=True
        ).astype(jnp.float32),
        lax.psum_scatter(
            grad_proj.astype(jnp.bfloat16), "dp", scatter_dimension=1, tiled=True
        ).astype(jnp.float32),
        lax.psum_scatter(
            grad_up.astype(jnp.bfloat16), "dp", scatter_dimension=0, tiled=True
        ).astype(jnp.float32),
        lax.psum_scatter(
            grad_down.astype(jnp.bfloat16), "dp", scatter_dimension=1, tiled=True
        ).astype(jnp.float32),
        lax.psum_scatter(
            grad_gains.astype(jnp.bfloat16), "dp", scatter_dimension=1, tiled=True
        ).astype(jnp.float32),
        lax.psum_scatter(
            grad_biases.astype(jnp.bfloat16), "dp", scatter_dimension=1, tiled=True
        ).astype(jnp.float32),
    )
    totals = (
        lax.psum(shared[0].astype(jnp.bfloat16), "ctx").astype(jnp.float32),
        lax.psum(shared[1].astype(jnp.bfloat16), "ctx").astype(jnp.float32),
        lax.psum(shared[2].astype(jnp.bfloat16), "ctx").astype(jnp.float32),
        lax.psum(shared[3].astype(jnp.bfloat16), "ctx").astype(jnp.float32),
        lax.psum(shared[4].astype(jnp.bfloat16), "ctx").astype(jnp.float32),
        lax.psum(shared[5].astype(jnp.bfloat16), "ctx").astype(jnp.float32),
    )
    return (
        result.astype(jnp.bfloat16),
        d_inputs.astype(jnp.bfloat16),
        totals[0],
        totals[1],
        totals[2],
        totals[3],
        totals[4],
        totals[5],
    )


def rows_device(
    dims,
    inputs,
    qkv_weight,
    out_weight,
    up_weight,
    down_weight,
    norm_gains,
    norm_biases,
    lengths,
    random_blocks,
    out_grad,
):
    n_dp = dims["dp"]
    n_out = n_dp // 2
    dp = lax.axis_index("dp")
    c = lax.axis_index("ctx")
    t = lax.axis_index("tp")
    z = dp // 2
    x = dp % 2
    f32, bf16 = jnp.float32, jnp.bfloat16
    pair = [(0, 1), (1, 0)]
    across_x = [(i, i ^ 1) for i in range(n_dp)]

    def across_z(s):
        return [(i, ((i // 2 + s) % n_out) * 2 + i % 2) for i in range(n_dp)]

    def swap_tp(v):
        return lax.ppermute(v, "tp", pair)

    def swap_ctx(v):
        return lax.ppermute(v, "ctx", pair)

    def gather_dp(v):
        near = [v] + [lax.ppermute(v, "dp", across_z(s)) for s in range(1, n_out)]
        far = [lax.ppermute(p, "dp", across_x) for p in near]
        order = [0] + [n_out - s for s in range(1, n_out)]
        near = jnp.stack([near[s] for s in order])
        far = jnp.stack([far[s] for s in order])
        both = jnp.stack([jnp.where(x == 0, near, far), jnp.where(x == 0, far, near)], axis=1)
        both = jnp.roll(both, z, axis=0)
        return both.reshape(n_dp * v.shape[0], v.shape[1])

    def scatter_dp(g):
        rows = g.shape[0] // n_dp
        g = g.astype(bf16).reshape(n_out, 2, rows, g.shape[1])
        away = lax.dynamic_index_in_dim(g, 1 - x, 1, False)
        own = lax.dynamic_index_in_dim(g, x, 1, False)
        half = (own.astype(f32) + lax.ppermute(away, "dp", across_x).astype(f32)).astype(bf16)
        total = lax.dynamic_index_in_dim(half, z, 0, False).astype(f32)
        for s in range(1, n_out):
            piece = lax.dynamic_index_in_dim(half, (z + s) % n_out, 0, False)
            total = total + lax.ppermute(piece, "dp", across_z(s)).astype(f32)
        return total.astype(bf16)

    rows = inputs.shape[0]
    part = rows // 2
    width = inputs.shape[1]
    shard = qkv_weight.shape[1]
    cols = qkv_weight.shape[2] // 2
    units = up_weight.shape[1] // 2
    heads = cols // HD
    own_blocks = rows // BLOCK
    per = own_blocks // 2

    def own_cols(w):
        n = w.shape[-1] // 2
        return lax.dynamic_slice_in_dim(w, c * n, n, w.ndim - 1)

    small = jnp.concatenate([norm_gains, norm_biases], axis=0)
    w1 = jnp.concatenate(
        [own_cols(qkv_weight[0]), own_cols(qkv_weight[1]), own_cols(qkv_weight[2]), jnp.pad(small.T, ((0, 0), (0, 60)))],
        axis=1,
    )
    w_out_t = own_cols(out_weight.T)
    w_up = own_cols(up_weight)
    w_down_t = own_cols(down_weight.T)
    w1 = gather_dp(w1)
    w_out_t = gather_dp(w_out_t)
    w_up = gather_dp(w_up)
    w_down_t = gather_dp(w_down_t)
    w_qkv = w1[:, : 3 * cols]
    vecs = w1[:, 3 * cols : 3 * cols + 4].T.astype(f32)

    def gather_rows(v):
        halves = v.reshape(2, part, v.shape[1])
        near = swap_ctx(lax.dynamic_index_in_dim(halves, t, 0, False))
        far = swap_tp(near)
        other = jnp.where(t == 0, jnp.stack([near, far]), jnp.stack([far, near]))
        return jnp.where(c == 0, jnp.stack([halves, other], 1), jnp.stack([other, halves], 1)).reshape(4 * part, v.shape[1])

    x_all = gather_rows(inputs)
    e_own = lax.dynamic_index_in_dim(out_grad.reshape(2, part, width), t, 0, False)
    e_far = swap_ctx(e_own)
    e_mine = jnp.where(c == 0, jnp.concatenate([e_own, e_far]), jnp.concatenate([e_far, e_own])).astype(f32)

    picks = random_blocks.reshape(own_blocks, 2, heads, 3)
    picks_own = lax.dynamic_index_in_dim(picks, c, 1, False)
    picks_far = swap_ctx(lax.dynamic_index_in_dim(picks, 1 - c, 1, False))
    picks = jnp.where(c == 0, jnp.concatenate([picks_own, picks_far]), jnp.concatenate([picks_far, picks_own]))
    blocks = jnp.arange(2 * own_blocks, dtype=jnp.int32)
    table, usable = block_table(blocks, lengths[0], picks)
    named = (table[..., None] == blocks) & usable[:, None, :, None]
    counts = jnp.sum(named.astype(f32), axis=2)
    order = [cc * own_blocks + tt * per + i for tt in range(2) for cc in range(2) for i in range(per)]
    order = jnp.array(order)
    counts = counts[order][:, :, order]
    bias = jnp.where(counts > 0, jnp.log(jnp.maximum(counts, 1.0)), -1e30)
    bias = jnp.repeat(jnp.repeat(bias.transpose(1, 0, 2), BLOCK, 1), BLOCK, 2)
    scale = 1.0 / math.sqrt(HD)

    qkv = jnp.dot(x_all, w_qkv, preferred_element_type=f32).astype(bf16)
    q, k, v = [qkv[:, i * cols : (i + 1) * cols].reshape(-1, heads, HD) for i in range(3)]
    scores = contract("qhd,khd->hqk", q, k) * scale + bias
    top = jnp.max(scores, axis=2, keepdims=True)
    log_total = top + jnp.log(jnp.sum(jnp.exp(scores - top), axis=2, keepdims=True))
    probs = jnp.exp(scores - log_total)
    o = contract("hqk,khd->qhd", probs.astype(bf16), v).reshape(-1, cols).astype(bf16)

    def mine(s):
        return lax.dynamic_index_in_dim(s.reshape(2, s.shape[0] // 2, s.shape[1]), t, 0, False)

    def theirs(s):
        return lax.dynamic_index_in_dim(s.reshape(2, s.shape[0] // 2, s.shape[1]), 1 - t, 0, False)

    def sum_row(s):
        s = s.astype(bf16)
        s = (mine(s).astype(f32) + swap_tp(theirs(s)).astype(f32)).astype(bf16)
        return s.astype(f32) + swap_ctx(s).astype(f32)

    def spread(s):
        far = swap_tp(s)
        return jnp.where(t == 0, jnp.concatenate([s, far]), jnp.concatenate([far, s]))

    a = sum_row(contract("te,de->td", o, w_out_t))
    y1, norm_pull = jax.vjp(layer_norm, mine(x_all).astype(f32) + a, vecs[0], vecs[2])
    y1_low = spread(y1.astype(bf16))
    hid = jnp.dot(y1_low, w_up, preferred_element_type=f32)
    act, gelu_pull = jax.vjp(gelu_tanh, hid)
    u = act.astype(bf16)
    m = sum_row(contract("tf,df->td", u, w_down_t))
    result, final_pull = jax.vjp(layer_norm, y1 + m, vecs[1], vecs[3])
    dz2, dg2, dc2 = final_pull(e_mine)
    dm = spread(dz2.astype(bf16))

    def keep(s):
        near = lax.dynamic_index_in_dim(s.reshape(2, part, s.shape[1]), c, 0, False)
        far = swap_tp(near)
        return jnp.where(t == 0, jnp.concatenate([near, far]), jnp.concatenate([far, near]))

    output = keep(result.astype(bf16))
    grad_down_t = contract("td,tf->df", dm, u)
    du = jnp.dot(dm, w_down_t, preferred_element_type=f32)
    dhid = gelu_pull(du)[0].astype(bf16)
    grad_up = contract("td,tf->df", y1_low, dhid)
    dy1 = dz2 + sum_row(contract("tf,df->td", dhid, w_up))
    dz1, dg1, dc1 = norm_pull(dy1)
    da = spread(dz1.astype(bf16))
    grad_out_t = contract("td,te->de", da, o)
    do = jnp.dot(da, w_out_t, preferred_element_type=f32).astype(bf16).reshape(-1, heads, HD)
    dp_ = contract("qhd,khd->hqk", do, v)
    ds = probs * (dp_ - jnp.sum(probs * dp_, axis=2, keepdims=True))
    dr = (ds * scale).astype(bf16)
    dq = contract("hqk,khd->qhd", dr, k).astype(bf16)
    dk = contract("hqk,qhd->khd", dr, q).astype(bf16)
    dv = contract("hqk,qhd->khd", probs.astype(bf16), do).astype(bf16)
    dqkv = jnp.concatenate([g.reshape(-1, cols) for g in (dq, dk, dv)], axis=1)
    grad_qkv = contract("td,te->de", x_all, dqkv)
    vec_grads = jnp.stack([dg1, dg2, dc1, dc2])
    vec_grads = vec_grads + swap_tp(vec_grads)
    grad_1 = jnp.concatenate([grad_qkv, jnp.pad(vec_grads.T, ((0, 0), (0, 60)))], axis=1)
    dx = contract("te,de->td", dqkv, w_qkv).astype(bf16)
    dx = (mine(dx).astype(f32) + swap_tp(theirs(dx)).astype(f32)).astype(bf16).reshape(2, part, width)
    dx_own = lax.dynamic_index_in_dim(dx, c, 0, False).astype(f32)
    dx_far = swap_ctx(lax.dynamic_index_in_dim(dx, 1 - c, 0, False)).astype(f32)
    dz1_own = lax.dynamic_index_in_dim(dz1.reshape(2, part, width), c, 0, False)
    dx = (dz1_own + dx_own + dx_far).astype(bf16)
    dx_tp = swap_tp(dx)
    input_grad = jnp.where(t == 0, jnp.concatenate([dx, dx_tp]), jnp.concatenate([dx_tp, dx]))

    def both_ctx(g):
        far = swap_ctx(g)
        return jnp.where(c == 0, jnp.concatenate([g, far], 1), jnp.concatenate([far, g], 1))

    grad_down = both_ctx(scatter_dp(grad_down_t)).astype(f32).T
    grad_up = both_ctx(scatter_dp(grad_up)).astype(f32)
    grad_out = both_ctx(scatter_dp(grad_out_t)).astype(f32).T
    grad_1 = scatter_dp(grad_1)
    far_1 = swap_ctx(grad_1)
    lo = jnp.where(c == 0, grad_1, far_1).astype(f32)
    hi = jnp.where(c == 0, far_1, grad_1).astype(f32)
    grad_qkv = jnp.stack(
        [jnp.concatenate([lo[:, i * cols : (i + 1) * cols], hi[:, i * cols : (i + 1) * cols]], 1) for i in range(3)]
    )
    vec = grad_1[:, 3 * cols : 3 * cols + 4].astype(f32).T
    return (output, input_grad, grad_qkv, grad_out, grad_up, grad_down, vec[:2], vec[2:])


def solution(mesh):
    dims = dict(mesh.shape)
    fast = dims["ctx"] == 2 and dims["tp"] == 2 and dims["dp"] % 2 == 0
    step = functools.partial(rows_device, dims) if fast else per_device
    return jax.shard_map(
        step,
        mesh=mesh,
        in_specs=(
            P(("dp", "ctx"), None),
            P(None, "dp", "tp"),
            P("tp", "dp"),
            P("dp", "tp"),
            P("tp", "dp"),
            P(None, "dp"),
            P(None, "dp"),
            P("dp", None),
            P(("dp", "ctx"), "tp", None),
            P(("dp", "ctx"), None),
        ),
        out_specs=(
            P(("dp", "ctx"), None),
            P(("dp", "ctx"), None),
            P(None, "dp", "tp"),
            P("tp", "dp"),
            P("dp", "tp"),
            P("tp", "dp"),
            P(None, "dp"),
            P(None, "dp"),
        ),
        check_vma=False,
    )
```

```python
import functools
import math

import jax
import jax.numpy as jnp
from jax import lax
from jax.experimental import pallas as pl
from jax.experimental.pallas import tpu as pltpu
from jax.sharding import PartitionSpec as P

HD = 64
BLOCK = 64


eps = 1e-06


def layer_norm(values, gain, shift):
    row_mean = jnp.mean(values, axis=-1, keepdims=True)
    centred = values - row_mean
    spread = jnp.mean(centred * centred, axis=-1, keepdims=True)
    return centred * lax.rsqrt(spread + eps) * gain + shift


def gelu_tanh(values):
    return jax.nn.gelu(values, approximate=True)


def contract(form, left, right):
    return jnp.einsum(form, left, right, preferred_element_type=jnp.float32)


def block_table(blocks, lengths_row, offsets):
    seq_ends = jnp.cumsum(lengths_row)
    starts = seq_ends - lengths_row
    inside = ((blocks[:, None] >= starts[None, :]) & (blocks[:, None] < seq_ends[None, :])).astype(
        jnp.int32
    )
    seq_first = jnp.sum(inside * starts[None, :], axis=1)
    seq_count = jnp.sum(inside * lengths_row[None, :], axis=1)
    position = blocks - seq_first
    has_before = position > 0
    has_behind = position < seq_count - 1
    before = jnp.where(has_before, blocks - 1, blocks)
    behind = jnp.where(has_behind, blocks + 1, blocks)
    fixed_ids = jnp.stack([before, blocks, behind, seq_first, seq_first + 1], axis=-1)
    random_ids = seq_first[:, None, None] + offsets % seq_count[:, None, None]
    head_count = offsets.shape[1]
    key_table = jnp.concatenate(
        [jnp.broadcast_to(fixed_ids[:, None, :], (blocks.shape[0], head_count, 5)), random_ids],
        axis=-1,
    )
    always = jnp.ones_like(has_before)
    usable = jnp.stack(
        [has_before, always, has_behind, always, always] + [always] * offsets.shape[2], axis=-1
    )
    return (key_table, usable)


def scores_of(query, key_sel, usable, scale):
    raw = contract("bqhd,bhkcd->bhqkc", query, key_sel)
    return jnp.where(usable[:, None, None, :, None], raw * scale, -1e30)


def per_device(
    inputs,
    qkv_weight,
    out_weight,
    up_weight,
    down_weight,
    norm_gains,
    norm_biases,
    lengths,
    random_blocks,
    out_grad,
):
    w_qkv, w_out, w_up, w_down, gains_low, biases_low = (
        lax.all_gather(qkv_weight, "dp", axis=1, tiled=True),
        lax.all_gather(out_weight, "dp", axis=1, tiled=True),
        lax.all_gather(up_weight, "dp", axis=0, tiled=True),
        lax.all_gather(down_weight, "dp", axis=1, tiled=True),
        lax.all_gather(norm_gains, "dp", axis=1, tiled=True),
        lax.all_gather(norm_biases, "dp", axis=1, tiled=True),
    )
    gains = gains_low.astype(jnp.float32)
    biases = biases_low.astype(jnp.float32)
    rows = inputs.shape[0]
    own_blocks = rows // BLOCK
    local_width = w_qkv.shape[2]
    local_heads = local_width // HD
    scale = 1.0 / math.sqrt(HD)
    x_float = inputs.astype(jnp.float32)
    projected = contract("td,kde->kte", inputs, w_qkv)
    q_low = projected[0].astype(jnp.bfloat16)
    k_low = projected[1].astype(jnp.bfloat16)
    v_low = projected[2].astype(jnp.bfloat16)
    key_all, value_all = (
        lax.all_gather(k_low, "ctx", axis=0, tiled=True),
        lax.all_gather(v_low, "ctx", axis=0, tiled=True),
    )
    group_blocks = key_all.shape[0] // BLOCK
    first_block = lax.axis_index("ctx") * own_blocks
    blocks = first_block + jnp.arange(own_blocks, dtype=jnp.int32)
    key_table, usable = block_table(blocks, lengths[0], random_blocks)
    head_pick = jnp.arange(local_heads, dtype=jnp.int32)[None, :, None]
    key_blocks = key_all.reshape(group_blocks, BLOCK, local_heads, HD)
    value_blocks = value_all.reshape(group_blocks, BLOCK, local_heads, HD)
    key_sel = key_blocks[key_table, :, head_pick, :]
    value_sel = value_blocks[key_table, :, head_pick, :]
    query = q_low.reshape(own_blocks, BLOCK, local_heads, HD)
    scores = scores_of(query, key_sel, usable, scale)
    top = jnp.max(scores, axis=(3, 4), keepdims=True)
    log_total = top + jnp.log(jnp.sum(jnp.exp(scores - top), axis=(3, 4), keepdims=True))
    probs = jnp.exp(scores - log_total)
    probs_low = probs.astype(jnp.bfloat16)
    attended = (
        contract("bhqkc,bhkcd->bqhd", probs_low, value_sel)
        .reshape(rows, local_width)
        .astype(jnp.bfloat16)
    )
    attn_sum = lax.psum(
        jnp.dot(attended, w_out, preferred_element_type=jnp.float32).astype(jnp.bfloat16), "tp"
    ).astype(jnp.float32)
    first_sum = x_float + attn_sum
    normed, norm_pull = jax.vjp(layer_norm, first_sum, gains[0], biases[0])
    normed_low = normed.astype(jnp.bfloat16)
    hidden = jnp.dot(normed_low, w_up, preferred_element_type=jnp.float32)
    activated, gelu_pull = jax.vjp(gelu_tanh, hidden)
    act_low = activated.astype(jnp.bfloat16)
    mlp_sum = lax.psum(
        jnp.dot(act_low, w_down, preferred_element_type=jnp.float32).astype(jnp.bfloat16), "tp"
    ).astype(jnp.float32)
    second_sum = normed + mlp_sum
    result, final_pull = jax.vjp(layer_norm, second_sum, gains[1], biases[1])
    d_second, d_gain_two, d_bias_two = final_pull(out_grad.astype(jnp.float32))
    d_mlp = d_second.astype(jnp.bfloat16)
    grad_down = contract("tf,td->fd", act_low, d_mlp)
    d_act = contract("td,fd->tf", d_mlp, w_down)
    d_hidden = gelu_pull(d_act)[0].astype(jnp.bfloat16)
    grad_up = contract("td,tf->df", normed_low, d_hidden)
    d_normed = d_second + lax.psum(
        contract("tf,df->td", d_hidden, w_up).astype(jnp.bfloat16), "tp"
    ).astype(jnp.float32)
    d_first, d_gain_one, d_bias_one = norm_pull(d_normed)
    d_attn = d_first.astype(jnp.bfloat16)
    grad_proj = contract("te,td->ed", attended, d_attn)
    d_attended = (
        contract("td,ed->te", d_attn, w_out)
        .astype(jnp.bfloat16)
        .reshape(own_blocks, BLOCK, local_heads, HD)
    )
    scores = scores_of(query, key_sel, usable, scale)
    probs = jnp.exp(scores - log_total)
    probs_low = probs.astype(jnp.bfloat16)
    d_probs = contract("bqhd,bhkcd->bhqkc", d_attended, value_sel)
    d_scores = probs * (d_probs - jnp.sum(probs * d_probs, axis=(3, 4), keepdims=True))
    d_raw = (d_scores * scale).astype(jnp.bfloat16)
    d_query = (
        contract("bhqkc,bhkcd->bqhd", d_raw, key_sel)
        .reshape(rows, local_width)
        .astype(jnp.bfloat16)
    )
    d_key_sel = contract("bhqkc,bqhd->bhkcd", d_raw, query)
    d_value_sel = contract("bhqkc,bqhd->bhkcd", probs_low, d_attended)
    empty = jnp.zeros((group_blocks, BLOCK, local_heads, HD), jnp.float32)
    d_key_all = (
        empty.at[key_table, :, head_pick, :]
        .add(d_key_sel)
        .reshape(group_blocks * BLOCK, local_width)
    )
    d_value_all = (
        empty.at[key_table, :, head_pick, :]
        .add(d_value_sel)
        .reshape(group_blocks * BLOCK, local_width)
    )
    d_key, d_value = (
        lax.psum_scatter(
            d_key_all.astype(jnp.bfloat16), "ctx", scatter_dimension=0, tiled=True
        ).astype(jnp.float32),
        lax.psum_scatter(
            d_value_all.astype(jnp.bfloat16), "ctx", scatter_dimension=0, tiled=True
        ).astype(jnp.float32),
    )
    d_projected = jnp.stack([d_query, d_key.astype(jnp.bfloat16), d_value.astype(jnp.bfloat16)])
    grad_qkv = contract("td,kte->kde", inputs, d_projected)
    d_inputs = d_first + lax.psum(
        contract("kte,kde->td", d_projected, w_qkv).astype(jnp.bfloat16), "tp"
    ).astype(jnp.float32)
    grad_gains = jnp.stack([d_gain_one, d_gain_two])
    grad_biases = jnp.stack([d_bias_one, d_bias_two])
    shared = (
        lax.psum_scatter(
            grad_qkv.astype(jnp.bfloat16), "dp", scatter_dimension=1, tiled=True
        ).astype(jnp.float32),
        lax.psum_scatter(
            grad_proj.astype(jnp.bfloat16), "dp", scatter_dimension=1, tiled=True
        ).astype(jnp.float32),
        lax.psum_scatter(
            grad_up.astype(jnp.bfloat16), "dp", scatter_dimension=0, tiled=True
        ).astype(jnp.float32),
        lax.psum_scatter(
            grad_down.astype(jnp.bfloat16), "dp", scatter_dimension=1, tiled=True
        ).astype(jnp.float32),
        lax.psum_scatter(
            grad_gains.astype(jnp.bfloat16), "dp", scatter_dimension=1, tiled=True
        ).astype(jnp.float32),
        lax.psum_scatter(
            grad_biases.astype(jnp.bfloat16), "dp", scatter_dimension=1, tiled=True
        ).astype(jnp.float32),
    )
    totals = (
        lax.psum(shared[0].astype(jnp.bfloat16), "ctx").astype(jnp.float32),
        lax.psum(shared[1].astype(jnp.bfloat16), "ctx").astype(jnp.float32),
        lax.psum(shared[2].astype(jnp.bfloat16), "ctx").astype(jnp.float32),
        lax.psum(shared[3].astype(jnp.bfloat16), "ctx").astype(jnp.float32),
        lax.psum(shared[4].astype(jnp.bfloat16), "ctx").astype(jnp.float32),
        lax.psum(shared[5].astype(jnp.bfloat16), "ctx").astype(jnp.float32),
    )
    return (
        result.astype(jnp.bfloat16),
        d_inputs.astype(jnp.bfloat16),
        totals[0],
        totals[1],
        totals[2],
        totals[3],
        totals[4],
        totals[5],
    )


def mul(left, right, left_dim, right_dim):
    dims = (((left_dim,), (right_dim,)), ((), ()))
    return lax.dot_general(left, right, dims, preferred_element_type=jnp.float32)


def call(body, outs, *args, scratch=(), flops=0):
    specs = [pl.BlockSpec(memory_space=pltpu.SMEM)] + [pl.BlockSpec(memory_space=pltpu.VMEM)] * (len(args) - 1)
    shapes = [jax.ShapeDtypeStruct(shape, dtype) for shape, dtype in outs]
    size = sum(math.prod(a.shape) * a.dtype.itemsize for a in list(args) + shapes)
    return pl.pallas_call(
        body,
        out_shape=shapes,
        in_specs=specs,
        out_specs=[pl.BlockSpec(memory_space=pltpu.VMEM)] * len(shapes),
        scratch_shapes=[pltpu.VMEM(shape, dtype) for shape, dtype in scratch],
        compiler_params=pltpu.CompilerParams(vmem_limit_bytes=48 << 20),
        cost_estimate=pl.CostEstimate(flops=flops, bytes_accessed=size, transcendentals=0),
    )(*args)


def head_masks(width):
    lane = lax.broadcasted_iota(jnp.int32, (1, width), 1)
    return [(lane >= h * HD) & (lane < (h + 1) * HD) for h in range(width // HD)]


def only(values, mask):
    return jnp.where(mask, values, jnp.zeros_like(values))


def biased(raw, bias, scale):
    blocks = bias.shape[0]
    size = raw.shape[0] // blocks
    return jnp.concatenate(
        [raw[j * size : (j + 1) * size] * scale + bias[j : j + 1] for j in range(blocks)], axis=0
    )


def attend_body(at, x_ref, w_ref, bias_ref, o_ref, qkv_ref, lse_ref, vec_ref, p_scr, v_scr):
    width = o_ref.shape[1]
    rows = x_ref.shape[0]
    scale = 1.0 / math.sqrt(HD)
    w = w_ref[...]
    qkv = mul(x_ref[...], w, 1, 0).astype(jnp.bfloat16)
    qkv_ref[...] = qkv[:, : 3 * width]
    vec = w[:, 3 * width :]
    unit = (
        lax.broadcasted_iota(jnp.int32, (8, vec.shape[1]), 0) == lax.broadcasted_iota(jnp.int32, (8, vec.shape[1]), 1)
    ).astype(jnp.bfloat16)
    vec_ref[...] = mul(unit, vec, 1, 1)
    q, k, v = [qkv[:, i * width : (i + 1) * width] for i in range(3)]
    lse_ref[...] = jnp.zeros_like(lse_ref)
    blocks = bias_ref.shape[0] // (width // HD)
    for h, mask in enumerate(head_masks(width)):
        s = biased(mul(k, only(q, mask), 1, 1), bias_ref[h * blocks : (h + 1) * blocks, :], scale)
        top = jnp.max(s, axis=0, keepdims=True)
        e = jnp.exp(s - top)
        total = jnp.sum(e, axis=0, keepdims=True)
        lse_ref[h : h + 1, :] = top + jnp.log(total)
        p_scr[h * rows : (h + 1) * rows, :] = (e * (1.0 / total)).astype(jnp.bfloat16)
        v_scr[h * rows : (h + 1) * rows, :] = only(v, mask)
    o_ref[...] = mul(p_scr[...], v_scr[...], 0, 0).astype(jnp.bfloat16)


def split_rows(at, value_of, mine_ref, theirs_ref):
    half = mine_ref.shape[0]
    t = at[3]
    theirs_ref[...] = value_of(pl.ds((1 - t) * half, half)).astype(theirs_ref.dtype)
    mine_ref[...] = value_of(pl.ds(t * half, half))


def project_body(at, o_ref, w_ref, mine_ref, theirs_ref):
    split_rows(at, lambda rows: mul(o_ref[rows, :], w_ref[...], 1, 1), mine_ref, theirs_ref)


def norm_parts(z):
    centred = z - jnp.mean(z, axis=1, keepdims=True)
    r = lax.rsqrt(jnp.mean(centred * centred, axis=1, keepdims=True) + eps)
    return centred * r, r


def norm_back(e2, n, r):
    return r * (e2 - jnp.mean(e2, axis=1, keepdims=True) - n * jnp.mean(e2 * n, axis=1, keepdims=True))


def norm_one_body(at, x_ref, a_ref, far_ref, vec_ref, n_ref, r_ref, low_ref):
    half = n_ref.shape[0]
    z = x_ref[pl.ds(at[3] * half, half), :].astype(jnp.float32)
    z = z + (a_ref[...].astype(jnp.float32) + far_ref[...].astype(jnp.float32))
    n, r = norm_parts(z)
    n_ref[...] = n
    r_ref[...] = jnp.broadcast_to(r, r_ref.shape)
    low_ref[...] = (n * vec_ref[0:1, :] + vec_ref[2:3, :]).astype(jnp.bfloat16)


def join(at, near_ref, far_ref, all_ref):
    half = near_ref.shape[0]
    t = at[3]
    all_ref[pl.ds(t * half, half), :] = near_ref[...]
    all_ref[pl.ds((1 - t) * half, half), :] = far_ref[...]


def ffn_body(at, near_ref, far_ref, up_ref, down_ref, y_ref, u_ref, slope_ref, mine_ref, theirs_ref):
    join(at, near_ref, far_ref, y_ref)
    hid = mul(y_ref[...], up_ref[...], 1, 0)
    root = math.sqrt(2.0 / math.pi)
    square = hid * hid
    bent = jnp.tanh(root * (hid + 0.044715 * (square * hid)))
    u_ref[...] = (0.5 * hid * (1.0 + bent)).astype(jnp.bfloat16)
    slope = 0.5 * (1.0 + bent) + 0.5 * hid * (1.0 - bent * bent) * (root * (1.0 + 3 * 0.044715 * square))
    slope_ref[...] = slope.astype(jnp.bfloat16)
    split_rows(at, lambda rows: mul(u_ref[rows, :], down_ref[...], 1, 1), mine_ref, theirs_ref)


def norm_two_body(at, n1_ref, m_ref, far_ref, e_ref, e_far_ref, vec_ref, out_ref, dz_ref, low_ref, grad_ref, e_scr, out_scr):
    part = e_far_ref.shape[0]
    c, t = at[2], at[3]
    e_scr[pl.ds(c * part, part), :] = e_ref[pl.ds(t * part, part), :].astype(jnp.float32)
    e_scr[pl.ds((1 - c) * part, part), :] = e_far_ref[...].astype(jnp.float32)
    y1 = n1_ref[...] * vec_ref[0:1, :] + vec_ref[2:3, :]
    z = y1 + (m_ref[...].astype(jnp.float32) + far_ref[...].astype(jnp.float32))
    n, r = norm_parts(z)
    out_scr[...] = n * vec_ref[1:2, :] + vec_ref[3:4, :]
    out_ref[...] = out_scr[pl.ds(c * part, part), :].astype(jnp.bfloat16)
    e = e_scr[...]
    dz = norm_back(e * vec_ref[1:2, :], n, r)
    dz_ref[...] = dz
    low_ref[...] = dz.astype(jnp.bfloat16)
    grad_ref[...] = jnp.zeros_like(grad_ref)
    grad_ref[1:2, :] = jnp.sum(e * n, axis=0, keepdims=True)
    grad_ref[3:4, :] = jnp.sum(e, axis=0, keepdims=True)


def ffn_back_body(at, near_ref, far_ref, slope_ref, down_ref, up_ref, dm_ref, dhid_ref, mine_ref, theirs_ref):
    join(at, near_ref, far_ref, dm_ref)
    du = mul(dm_ref[...], down_ref[...], 1, 0)
    dhid_ref[...] = (du * slope_ref[...].astype(jnp.float32)).astype(jnp.bfloat16)
    split_rows(at, lambda rows: mul(dhid_ref[rows, :], up_ref[...], 1, 1), mine_ref, theirs_ref)


def deal(at, grad, own_ref, away_ref, scr):
    shard = own_ref.shape[1]
    scr[...] = grad
    x = at[1]
    for i in range(own_ref.shape[0]):
        away_ref[i] = scr[pl.ds((2 * i + 1 - x) * shard, shard), :].astype(away_ref.dtype)
        own_ref[i] = scr[pl.ds((2 * i + x) * shard, shard), :].astype(own_ref.dtype)


def grad_body(at, left_ref, right_ref, own_ref, away_ref, scr):
    deal(at, mul(left_ref[...], right_ref[...], 0, 0), own_ref, away_ref, scr)


def norm_one_back_body(at, dz2_ref, d_ref, far_ref, n_ref, r_ref, vec_ref, grad2_ref, dz_ref, low_ref, grad_ref):
    dy = dz2_ref[...] + (d_ref[...].astype(jnp.float32) + far_ref[...].astype(jnp.float32))
    n = n_ref[...]
    dz = norm_back(dy * vec_ref[0:1, :], n, r_ref[:, 0:1])
    dz_ref[...] = dz
    low_ref[...] = dz.astype(jnp.bfloat16)
    grad_ref[...] = grad2_ref[...]
    grad_ref[0:1, :] = jnp.sum(dy * n, axis=0, keepdims=True)
    grad_ref[2:3, :] = jnp.sum(dy, axis=0, keepdims=True)


def attend_back_body(
    at, near_ref, far_ref, w_out_ref, w_ref, qkv_ref, o_ref, lse_ref, bias_ref, x_ref, vec_ref, vec_far_ref,
    own_ref, away_ref, own_o_ref, away_o_ref, mine_ref, theirs_ref,
    da_scr, p_scr, dr_scr, q_scr, do_scr, all_scr, grad_scr, grad_o_scr,
):
    width = o_ref.shape[1]
    rows = x_ref.shape[0]
    scale = 1.0 / math.sqrt(HD)
    join(at, near_ref, far_ref, da_scr)
    da = da_scr[...]
    deal(at, mul(da, o_ref[...], 0, 0), own_o_ref, away_o_ref, grad_o_scr)
    do = mul(da, w_out_ref[...], 1, 0).astype(jnp.bfloat16)
    q, k, v = [qkv_ref[:, i * width : (i + 1) * width] for i in range(3)]
    blocks = bias_ref.shape[0] // (width // HD)
    dq = jnp.zeros((rows, width), jnp.float32)
    for h, mask in enumerate(head_masks(width)):
        q_h, do_h = only(q, mask), only(do, mask)
        s = biased(mul(k, q_h, 1, 1), bias_ref[h * blocks : (h + 1) * blocks, :], scale)
        p = jnp.exp(s - lse_ref[h : h + 1, :])
        dp = mul(v, do_h, 1, 1)
        pd = p * dp
        ds = pd - p * jnp.sum(pd, axis=0, keepdims=True)
        dr = (ds * scale).astype(jnp.bfloat16)
        p_scr[:, h * rows : (h + 1) * rows] = p.astype(jnp.bfloat16)
        dr_scr[:, h * rows : (h + 1) * rows] = dr
        q_scr[h * rows : (h + 1) * rows, :] = q_h
        do_scr[h * rows : (h + 1) * rows, :] = do_h
        dq = dq + mul(dr, only(k, mask), 0, 0)
    all_scr[:, 0:width] = dq.astype(jnp.bfloat16)
    all_scr[:, width : 2 * width] = mul(dr_scr[...], q_scr[...], 1, 0).astype(jnp.bfloat16)
    all_scr[:, 2 * width : 3 * width] = mul(p_scr[...], do_scr[...], 1, 0).astype(jnp.bfloat16)
    vec = (vec_ref[...] + vec_far_ref[...]).astype(jnp.bfloat16)
    extra = grad_scr.shape[1] - 3 * width
    unit = (
        lax.broadcasted_iota(jnp.int32, (8, extra), 0) == lax.broadcasted_iota(jnp.int32, (8, extra), 1)
    ).astype(jnp.bfloat16)
    grad = jnp.concatenate([mul(x_ref[...], all_scr[...], 0, 0), mul(vec, unit, 0, 0)], axis=1)
    deal(at, grad, own_ref, away_ref, grad_scr)
    w = w_ref[:, 0 : 3 * width]
    split_rows(at, lambda r: mul(all_scr[r, :], w, 1, 1), mine_ref, theirs_ref)


def rows_device(
    dims,
    inputs,
    qkv_weight,
    out_weight,
    up_weight,
    down_weight,
    norm_gains,
    norm_biases,
    lengths,
    random_blocks,
    out_grad,
):
    n_dp = dims["dp"]
    n_out = n_dp // 2
    dp = lax.axis_index("dp")
    c = lax.axis_index("ctx")
    t = lax.axis_index("tp")
    z = dp // 2
    x = dp % 2
    at = jnp.stack([z, x, c, t]).astype(jnp.int32)
    f32, bf16 = jnp.float32, jnp.bfloat16
    pair = [(0, 1), (1, 0)]
    across_x = [(i, i ^ 1) for i in range(n_dp)]

    def across_z(s):
        return [(i, ((i // 2 + s) % n_out) * 2 + i % 2) for i in range(n_dp)]

    def swap_tp(v):
        return lax.ppermute(v, "tp", pair)

    def swap_ctx(v):
        return lax.ppermute(v, "ctx", pair)

    def gather_dp(v):
        near = [v] + [lax.ppermute(v, "dp", across_z(s)) for s in range(1, n_out)]
        order = [0] + [n_out - s for s in range(1, n_out)]
        first = lax.ppermute(v, "dp", across_x)
        near = jnp.stack([near[s] for s in order])
        rest = lax.ppermute(near[1:], "dp", across_x)
        far = jnp.concatenate([first[None], rest])
        both = jnp.stack([jnp.where(x == 0, near, far), jnp.where(x == 0, far, near)], axis=1)
        both = jnp.roll(both, z, axis=0)
        return both.reshape(n_dp * v.shape[0], v.shape[1])

    def scatter_dp(own, away):
        half = (own.astype(f32) + lax.ppermute(away, "dp", across_x).astype(f32)).astype(bf16)
        total = lax.dynamic_index_in_dim(half, z, 0, False).astype(f32)
        for s in range(1, n_out):
            piece = lax.dynamic_index_in_dim(half, (z + s) % n_out, 0, False)
            total = total + lax.ppermute(piece, "dp", across_z(s)).astype(f32)
        return total.astype(bf16)

    rows = inputs.shape[0]
    part = rows // 2
    width = inputs.shape[1]
    shard = qkv_weight.shape[1]
    cols = qkv_weight.shape[2] // 2
    units = up_weight.shape[1] // 2
    heads = cols // HD
    own_blocks = rows // BLOCK
    per = own_blocks // 2
    total_rows = 2 * rows
    pad = -(3 * cols + 4) % 128

    def own_cols(w):
        n = w.shape[-1] // 2
        return lax.dynamic_slice_in_dim(w, c * n, n, w.ndim - 1)

    small = jnp.concatenate([norm_gains, norm_biases], axis=0)
    w1 = jnp.concatenate([own_cols(qkv_weight[i]) for i in range(3)] + [jnp.pad(small.T, ((0, 0), (0, pad)))], axis=1)
    w_out_t = own_cols(out_weight.T)
    w_up = own_cols(up_weight)
    w_down_t = own_cols(down_weight.T)
    w1 = gather_dp(w1)
    w_out_t = gather_dp(w_out_t)
    w_up = gather_dp(w_up)
    w_down_t = gather_dp(w_down_t)

    halves = inputs.reshape(2, part, width)
    near = swap_ctx(lax.dynamic_index_in_dim(halves, t, 0, False))
    far = swap_tp(near)
    other = jnp.where(t == 0, jnp.stack([near, far]), jnp.stack([far, near]))
    x_all = jnp.where(c == 0, jnp.stack([halves, other], 1), jnp.stack([other, halves], 1)).reshape(total_rows, width)
    e_far = swap_ctx(lax.dynamic_index_in_dim(out_grad.reshape(2, part, width), t, 0, False))

    picks = random_blocks.reshape(own_blocks, 2, heads, 3)
    picks_own = lax.dynamic_index_in_dim(picks, c, 1, False)
    picks_far = swap_ctx(lax.dynamic_index_in_dim(picks, 1 - c, 1, False))
    picks = jnp.where(c == 0, jnp.stack([picks_own, picks_far]), jnp.stack([picks_far, picks_own]))
    picks = picks.reshape(2 * own_blocks, heads, 3)
    blocks = jnp.arange(2 * own_blocks, dtype=jnp.int32)
    table, usable = block_table(blocks, lengths[0], picks)
    named = (table[..., None] == blocks) & usable[:, None, :, None]
    counts = jnp.sum(named.astype(f32), axis=2)
    counts = counts.reshape(2, 2, per, heads, 2, 2, per).transpose(3, 5, 4, 6, 1, 0, 2)
    bias = jnp.where(counts > 0, jnp.log(jnp.maximum(counts, 1.0)), -1e30)
    bias = bias.reshape(heads * 2 * own_blocks, 2 * own_blocks, 1)
    bias = jnp.broadcast_to(bias, bias.shape[:2] + (BLOCK,)).reshape(-1, total_rows)

    low = [((rows, width), bf16)]
    wide = [((rows, width), f32)]
    o, qkv, lse, vecs = call(
        attend_body,
        [((total_rows, cols), bf16), ((total_rows, 3 * cols), bf16), ((8, total_rows), f32), ((8, width), f32)],
        at, x_all, w1, bias,
        scratch=[((heads * total_rows, total_rows), bf16), ((heads * total_rows, cols), bf16)],
        flops=10**9,
    )

    def sum_row(mine, theirs):
        s = (mine + swap_tp(theirs).astype(f32)).astype(bf16)
        return s, swap_ctx(s)

    a, a_far = sum_row(*call(project_body, wide + low, at, o, w_out_t))
    n1, r1, y_low = call(norm_one_body, wide + [((rows, 128), f32)] + low, at, x_all, a, a_far, vecs)
    flat = [((total_rows, units), bf16)]
    y_all, u, slope, mine, theirs = call(
        ffn_body, [((total_rows, width), bf16)] + flat * 2 + wide + low, at, y_low, swap_tp(y_low), w_up, w_down_t,
        flops=10**9,
    )
    m, m_far = sum_row(mine, theirs)
    out, dz2, dm_low, grad2 = call(
        norm_two_body,
        [((part, width), bf16)] + wide + low + [((8, width), f32)],
        at, n1, m, m_far, out_grad, e_far, vecs,
        scratch=wide * 2,
    )
    dm_all, dhid, mine, theirs = call(
        ffn_back_body, [((total_rows, width), bf16)] + flat + wide + low,
        at, dm_low, swap_tp(dm_low), slope, w_down_t, w_up,
        flops=10**9,
    )
    d, d_far = sum_row(mine, theirs)

    def dealt(n):
        return [((n_out, shard, n), f32), ((n_out, shard, n), bf16)]

    down_own, down_away = call(grad_body, dealt(units), at, dm_all, u, scratch=[((width, units), f32)])
    up_own, up_away = call(grad_body, dealt(units), at, y_all, dhid, scratch=[((width, units), f32)])
    dz1, da_low, grad1 = call(
        norm_one_back_body, wide + low + [((8, width), f32)], at, dz2, d, d_far, n1, r1, vecs, grad2
    )
    qkv_own, qkv_away, o_own, o_away, mine, theirs = call(
        attend_back_body,
        dealt(w1.shape[1]) + dealt(cols) + wide + low,
        at, da_low, swap_tp(da_low), w_out_t, w1, qkv, o, lse, bias, x_all, grad1, swap_tp(grad1),
        scratch=[
            ((total_rows, width), bf16),
            ((total_rows, heads * total_rows), bf16),
            ((total_rows, heads * total_rows), bf16),
            ((heads * total_rows, cols), bf16),
            ((heads * total_rows, cols), bf16),
            ((total_rows, 3 * cols), bf16),
            ((width, w1.shape[1]), f32),
            ((width, cols), f32),
        ],
        flops=2 * 10**9,
    )
    dx = (mine + swap_tp(theirs).astype(f32)).astype(bf16).reshape(2, part, width)
    dx_own = lax.dynamic_index_in_dim(dx, c, 0, False).astype(f32)
    dx_far = swap_ctx(lax.dynamic_index_in_dim(dx, 1 - c, 0, False)).astype(f32)
    dz1_own = lax.dynamic_index_in_dim(dz1.reshape(2, part, width), c, 0, False)
    dx = (dz1_own + dx_own + dx_far).astype(bf16)

    def both_tp(near):
        far = swap_tp(near)
        return jnp.where(t == 0, jnp.concatenate([near, far]), jnp.concatenate([far, near]))

    output = both_tp(out)
    input_grad = both_tp(dx)

    def both_ctx(g):
        far = swap_ctx(g)
        return jnp.where(c == 0, jnp.concatenate([g, far], 1), jnp.concatenate([far, g], 1))

    grad_down = both_ctx(scatter_dp(down_own, down_away)).astype(f32).T
    grad_up = both_ctx(scatter_dp(up_own, up_away)).astype(f32)
    grad_out = both_ctx(scatter_dp(o_own, o_away)).astype(f32).T
    grad_1 = scatter_dp(qkv_own, qkv_away)
    far_1 = swap_ctx(grad_1)
    lo = jnp.where(c == 0, grad_1, far_1).astype(f32)
    hi = jnp.where(c == 0, far_1, grad_1).astype(f32)
    grad_qkv = jnp.stack(
        [jnp.concatenate([lo[:, i * cols : (i + 1) * cols], hi[:, i * cols : (i + 1) * cols]], 1) for i in range(3)]
    )
    vec = grad_1[:, 3 * cols : 3 * cols + 4].astype(f32).T
    return (output, input_grad, grad_qkv, grad_out, grad_up, grad_down, vec[:2], vec[2:])


def solution(mesh):
    dims = dict(mesh.shape)
    fast = dims["ctx"] == 2 and dims["tp"] == 2 and dims["dp"] % 2 == 0
    step = functools.partial(rows_device, dims) if fast else per_device
    return jax.shard_map(
        step,
        mesh=mesh,
        in_specs=(
            P(("dp", "ctx"), None),
            P(None, "dp", "tp"),
            P("tp", "dp"),
            P("dp", "tp"),
            P("tp", "dp"),
            P(None, "dp"),
            P(None, "dp"),
            P("dp", None),
            P(("dp", "ctx"), "tp", None),
            P(("dp", "ctx"), None),
        ),
        out_specs=(
            P(("dp", "ctx"), None),
            P(("dp", "ctx"), None),
            P(None, "dp", "tp"),
            P("tp", "dp"),
            P("dp", "tp"),
            P("tp", "dp"),
            P(None, "dp"),
            P(None, "dp"),
        ),
        check_vma=False,
    )
```

```python
import functools
import math

import jax
import jax.numpy as jnp
from jax import lax
from jax.experimental import pallas as pl
from jax.experimental.pallas import tpu as pltpu
from jax.sharding import PartitionSpec as P

HD = 64
BLOCK = 64


eps = 1e-06


def layer_norm(values, gain, shift):
    row_mean = jnp.mean(values, axis=-1, keepdims=True)
    centred = values - row_mean
    spread = jnp.mean(centred * centred, axis=-1, keepdims=True)
    return centred * lax.rsqrt(spread + eps) * gain + shift


def gelu_tanh(values):
    return jax.nn.gelu(values, approximate=True)


def contract(form, left, right):
    return jnp.einsum(form, left, right, preferred_element_type=jnp.float32)


def block_table(blocks, lengths_row, offsets):
    seq_ends = jnp.cumsum(lengths_row)
    starts = seq_ends - lengths_row
    inside = ((blocks[:, None] >= starts[None, :]) & (blocks[:, None] < seq_ends[None, :])).astype(
        jnp.int32
    )
    seq_first = jnp.sum(inside * starts[None, :], axis=1)
    seq_count = jnp.sum(inside * lengths_row[None, :], axis=1)
    position = blocks - seq_first
    has_before = position > 0
    has_behind = position < seq_count - 1
    before = jnp.where(has_before, blocks - 1, blocks)
    behind = jnp.where(has_behind, blocks + 1, blocks)
    fixed_ids = jnp.stack([before, blocks, behind, seq_first, seq_first + 1], axis=-1)
    random_ids = seq_first[:, None, None] + offsets % seq_count[:, None, None]
    head_count = offsets.shape[1]
    key_table = jnp.concatenate(
        [jnp.broadcast_to(fixed_ids[:, None, :], (blocks.shape[0], head_count, 5)), random_ids],
        axis=-1,
    )
    always = jnp.ones_like(has_before)
    usable = jnp.stack(
        [has_before, always, has_behind, always, always] + [always] * offsets.shape[2], axis=-1
    )
    return (key_table, usable)


def scores_of(query, key_sel, usable, scale):
    raw = contract("bqhd,bhkcd->bhqkc", query, key_sel)
    return jnp.where(usable[:, None, None, :, None], raw * scale, -1e30)


def per_device(
    inputs,
    qkv_weight,
    out_weight,
    up_weight,
    down_weight,
    norm_gains,
    norm_biases,
    lengths,
    random_blocks,
    out_grad,
):
    w_qkv, w_out, w_up, w_down, gains_low, biases_low = (
        lax.all_gather(qkv_weight, "dp", axis=1, tiled=True),
        lax.all_gather(out_weight, "dp", axis=1, tiled=True),
        lax.all_gather(up_weight, "dp", axis=0, tiled=True),
        lax.all_gather(down_weight, "dp", axis=1, tiled=True),
        lax.all_gather(norm_gains, "dp", axis=1, tiled=True),
        lax.all_gather(norm_biases, "dp", axis=1, tiled=True),
    )
    gains = gains_low.astype(jnp.float32)
    biases = biases_low.astype(jnp.float32)
    rows = inputs.shape[0]
    own_blocks = rows // BLOCK
    local_width = w_qkv.shape[2]
    local_heads = local_width // HD
    scale = 1.0 / math.sqrt(HD)
    x_float = inputs.astype(jnp.float32)
    projected = contract("td,kde->kte", inputs, w_qkv)
    q_low = projected[0].astype(jnp.bfloat16)
    k_low = projected[1].astype(jnp.bfloat16)
    v_low = projected[2].astype(jnp.bfloat16)
    key_all, value_all = (
        lax.all_gather(k_low, "ctx", axis=0, tiled=True),
        lax.all_gather(v_low, "ctx", axis=0, tiled=True),
    )
    group_blocks = key_all.shape[0] // BLOCK
    first_block = lax.axis_index("ctx") * own_blocks
    blocks = first_block + jnp.arange(own_blocks, dtype=jnp.int32)
    key_table, usable = block_table(blocks, lengths[0], random_blocks)
    head_pick = jnp.arange(local_heads, dtype=jnp.int32)[None, :, None]
    key_blocks = key_all.reshape(group_blocks, BLOCK, local_heads, HD)
    value_blocks = value_all.reshape(group_blocks, BLOCK, local_heads, HD)
    key_sel = key_blocks[key_table, :, head_pick, :]
    value_sel = value_blocks[key_table, :, head_pick, :]
    query = q_low.reshape(own_blocks, BLOCK, local_heads, HD)
    scores = scores_of(query, key_sel, usable, scale)
    top = jnp.max(scores, axis=(3, 4), keepdims=True)
    log_total = top + jnp.log(jnp.sum(jnp.exp(scores - top), axis=(3, 4), keepdims=True))
    probs = jnp.exp(scores - log_total)
    probs_low = probs.astype(jnp.bfloat16)
    attended = (
        contract("bhqkc,bhkcd->bqhd", probs_low, value_sel)
        .reshape(rows, local_width)
        .astype(jnp.bfloat16)
    )
    attn_sum = lax.psum(
        jnp.dot(attended, w_out, preferred_element_type=jnp.float32).astype(jnp.bfloat16), "tp"
    ).astype(jnp.float32)
    first_sum = x_float + attn_sum
    normed, norm_pull = jax.vjp(layer_norm, first_sum, gains[0], biases[0])
    normed_low = normed.astype(jnp.bfloat16)
    hidden = jnp.dot(normed_low, w_up, preferred_element_type=jnp.float32)
    activated, gelu_pull = jax.vjp(gelu_tanh, hidden)
    act_low = activated.astype(jnp.bfloat16)
    mlp_sum = lax.psum(
        jnp.dot(act_low, w_down, preferred_element_type=jnp.float32).astype(jnp.bfloat16), "tp"
    ).astype(jnp.float32)
    second_sum = normed + mlp_sum
    result, final_pull = jax.vjp(layer_norm, second_sum, gains[1], biases[1])
    d_second, d_gain_two, d_bias_two = final_pull(out_grad.astype(jnp.float32))
    d_mlp = d_second.astype(jnp.bfloat16)
    grad_down = contract("tf,td->fd", act_low, d_mlp)
    d_act = contract("td,fd->tf", d_mlp, w_down)
    d_hidden = gelu_pull(d_act)[0].astype(jnp.bfloat16)
    grad_up = contract("td,tf->df", normed_low, d_hidden)
    d_normed = d_second + lax.psum(
        contract("tf,df->td", d_hidden, w_up).astype(jnp.bfloat16), "tp"
    ).astype(jnp.float32)
    d_first, d_gain_one, d_bias_one = norm_pull(d_normed)
    d_attn = d_first.astype(jnp.bfloat16)
    grad_proj = contract("te,td->ed", attended, d_attn)
    d_attended = (
        contract("td,ed->te", d_attn, w_out)
        .astype(jnp.bfloat16)
        .reshape(own_blocks, BLOCK, local_heads, HD)
    )
    scores = scores_of(query, key_sel, usable, scale)
    probs = jnp.exp(scores - log_total)
    probs_low = probs.astype(jnp.bfloat16)
    d_probs = contract("bqhd,bhkcd->bhqkc", d_attended, value_sel)
    d_scores = probs * (d_probs - jnp.sum(probs * d_probs, axis=(3, 4), keepdims=True))
    d_raw = (d_scores * scale).astype(jnp.bfloat16)
    d_query = (
        contract("bhqkc,bhkcd->bqhd", d_raw, key_sel)
        .reshape(rows, local_width)
        .astype(jnp.bfloat16)
    )
    d_key_sel = contract("bhqkc,bqhd->bhkcd", d_raw, query)
    d_value_sel = contract("bhqkc,bqhd->bhkcd", probs_low, d_attended)
    empty = jnp.zeros((group_blocks, BLOCK, local_heads, HD), jnp.float32)
    d_key_all = (
        empty.at[key_table, :, head_pick, :]
        .add(d_key_sel)
        .reshape(group_blocks * BLOCK, local_width)
    )
    d_value_all = (
        empty.at[key_table, :, head_pick, :]
        .add(d_value_sel)
        .reshape(group_blocks * BLOCK, local_width)
    )
    d_key, d_value = (
        lax.psum_scatter(
            d_key_all.astype(jnp.bfloat16), "ctx", scatter_dimension=0, tiled=True
        ).astype(jnp.float32),
        lax.psum_scatter(
            d_value_all.astype(jnp.bfloat16), "ctx", scatter_dimension=0, tiled=True
        ).astype(jnp.float32),
    )
    d_projected = jnp.stack([d_query, d_key.astype(jnp.bfloat16), d_value.astype(jnp.bfloat16)])
    grad_qkv = contract("td,kte->kde", inputs, d_projected)
    d_inputs = d_first + lax.psum(
        contract("kte,kde->td", d_projected, w_qkv).astype(jnp.bfloat16), "tp"
    ).astype(jnp.float32)
    grad_gains = jnp.stack([d_gain_one, d_gain_two])
    grad_biases = jnp.stack([d_bias_one, d_bias_two])
    shared = (
        lax.psum_scatter(
            grad_qkv.astype(jnp.bfloat16), "dp", scatter_dimension=1, tiled=True
        ).astype(jnp.float32),
        lax.psum_scatter(
            grad_proj.astype(jnp.bfloat16), "dp", scatter_dimension=1, tiled=True
        ).astype(jnp.float32),
        lax.psum_scatter(
            grad_up.astype(jnp.bfloat16), "dp", scatter_dimension=0, tiled=True
        ).astype(jnp.float32),
        lax.psum_scatter(
            grad_down.astype(jnp.bfloat16), "dp", scatter_dimension=1, tiled=True
        ).astype(jnp.float32),
        lax.psum_scatter(
            grad_gains.astype(jnp.bfloat16), "dp", scatter_dimension=1, tiled=True
        ).astype(jnp.float32),
        lax.psum_scatter(
            grad_biases.astype(jnp.bfloat16), "dp", scatter_dimension=1, tiled=True
        ).astype(jnp.float32),
    )
    totals = (
        lax.psum(shared[0].astype(jnp.bfloat16), "ctx").astype(jnp.float32),
        lax.psum(shared[1].astype(jnp.bfloat16), "ctx").astype(jnp.float32),
        lax.psum(shared[2].astype(jnp.bfloat16), "ctx").astype(jnp.float32),
        lax.psum(shared[3].astype(jnp.bfloat16), "ctx").astype(jnp.float32),
        lax.psum(shared[4].astype(jnp.bfloat16), "ctx").astype(jnp.float32),
        lax.psum(shared[5].astype(jnp.bfloat16), "ctx").astype(jnp.float32),
    )
    return (
        result.astype(jnp.bfloat16),
        d_inputs.astype(jnp.bfloat16),
        totals[0],
        totals[1],
        totals[2],
        totals[3],
        totals[4],
        totals[5],
    )


def mul(left, right, left_dim, right_dim):
    dims = (((left_dim,), (right_dim,)), ((), ()))
    return lax.dot_general(left, right, dims, preferred_element_type=jnp.float32)


def call(body, outs, *args, scratch=(), copies=0, spec=None, room=32, flops=0):
    spec = spec or pl.BlockSpec(memory_space=pltpu.VMEM)
    specs = [spec] * len(args)
    shapes = [jax.ShapeDtypeStruct(shape, dtype) for shape, dtype in outs]
    return pl.pallas_call(
        body,
        out_shape=shapes,
        in_specs=specs,
        out_specs=[pl.BlockSpec(memory_space=pltpu.VMEM)] * len(shapes),
        scratch_shapes=[pltpu.VMEM(shape, dtype) for shape, dtype in scratch]
        + ([pltpu.SemaphoreType.DMA((copies,))] if copies else []),
        compiler_params=pltpu.CompilerParams(vmem_limit_bytes=room << 20),
        cost_estimate=pl.CostEstimate(flops=flops, bytes_accessed=0, transcendentals=0),
    )(*args)


def head_masks(width):
    lane = lax.broadcasted_iota(jnp.int32, (1, width), 1)
    return [(lane >= h * HD) & (lane < (h + 1) * HD) for h in range(width // HD)]


def only(values, mask):
    return jnp.where(mask, values, jnp.zeros_like(values))


def biased(raw, bias, scale):
    blocks = bias.shape[0]
    size = raw.shape[0] // blocks
    return jnp.concatenate(
        [raw[j * size : (j + 1) * size] * scale + bias[j : j + 1] for j in range(blocks)], axis=0
    )


def place(pieces, all_ref, window):
    index = 0
    shard, width = pieces[0].shape
    for piece in pieces:
        parts = [piece] if len(piece.shape) == 2 else [piece.at[i] for i in range(piece.shape[0])]
        for part in parts:
            owner = lax.axis_index("dp") ^ (2 * (index % 4) + index // 4)
            start = window if part.shape[1] != width else 0
            all_ref[pl.ds(pl.multiple_of(owner * shard, 32), shard), :] = part[:, start : start + width]
            index += 1


def fetch(pairs, sems):
    copies = [pltpu.make_async_copy(src, dst, sems.at[i]) for i, (src, dst) in enumerate(pairs)]
    for copy in copies:
        copy.start()
    for copy in copies:
        copy.wait()


def own_half(src, dst):
    n = dst.shape[1]
    dst[...] = jnp.where(lax.axis_index("ctx") == 0, src[:, :n], src[:, n:])


def pack_first_body(qkv_hbm, gain_hbm, bias_hbm, out_hbm, w_ref, out_ref, pack_ref, qkv, gain, bias, out, sems):
    fetch(((qkv_hbm, qkv), (gain_hbm, gain), (bias_hbm, bias), (out_hbm, out)), sems)
    c = lax.axis_index("ctx")
    n = qkv.shape[2] // 2
    for i in range(3):
        w_ref[:, i * n : (i + 1) * n] = jnp.where(c == 0, qkv[i, :, :n], qkv[i, :, n:])
    first = w_ref.shape[1]
    extra = first - 3 * n
    row = lax.broadcasted_iota(jnp.int32, (2, extra), 0)
    lane = lax.broadcasted_iota(jnp.int32, (2, extra), 1)
    cols = mul(gain[...], (row == lane).astype(jnp.bfloat16), 0, 0)
    cols = cols + mul(bias[...], (row + 2 == lane).astype(jnp.bfloat16), 0, 0)
    w_ref[:, 3 * n :] = cols.astype(jnp.bfloat16)
    own_half(out, out_ref)
    pack_ref[:, 0:first] = w_ref[...]
    pack_ref[:, first:] = out_ref[...]


def pack_second_body(up_hbm, down_hbm, up_ref, down_ref, pack_ref, up, down, sems):
    fetch(((up_hbm, up), (down_hbm, down)), sems)
    own_half(up, up_ref)
    own_half(down, down_ref)
    n = up_ref.shape[1]
    pack_ref[:, 0:n] = up_ref[...]
    pack_ref[:, n:] = down_ref[...]


def attend_body(
    own_ref, far_ref, w0, w1, w2, w3, w4, w5, w6, bias_ref,
    o_ref, qkv_ref, lse_ref, vec_ref, x_ref, w_ref, p_scr, v_scr,
):
    width = o_ref.shape[1]
    rows = x_ref.shape[0]
    part = far_ref.shape[0] // 2
    c = lax.axis_index("ctx")
    for t in range(2):
        x_ref[pl.ds((2 * t + c) * part, part), :] = own_ref[t * part : (t + 1) * part, :]
        x_ref[pl.ds((2 * t + 1 - c) * part, part), :] = far_ref[t * part : (t + 1) * part, :]
    place((w0, w1, w2, w3, w4, w5, w6), w_ref, 0)
    scale = 1.0 / math.sqrt(HD)
    w = w_ref[...]
    qkv = mul(x_ref[...], w, 1, 0).astype(jnp.bfloat16)
    qkv_ref[...] = qkv[:, : 3 * width]
    vec = w[:, 3 * width :]
    unit = (
        lax.broadcasted_iota(jnp.int32, (8, vec.shape[1]), 0) == lax.broadcasted_iota(jnp.int32, (8, vec.shape[1]), 1)
    ).astype(jnp.bfloat16)
    vec_ref[...] = mul(unit, vec, 1, 1)
    q, k, v = [qkv[:, i * width : (i + 1) * width] for i in range(3)]
    lse_ref[...] = jnp.zeros_like(lse_ref)
    blocks = bias_ref.shape[0] // (width // HD)
    for h, mask in enumerate(head_masks(width)):
        s = biased(mul(k, only(q, mask), 1, 1), bias_ref[h * blocks : (h + 1) * blocks, :], scale)
        top = jnp.max(s, axis=0, keepdims=True)
        e = jnp.exp(s - top)
        total = jnp.sum(e, axis=0, keepdims=True)
        lse_ref[h : h + 1, :] = top + jnp.log(total)
        p_scr[h * rows : (h + 1) * rows, :] = (e * (1.0 / total)).astype(jnp.bfloat16)
        v_scr[h * rows : (h + 1) * rows, :] = only(v, mask)
    o_ref[...] = mul(p_scr[...], v_scr[...], 0, 0).astype(jnp.bfloat16)


def split_rows(value_of, mine_ref, theirs_ref):
    half = mine_ref.shape[0]
    t = lax.axis_index("tp")
    theirs_ref[...] = value_of(pl.ds((1 - t) * half, half)).astype(theirs_ref.dtype)
    mine_ref[...] = value_of(pl.ds(t * half, half))


def project_body(window, o_ref, w0, w1, w2, w3, w4, w5, mine_ref, theirs_ref, w_ref):
    place((w0, w1, w2, w3, w4, w5), w_ref, window)
    split_rows(lambda rows: mul(o_ref[rows, :], w_ref[...], 1, 1), mine_ref, theirs_ref)


def add_tp_body(mine_ref, both_ref, sum_ref):
    sum_ref[...] = (mine_ref[...] + both_ref[1 - lax.axis_index("tp")].astype(jnp.float32)).astype(jnp.bfloat16)


def norm_parts(z):
    centred = z - jnp.mean(z, axis=1, keepdims=True)
    r = lax.rsqrt(jnp.mean(centred * centred, axis=1, keepdims=True) + eps)
    return centred * r, r


def norm_back(e2, n, r):
    return r * (e2 - jnp.mean(e2, axis=1, keepdims=True) - n * jnp.mean(e2 * n, axis=1, keepdims=True))


def norm_one_body(x_ref, a_ref, far_ref, vec_ref, n_ref, r_ref, low_ref):
    half = n_ref.shape[0]
    z = x_ref[pl.ds(lax.axis_index("tp") * half, half), :].astype(jnp.float32)
    z = z + (a_ref[...].astype(jnp.float32) + far_ref[...].astype(jnp.float32))
    n, r = norm_parts(z)
    n_ref[...] = n
    r_ref[...] = jnp.broadcast_to(r, r_ref.shape)
    low_ref[...] = (n * vec_ref[0:1, :] + vec_ref[2:3, :]).astype(jnp.bfloat16)


def ffn_body(window, y_ref, w0, w1, w2, w3, w4, w5, u_ref, slope_ref, up_ref):
    place((w0, w1, w2, w3, w4, w5), up_ref, window)
    hid = mul(y_ref[...], up_ref[...], 1, 0)
    root = math.sqrt(2.0 / math.pi)
    square = hid * hid
    bent = jnp.tanh(root * (hid + 0.044715 * (square * hid)))
    u_ref[...] = (0.5 * hid * (1.0 + bent)).astype(jnp.bfloat16)
    slope = 0.5 * (1.0 + bent) + 0.5 * hid * (1.0 - bent * bent) * (root * (1.0 + 3 * 0.044715 * square))
    slope_ref[...] = slope.astype(jnp.bfloat16)


def norm_two_body(n1_ref, m_ref, far_ref, e_ref, e_far_ref, vec_ref, out_ref, dz_ref, low_ref, grad_ref, e_scr, out_scr):
    part = out_ref.shape[0]
    c, t = lax.axis_index("ctx"), lax.axis_index("tp")
    e_scr[pl.ds(c * part, part), :] = e_ref[pl.ds(t * part, part), :].astype(jnp.float32)
    e_scr[pl.ds((1 - c) * part, part), :] = e_far_ref[pl.ds(t * part, part), :].astype(jnp.float32)
    y1 = n1_ref[...] * vec_ref[0:1, :] + vec_ref[2:3, :]
    z = y1 + (m_ref[...].astype(jnp.float32) + far_ref[...].astype(jnp.float32))
    n, r = norm_parts(z)
    out_scr[...] = n * vec_ref[1:2, :] + vec_ref[3:4, :]
    out_ref[...] = out_scr[pl.ds(c * part, part), :].astype(jnp.bfloat16)
    e = e_scr[...]
    dz = norm_back(e * vec_ref[1:2, :], n, r)
    dz_ref[...] = dz
    low_ref[...] = dz.astype(jnp.bfloat16)
    grad_ref[...] = jnp.zeros_like(grad_ref)
    grad_ref[1:2, :] = jnp.sum(e * n, axis=0, keepdims=True)
    grad_ref[3:4, :] = jnp.sum(e, axis=0, keepdims=True)


def ffn_back_body(dm_ref, slope_ref, down_ref, up_ref, dhid_ref, mine_ref, theirs_ref):
    du = mul(dm_ref[...], down_ref[...], 1, 0)
    dhid_ref[...] = (du * slope_ref[...].astype(jnp.float32)).astype(jnp.bfloat16)
    split_rows(lambda rows: mul(dhid_ref[rows, :], up_ref[...], 1, 1), mine_ref, theirs_ref)


def deal(own_ref, away_ref, scr, order, start=0):
    one, two, three = order
    shard, width = own_ref.shape[1:]
    dp = lax.axis_index("dp")
    for i, bits in enumerate((0, three, two, two ^ three)):
        for ref, owner in ((own_ref, dp ^ bits), (away_ref, dp ^ bits ^ one)):
            part = scr[pl.ds(pl.multiple_of(owner * shard, 32), shard), start : start + width]
            ref[i] = part.astype(ref.dtype)


def grad_body(order, left_ref, right_ref, own_ref, away_ref, scr):
    scr[...] = mul(left_ref[...], right_ref[...], 0, 0)
    deal(own_ref, away_ref, scr, order)


def fold_pair(own_ref, got_ref, keep_ref, send_ref):
    half = keep_ref.shape[0]
    keep_ref[...] = own_ref[0:half] + got_ref[0:half].astype(jnp.float32)
    send_ref[...] = (own_ref[half:] + got_ref[half:].astype(jnp.float32)).astype(jnp.bfloat16)


def fold_body(own_ref, got_ref, keep_ref, send_ref):
    fold_pair(own_ref, got_ref, keep_ref, send_ref)


def fold_two_body(own_ref, got_ref, own2_ref, got2_ref, keep_ref, send_ref, keep2_ref, send2_ref):
    fold_pair(own_ref, got_ref, keep_ref, send_ref)
    fold_pair(own2_ref, got2_ref, keep2_ref, send2_ref)


def fold_join_body(own_ref, got_ref, own2_ref, got2_ref, keep_ref, send_ref):
    width = own_ref.shape[2]
    for own, got, lanes in ((own_ref, got_ref, slice(0, width)), (own2_ref, got2_ref, slice(width, keep_ref.shape[2]))):
        keep_ref[0, :, lanes] = own[0] + got[0].astype(jnp.float32)
        send_ref[0, :, lanes] = (own[1] + got[1].astype(jnp.float32)).astype(jnp.bfloat16)


def fold_last_body(own_ref, got_ref, sum_ref):
    sum_ref[...] = (own_ref[0] + got_ref[0].astype(jnp.float32)).astype(jnp.bfloat16)


def norm_one_back_body(dz2_ref, d_ref, far_ref, n_ref, r_ref, vec_ref, grad2_ref, dz_ref, low_ref):
    dy = dz2_ref[...] + (d_ref[...].astype(jnp.float32) + far_ref[...].astype(jnp.float32))
    n = n_ref[...]
    dz = norm_back(dy * vec_ref[0:1, :], n, r_ref[:, 0:1])
    dz_ref[...] = dz
    half = dz.shape[0]
    low_ref[0:half, :] = dz.astype(jnp.bfloat16)
    sums = [
        jnp.sum(dy * n, axis=0, keepdims=True), grad2_ref[1:2, :],
        jnp.sum(dy, axis=0, keepdims=True), grad2_ref[3:4, :], jnp.zeros((12, dz.shape[1]), jnp.float32),
    ]
    low_ref[half : half + 16, :] = jnp.concatenate(sums, axis=0).astype(jnp.bfloat16)


def attend_back_body(
    da_ref, w_out_ref, w_ref, qkv_ref, o_ref, lse_ref, bias_ref, x_ref,
    own_ref, away_ref, own2_ref, away2_ref, mine_ref, theirs_ref,
    p_scr, dr_scr, q_scr, do_scr, all_scr, grad_scr,
):
    width = o_ref.shape[1]
    rows = x_ref.shape[0]
    scale = 1.0 / math.sqrt(HD)
    half = rows // 2
    da = jnp.concatenate([da_ref[0, 0:half, :], da_ref[1, 0:half, :]], axis=0)
    do = mul(da, w_out_ref[...], 1, 0).astype(jnp.bfloat16)
    q, k, v = [qkv_ref[:, i * width : (i + 1) * width] for i in range(3)]
    blocks = bias_ref.shape[0] // (width // HD)
    dq = jnp.zeros((rows, width), jnp.float32)
    for h, mask in enumerate(head_masks(width)):
        q_h, do_h = only(q, mask), only(do, mask)
        s = biased(mul(k, q_h, 1, 1), bias_ref[h * blocks : (h + 1) * blocks, :], scale)
        p = jnp.exp(s - lse_ref[h : h + 1, :])
        dp = mul(v, do_h, 1, 1)
        pd = p * dp
        ds = pd - p * jnp.sum(pd, axis=0, keepdims=True)
        dr = (ds * scale).astype(jnp.bfloat16)
        p_scr[:, h * rows : (h + 1) * rows] = p.astype(jnp.bfloat16)
        dr_scr[:, h * rows : (h + 1) * rows] = dr
        q_scr[h * rows : (h + 1) * rows, :] = q_h
        do_scr[h * rows : (h + 1) * rows, :] = do_h
        dq = dq + mul(dr, only(k, mask), 0, 0)
    all_scr[:, 0:width] = dq.astype(jnp.bfloat16)
    all_scr[:, width : 2 * width] = mul(dr_scr[...], q_scr[...], 1, 0).astype(jnp.bfloat16)
    all_scr[:, 2 * width : 3 * width] = mul(p_scr[...], do_scr[...], 1, 0).astype(jnp.bfloat16)
    vec = sum(da_ref[i, half : half + 16, :].astype(jnp.float32) for i in range(2)).astype(jnp.bfloat16)
    extra = w_ref.shape[1] - 3 * width
    unit = (
        lax.broadcasted_iota(jnp.int32, (16, extra), 0) == lax.broadcasted_iota(jnp.int32, (16, extra), 1)
    ).astype(jnp.bfloat16)
    grad_scr[...] = jnp.concatenate(
        [mul(x_ref[...], all_scr[...], 0, 0), mul(vec, unit, 0, 0), mul(da, o_ref[...], 0, 0)], axis=1
    )
    deal(own_ref, away_ref, grad_scr, (1, 2, 4))
    deal(own2_ref, away2_ref, grad_scr, (2, 1, 4), own_ref.shape[2])
    w = w_ref[:, 0 : 3 * width]
    split_rows(lambda r: mul(all_scr[r, :], w, 1, 1), mine_ref, theirs_ref)


def fold_input_body(mine_ref, both_ref, dz_ref, keep_ref, send_ref):
    part = keep_ref.shape[0]
    c, far = lax.axis_index("ctx"), 1 - lax.axis_index("tp")
    own, other = pl.ds(c * part, part), pl.ds((1 - c) * part, part)
    send_ref[...] = (mine_ref[other, :] + both_ref[far, other, :].astype(jnp.float32)).astype(jnp.bfloat16)
    keep_ref[...] = dz_ref[own, :] + (mine_ref[own, :] + both_ref[far, own, :].astype(jnp.float32))


def last_input_body(keep_ref, got_ref, out_ref):
    out_ref[...] = (keep_ref[...] + got_ref[...].astype(jnp.float32)).astype(jnp.bfloat16)


def finish_body(near_ref, far_ref, qkv_ref, out_ref, gain_ref, bias_ref):
    c = lax.axis_index("ctx")
    n = qkv_ref.shape[2] // 2
    m = out_ref.shape[1] // 2
    near, far = near_ref[...].astype(jnp.float32), far_ref[...].astype(jnp.float32)
    low, high = jnp.where(c == 0, near, far), jnp.where(c == 0, far, near)
    for i in range(3):
        qkv_ref[i] = jnp.concatenate([low[:, i * n : (i + 1) * n], high[:, i * n : (i + 1) * n]], axis=1)
    out_ref[...] = jnp.concatenate([low[:, low.shape[1] - m :], high[:, high.shape[1] - m :]], axis=1)
    vec = near_ref[:, 3 * n : near_ref.shape[1] - m]
    row = lax.broadcasted_iota(jnp.int32, (2, vec.shape[1]), 0)
    lane = lax.broadcasted_iota(jnp.int32, (2, vec.shape[1]), 1)
    gain_ref[...] = mul((row == lane).astype(jnp.bfloat16), vec, 1, 1)
    bias_ref[...] = mul((row + 2 == lane).astype(jnp.bfloat16), vec, 1, 1)


def rows_device(
    dims,
    inputs,
    qkv_weight,
    out_weight,
    up_weight,
    down_weight,
    norm_gains,
    norm_biases,
    lengths,
    random_blocks,
    out_grad,
):
    n_dp = dims["dp"]
    n_out = n_dp // 2
    c = lax.axis_index("ctx")
    f32, bf16 = jnp.float32, jnp.bfloat16
    pair = [(0, 1), (1, 0)]

    def both_tp(v, tiled=False):
        return lax.all_gather(v, "tp", axis=0, tiled=tiled)

    def swap_ctx(v):
        return lax.ppermute(v, "ctx", pair)

    def swap_dp(v, bits):
        return lax.ppermute(v, "dp", [(i, i ^ bits) for i in range(n_dp)])

    def after(v, *others):
        return lax.optimization_barrier((v,) + others)[0]

    def all_after(vs, *others):
        return list(lax.optimization_barrier(tuple(vs) + others)[: len(vs)])

    rows, width = inputs.shape
    part = rows // 2
    shard = qkv_weight.shape[1]
    cols = qkv_weight.shape[2] // 2
    units = up_weight.shape[1] // 2
    heads = cols // HD
    own_blocks = rows // BLOCK
    per = own_blocks // 2
    total_rows = 2 * rows
    first = 3 * cols + 4 + (-(3 * cols + 4)) % 128

    half = ((part, width), bf16)
    hbm = pl.BlockSpec(memory_space=pltpu.HBM)

    def packed(body, widths, *given):
        return call(
            body, [((shard, n), bf16) for n in widths], *given,
            scratch=[(w.shape, bf16) for w in given], copies=len(given), spec=hbm, room=60,
        )

    def near_of(v):
        return [v] + [swap_dp(v, 2 * k) for k in range(1, n_out)]

    def far_rest(near):
        return swap_dp(jnp.stack(near), 1)

    x_far = swap_ctx(inputs)
    w1, w_out, pack_one = packed(
        pack_first_body, (first, cols, first + cols), qkv_weight, norm_gains, norm_biases, out_weight.T
    )
    w1_near = near_of(w1)
    far_one = swap_dp(pack_one, 1)
    w_up, w_down, pack_two = packed(pack_second_body, (units, units, 2 * units), up_weight, down_weight.T)
    picks_far = swap_ctx(random_blocks)
    w1_pieces = w1_near + [far_one, swap_dp(after(w1_near[1], far_one), 1), far_rest(w1_near[2:])]
    out_near = near_of(after(w_out, *w1_near[1:]))
    out_pieces = out_near + [far_one, far_rest(out_near[1:])]
    up_near = near_of(after(w_up, *w1_near[1:]))
    far_two = swap_dp(after(pack_two, *w1_near[1:]), 1)
    e_far = swap_ctx(after(out_grad, x_far))

    picks = jnp.where(c == 0, jnp.stack([random_blocks, picks_far]), jnp.stack([picks_far, random_blocks]))
    picks = lax.dynamic_slice_in_dim(picks.reshape(2 * own_blocks, 2 * heads, 3), c * heads, heads, 1)
    blocks = jnp.arange(2 * own_blocks, dtype=jnp.int32)
    table, usable = block_table(blocks, lengths[0], picks)
    named = (table[..., None] == blocks) & usable[:, None, :, None]
    counts = jnp.sum(named.astype(f32), axis=2)
    counts = counts.reshape(2, 2, per, heads, 2, 2, per).transpose(3, 5, 4, 6, 1, 0, 2)
    bias = jnp.where(counts > 0, jnp.log(jnp.maximum(counts, 1.0)), -1e30)
    bias = bias.reshape(heads * 2 * own_blocks, 2 * own_blocks, 1)
    bias = jnp.broadcast_to(bias, bias.shape[:2] + (BLOCK,)).reshape(-1, total_rows)

    low = [((rows, width), bf16)]
    wide = [((rows, width), f32)]
    small = [((8, width), f32)]
    o, qkv, lse, vecs, x_all, w1_all = call(
        attend_body,
        [
            ((total_rows, cols), bf16), ((total_rows, 3 * cols), bf16), ((8, total_rows), f32), ((8, width), f32),
            ((total_rows, width), bf16), ((width, first), bf16),
        ],
        inputs, after(x_far, e_far), *w1_pieces, bias,
        scratch=[((heads * total_rows, total_rows), bf16), ((heads * total_rows, cols), bf16)],
        flops=2 * 10**10,
    )

    def sum_tp(mine, theirs):
        return call(add_tp_body, low, mine, both_tp(theirs))[0]

    mine, theirs, w_out_all = call(functools.partial(project_body, first), wide + low + [((width, cols), bf16)], o, *out_pieces)
    a = after(sum_tp(mine, theirs), *up_near[1:])
    a_far = swap_ctx(a)
    up_near = up_near[:1] + all_after(up_near[1:], a)
    up_pieces = up_near + [far_two, far_rest(up_near[1:])]
    down_near = near_of(after(w_down, a))
    n1, r1, y_low = call(norm_one_body, wide + [((rows, 128), f32)] + low, x_all, a, a_far, vecs)
    flat = [((total_rows, units), bf16)]
    square = [((width, units), bf16)]
    y_all = both_tp(y_low, True)
    down_near = down_near[:1] + all_after(down_near[1:], y_all)
    down_pieces = down_near + [far_two, far_rest(down_near[1:])]
    u, slope, w_up_all = call(functools.partial(ffn_body, 0), flat * 2 + square, y_all, *up_pieces)
    mine, theirs, w_down_all = call(functools.partial(project_body, units), wide + low + square, u, *down_pieces)
    m = sum_tp(mine, theirs)
    m_far = swap_ctx(m)
    out, dz2, dm_low, grad2 = call(
        norm_two_body,
        [((part, width), bf16)] + wide + low + small,
        n1, m, m_far, out_grad, e_far, vecs,
        scratch=wide * 2,
    )

    def dealt(n):
        return [((n_out, shard, n), f32), ((n_out, shard, n), bf16)]

    def kept(k, n):
        return [((k, shard, n), f32), ((k, shard, n), bf16)]

    def fold(own, got):
        return call(fold_body, kept(own.shape[0] // 2, own.shape[2]), own, got)

    def last_sum(keep, send, bits):
        total = call(fold_last_body, [(keep.shape[1:], bf16)], keep, swap_dp(send, bits))[0]
        return total, swap_ctx(total)

    down_order, up_order = (2, 1, 4), (1, 2, 4)
    dm_all = both_tp(dm_low, True)
    down_own, down_away = call(functools.partial(grad_body, down_order), dealt(units), dm_all, u, scratch=[((width, units), f32)])
    dm_all = after(dm_all, down_away)
    dhid, mine, theirs = call(
        ffn_back_body, flat + wide + low, dm_all, slope, w_down_all, w_up_all
    )
    d = sum_tp(mine, theirs)
    d_far = swap_ctx(d)
    y_late, dhid = lax.optimization_barrier((y_all, dhid, d))[:2]
    up_own, up_away = call(functools.partial(grad_body, up_order), dealt(units), y_late, dhid, scratch=[((width, units), f32)])
    dz1, da_low = call(
        norm_one_back_body, wide + [((rows + 16, width), bf16)], dz2, d, after(d_far, up_away), n1, r1, vecs, grad2
    )
    down_keep, down_send = fold(down_own, swap_dp(down_away, down_order[0]))
    last = first + cols
    left = last // 256 * 128
    own, away, own2, away2, mine, theirs = call(
        attend_back_body,
        dealt(left) + dealt(last - left) + wide + low,
        after(both_tp(da_low), down_send), w_out_all, w1_all, qkv, o, lse, bias, x_all,
        scratch=[
            ((total_rows, heads * total_rows), bf16),
            ((total_rows, heads * total_rows), bf16),
            ((heads * total_rows, cols), bf16),
            ((heads * total_rows, cols), bf16),
            ((total_rows, 3 * cols), bf16),
            ((width, last), f32),
        ],
    )
    up_own = after(up_own, theirs)
    keep, send = call(fold_input_body, [((part, width), f32), half], mine, both_tp(theirs), dz1)
    up_keep, up_send = fold(up_own, swap_dp(up_away, up_order[0]))
    down_keep, down_send = fold(down_keep, swap_dp(down_send, down_order[1]))
    keep1, send1, keep2, send2 = call(
        fold_two_body, kept(2, left) + kept(2, last - left),
        own, swap_dp(away, 1), own2, swap_dp(away2, 2),
    )
    up_keep, up_send = fold(up_keep, swap_dp(up_send, up_order[1]))
    keep1, send1 = call(
        fold_join_body, kept(1, last), keep1, swap_dp(send1, 2), keep2, swap_dp(send2, 1)
    )
    grad_down, down_far = last_sum(down_keep, down_send, 4)
    grad_up, up_far = last_sum(up_keep, up_send, 4)
    grad_1, far_1 = last_sum(keep1, send1, 4)
    dx = call(last_input_body, [half], keep, swap_ctx(send))[0]
    output, input_grad = both_tp(out, True), both_tp(dx, True)

    def both_ctx(g, far):
        return jnp.where(c == 0, jnp.concatenate([g, far], 1), jnp.concatenate([far, g], 1)).astype(f32)

    grad_qkv, grad_out, gains, biases = call(
        finish_body,
        [((3, shard, 2 * cols), f32), ((shard, 2 * cols), f32), ((2, shard), f32), ((2, shard), f32)],
        grad_1, far_1,
    )
    return (
        output, input_grad, grad_qkv, grad_out.T, both_ctx(grad_up, up_far), both_ctx(grad_down, down_far).T, gains, biases
    )


def solution(mesh):
    dims = dict(mesh.shape)
    fast = dims["ctx"] == 2 and dims["tp"] == 2 and dims["dp"] == 8
    step = functools.partial(rows_device, dims) if fast else per_device
    return jax.shard_map(
        step,
        mesh=mesh,
        in_specs=(
            P(("dp", "ctx"), None),
            P(None, "dp", "tp"),
            P("tp", "dp"),
            P("dp", "tp"),
            P("tp", "dp"),
            P(None, "dp"),
            P(None, "dp"),
            P("dp", None),
            P(("dp", "ctx"), "tp", None),
            P(("dp", "ctx"), None),
        ),
        out_specs=(
            P(("dp", "ctx"), None),
            P(("dp", "ctx"), None),
            P(None, "dp", "tp"),
            P("tp", "dp"),
            P("dp", "tp"),
            P("tp", "dp"),
            P(None, "dp"),
            P(None, "dp"),
        ),
        check_vma=False,
    )
```

```python
import functools
import math

import jax
import jax.numpy as jnp
from jax import lax
from jax.experimental import pallas as pl
from jax.experimental.pallas import tpu as pltpu
from jax.sharding import PartitionSpec as P

HD = 64
BLOCK = 64


eps = 1e-06


def layer_norm(values, gain, shift):
    row_mean = jnp.mean(values, axis=-1, keepdims=True)
    centred = values - row_mean
    spread = jnp.mean(centred * centred, axis=-1, keepdims=True)
    return centred * lax.rsqrt(spread + eps) * gain + shift


def gelu_tanh(values):
    return jax.nn.gelu(values, approximate=True)


def contract(form, left, right):
    return jnp.einsum(form, left, right, preferred_element_type=jnp.float32)


def block_table(blocks, lengths_row, offsets):
    seq_ends = jnp.cumsum(lengths_row)
    starts = seq_ends - lengths_row
    inside = ((blocks[:, None] >= starts[None, :]) & (blocks[:, None] < seq_ends[None, :])).astype(
        jnp.int32
    )
    seq_first = jnp.sum(inside * starts[None, :], axis=1)
    seq_count = jnp.sum(inside * lengths_row[None, :], axis=1)
    position = blocks - seq_first
    has_before = position > 0
    has_behind = position < seq_count - 1
    before = jnp.where(has_before, blocks - 1, blocks)
    behind = jnp.where(has_behind, blocks + 1, blocks)
    fixed_ids = jnp.stack([before, blocks, behind, seq_first, seq_first + 1], axis=-1)
    random_ids = seq_first[:, None, None] + offsets % seq_count[:, None, None]
    head_count = offsets.shape[1]
    key_table = jnp.concatenate(
        [jnp.broadcast_to(fixed_ids[:, None, :], (blocks.shape[0], head_count, 5)), random_ids],
        axis=-1,
    )
    always = jnp.ones_like(has_before)
    usable = jnp.stack(
        [has_before, always, has_behind, always, always] + [always] * offsets.shape[2], axis=-1
    )
    return (key_table, usable)


def scores_of(query, key_sel, usable, scale):
    raw = contract("bqhd,bhkcd->bhqkc", query, key_sel)
    return jnp.where(usable[:, None, None, :, None], raw * scale, -1e30)


def per_device(
    inputs,
    qkv_weight,
    out_weight,
    up_weight,
    down_weight,
    norm_gains,
    norm_biases,
    lengths,
    random_blocks,
    out_grad,
):
    w_qkv, w_out, w_up, w_down, gains_low, biases_low = (
        lax.all_gather(qkv_weight, "dp", axis=1, tiled=True),
        lax.all_gather(out_weight, "dp", axis=1, tiled=True),
        lax.all_gather(up_weight, "dp", axis=0, tiled=True),
        lax.all_gather(down_weight, "dp", axis=1, tiled=True),
        lax.all_gather(norm_gains, "dp", axis=1, tiled=True),
        lax.all_gather(norm_biases, "dp", axis=1, tiled=True),
    )
    gains = gains_low.astype(jnp.float32)
    biases = biases_low.astype(jnp.float32)
    rows = inputs.shape[0]
    own_blocks = rows // BLOCK
    local_width = w_qkv.shape[2]
    local_heads = local_width // HD
    scale = 1.0 / math.sqrt(HD)
    x_float = inputs.astype(jnp.float32)
    projected = contract("td,kde->kte", inputs, w_qkv)
    q_low = projected[0].astype(jnp.bfloat16)
    k_low = projected[1].astype(jnp.bfloat16)
    v_low = projected[2].astype(jnp.bfloat16)
    key_all, value_all = (
        lax.all_gather(k_low, "ctx", axis=0, tiled=True),
        lax.all_gather(v_low, "ctx", axis=0, tiled=True),
    )
    group_blocks = key_all.shape[0] // BLOCK
    first_block = lax.axis_index("ctx") * own_blocks
    blocks = first_block + jnp.arange(own_blocks, dtype=jnp.int32)
    key_table, usable = block_table(blocks, lengths[0], random_blocks)
    head_pick = jnp.arange(local_heads, dtype=jnp.int32)[None, :, None]
    key_blocks = key_all.reshape(group_blocks, BLOCK, local_heads, HD)
    value_blocks = value_all.reshape(group_blocks, BLOCK, local_heads, HD)
    key_sel = key_blocks[key_table, :, head_pick, :]
    value_sel = value_blocks[key_table, :, head_pick, :]
    query = q_low.reshape(own_blocks, BLOCK, local_heads, HD)
    scores = scores_of(query, key_sel, usable, scale)
    top = jnp.max(scores, axis=(3, 4), keepdims=True)
    log_total = top + jnp.log(jnp.sum(jnp.exp(scores - top), axis=(3, 4), keepdims=True))
    probs = jnp.exp(scores - log_total)
    probs_low = probs.astype(jnp.bfloat16)
    attended = (
        contract("bhqkc,bhkcd->bqhd", probs_low, value_sel)
        .reshape(rows, local_width)
        .astype(jnp.bfloat16)
    )
    attn_sum = lax.psum(
        jnp.dot(attended, w_out, preferred_element_type=jnp.float32).astype(jnp.bfloat16), "tp"
    ).astype(jnp.float32)
    first_sum = x_float + attn_sum
    normed, norm_pull = jax.vjp(layer_norm, first_sum, gains[0], biases[0])
    normed_low = normed.astype(jnp.bfloat16)
    hidden = jnp.dot(normed_low, w_up, preferred_element_type=jnp.float32)
    activated, gelu_pull = jax.vjp(gelu_tanh, hidden)
    act_low = activated.astype(jnp.bfloat16)
    mlp_sum = lax.psum(
        jnp.dot(act_low, w_down, preferred_element_type=jnp.float32).astype(jnp.bfloat16), "tp"
    ).astype(jnp.float32)
    second_sum = normed + mlp_sum
    result, final_pull = jax.vjp(layer_norm, second_sum, gains[1], biases[1])
    d_second, d_gain_two, d_bias_two = final_pull(out_grad.astype(jnp.float32))
    d_mlp = d_second.astype(jnp.bfloat16)
    grad_down = contract("tf,td->fd", act_low, d_mlp)
    d_act = contract("td,fd->tf", d_mlp, w_down)
    d_hidden = gelu_pull(d_act)[0].astype(jnp.bfloat16)
    grad_up = contract("td,tf->df", normed_low, d_hidden)
    d_normed = d_second + lax.psum(
        contract("tf,df->td", d_hidden, w_up).astype(jnp.bfloat16), "tp"
    ).astype(jnp.float32)
    d_first, d_gain_one, d_bias_one = norm_pull(d_normed)
    d_attn = d_first.astype(jnp.bfloat16)
    grad_proj = contract("te,td->ed", attended, d_attn)
    d_attended = (
        contract("td,ed->te", d_attn, w_out)
        .astype(jnp.bfloat16)
        .reshape(own_blocks, BLOCK, local_heads, HD)
    )
    scores = scores_of(query, key_sel, usable, scale)
    probs = jnp.exp(scores - log_total)
    probs_low = probs.astype(jnp.bfloat16)
    d_probs = contract("bqhd,bhkcd->bhqkc", d_attended, value_sel)
    d_scores = probs * (d_probs - jnp.sum(probs * d_probs, axis=(3, 4), keepdims=True))
    d_raw = (d_scores * scale).astype(jnp.bfloat16)
    d_query = (
        contract("bhqkc,bhkcd->bqhd", d_raw, key_sel)
        .reshape(rows, local_width)
        .astype(jnp.bfloat16)
    )
    d_key_sel = contract("bhqkc,bqhd->bhkcd", d_raw, query)
    d_value_sel = contract("bhqkc,bqhd->bhkcd", probs_low, d_attended)
    empty = jnp.zeros((group_blocks, BLOCK, local_heads, HD), jnp.float32)
    d_key_all = (
        empty.at[key_table, :, head_pick, :]
        .add(d_key_sel)
        .reshape(group_blocks * BLOCK, local_width)
    )
    d_value_all = (
        empty.at[key_table, :, head_pick, :]
        .add(d_value_sel)
        .reshape(group_blocks * BLOCK, local_width)
    )
    d_key, d_value = (
        lax.psum_scatter(
            d_key_all.astype(jnp.bfloat16), "ctx", scatter_dimension=0, tiled=True
        ).astype(jnp.float32),
        lax.psum_scatter(
            d_value_all.astype(jnp.bfloat16), "ctx", scatter_dimension=0, tiled=True
        ).astype(jnp.float32),
    )
    d_projected = jnp.stack([d_query, d_key.astype(jnp.bfloat16), d_value.astype(jnp.bfloat16)])
    grad_qkv = contract("td,kte->kde", inputs, d_projected)
    d_inputs = d_first + lax.psum(
        contract("kte,kde->td", d_projected, w_qkv).astype(jnp.bfloat16), "tp"
    ).astype(jnp.float32)
    grad_gains = jnp.stack([d_gain_one, d_gain_two])
    grad_biases = jnp.stack([d_bias_one, d_bias_two])
    shared = (
        lax.psum_scatter(
            grad_qkv.astype(jnp.bfloat16), "dp", scatter_dimension=1, tiled=True
        ).astype(jnp.float32),
        lax.psum_scatter(
            grad_proj.astype(jnp.bfloat16), "dp", scatter_dimension=1, tiled=True
        ).astype(jnp.float32),
        lax.psum_scatter(
            grad_up.astype(jnp.bfloat16), "dp", scatter_dimension=0, tiled=True
        ).astype(jnp.float32),
        lax.psum_scatter(
            grad_down.astype(jnp.bfloat16), "dp", scatter_dimension=1, tiled=True
        ).astype(jnp.float32),
        lax.psum_scatter(
            grad_gains.astype(jnp.bfloat16), "dp", scatter_dimension=1, tiled=True
        ).astype(jnp.float32),
        lax.psum_scatter(
            grad_biases.astype(jnp.bfloat16), "dp", scatter_dimension=1, tiled=True
        ).astype(jnp.float32),
    )
    totals = (
        lax.psum(shared[0].astype(jnp.bfloat16), "ctx").astype(jnp.float32),
        lax.psum(shared[1].astype(jnp.bfloat16), "ctx").astype(jnp.float32),
        lax.psum(shared[2].astype(jnp.bfloat16), "ctx").astype(jnp.float32),
        lax.psum(shared[3].astype(jnp.bfloat16), "ctx").astype(jnp.float32),
        lax.psum(shared[4].astype(jnp.bfloat16), "ctx").astype(jnp.float32),
        lax.psum(shared[5].astype(jnp.bfloat16), "ctx").astype(jnp.float32),
    )
    return (
        result.astype(jnp.bfloat16),
        d_inputs.astype(jnp.bfloat16),
        totals[0],
        totals[1],
        totals[2],
        totals[3],
        totals[4],
        totals[5],
    )


def mul(left, right, left_dim, right_dim):
    dims = (((left_dim,), (right_dim,)), ((), ()))
    return lax.dot_general(left, right, dims, preferred_element_type=jnp.float32)


def call(body, outs, *args, scratch=(), copies=0, spec=None, room=32, flops=0):
    spec = spec or pl.BlockSpec(memory_space=pltpu.VMEM)
    specs = [spec] * len(args)
    shapes = [jax.ShapeDtypeStruct(shape, dtype) for shape, dtype in outs]
    return pl.pallas_call(
        body,
        out_shape=shapes,
        in_specs=specs,
        out_specs=[pl.BlockSpec(memory_space=pltpu.VMEM)] * len(shapes),
        scratch_shapes=[pltpu.VMEM(shape, dtype) for shape, dtype in scratch]
        + ([pltpu.SemaphoreType.DMA((copies,))] if copies else []),
        compiler_params=pltpu.CompilerParams(vmem_limit_bytes=room << 20),
        cost_estimate=pl.CostEstimate(flops=flops, bytes_accessed=0, transcendentals=0),
    )(*args)


def head_masks(width):
    lane = lax.broadcasted_iota(jnp.int32, (1, width), 1)
    return [(lane >= h * HD) & (lane < (h + 1) * HD) for h in range(width // HD)]


def only(values, mask):
    return jnp.where(mask, values, jnp.zeros_like(values))


def biased(raw, bias, scale):
    blocks = bias.shape[0]
    size = raw.shape[0] // blocks
    return jnp.concatenate(
        [raw[j * size : (j + 1) * size] * scale + bias[j : j + 1] for j in range(blocks)], axis=0
    )


DIRECT = (0, 2, 4, 6, 1, 3, 5, 7)
OUT_WAYS = (0, 1, 4, 5, 2, 3, 6, 7)
UP_WAYS = (0, 4, 2, 6, 1, 5, 3, 7)
DOWN_WAYS = (0, 4, 1, 5, 2, 6, 3, 7)


def place(pieces, all_ref, ways, window=0):
    width = all_ref.shape[1]
    parts = []
    for piece in pieces:
        parts += [piece] if len(piece.shape) == 2 else [piece.at[i] for i in range(piece.shape[0])]
    for part, bits in zip(parts, ways, strict=True):
        shard = part.shape[0]
        owner = lax.axis_index("dp") ^ bits
        start = window if part.shape[1] > width else 0
        all_ref[pl.ds(pl.multiple_of(owner * shard, 32), shard), :] = part[:, start : start + width]


def fetch(pairs, sems):
    copies = [pltpu.make_async_copy(src, dst, sems.at[i]) for i, (src, dst) in enumerate(pairs)]
    for copy in copies:
        copy.start()
    for copy in copies:
        copy.wait()


def own_half(src, dst):
    n = dst.shape[1]
    dst[...] = jnp.where(lax.axis_index("ctx") == 0, src[:, :n], src[:, n:])


def pack_first_body(qkv_hbm, gain_hbm, bias_hbm, out_hbm, w_ref, pack_ref, qkv, gain, bias, out, sems):
    fetch(((qkv_hbm, qkv), (gain_hbm, gain), (bias_hbm, bias), (out_hbm, out)), sems)
    c = lax.axis_index("ctx")
    n = qkv.shape[2] // 2
    for i in range(3):
        w_ref[:, i * n : (i + 1) * n] = jnp.where(c == 0, qkv[i, :, :n], qkv[i, :, n:])
    first = w_ref.shape[1]
    row = lax.broadcasted_iota(jnp.int32, (2, first - 3 * n), 0)
    lane = lax.broadcasted_iota(jnp.int32, (2, first - 3 * n), 1)
    cols = mul(gain[...], (row == lane).astype(jnp.bfloat16), 0, 0)
    cols = cols + mul(bias[...], (row + 2 == lane).astype(jnp.bfloat16), 0, 0)
    w_ref[:, 3 * n :] = cols.astype(jnp.bfloat16)
    m = out.shape[1] // 2
    pack_ref[:, 0:first] = w_ref[...]
    pack_ref[:, first:] = jnp.where(c == 0, out[:, :m], out[:, m:])


def pack_second_body(up_hbm, down_hbm, up_ref, down_ref, up, down, sems):
    fetch(((up_hbm, up), (down_hbm, down)), sems)
    own_half(up, up_ref)
    own_half(down, down_ref)


def attend_body(
    own_ref, far_ref, w0, w1, w2, w3, w4, w5, bias_ref,
    o_ref, qkv_ref, lse_ref, vec_ref, x_ref, w_ref, p_scr, v_scr,
):
    width = o_ref.shape[1]
    rows = x_ref.shape[0]
    part = far_ref.shape[0] // 2
    c = lax.axis_index("ctx")
    for t in range(2):
        x_ref[pl.ds((2 * t + c) * part, part), :] = own_ref[t * part : (t + 1) * part, :]
        x_ref[pl.ds((2 * t + 1 - c) * part, part), :] = far_ref[t * part : (t + 1) * part, :]
    place((w0, w1, w2, w3, w4, w5), w_ref, DIRECT)
    scale = 1.0 / math.sqrt(HD)
    w = w_ref[...]
    qkv = mul(x_ref[...], w, 1, 0).astype(jnp.bfloat16)
    qkv_ref[...] = qkv[:, : 3 * width]
    vec = w[:, 3 * width :]
    unit = (
        lax.broadcasted_iota(jnp.int32, (8, vec.shape[1]), 0) == lax.broadcasted_iota(jnp.int32, (8, vec.shape[1]), 1)
    ).astype(jnp.bfloat16)
    vec_ref[...] = mul(unit, vec, 1, 1)
    q, k, v = [qkv[:, i * width : (i + 1) * width] for i in range(3)]
    lse_ref[...] = jnp.zeros_like(lse_ref)
    blocks = bias_ref.shape[0] // (width // HD)
    for h, mask in enumerate(head_masks(width)):
        s = biased(mul(k, only(q, mask), 1, 1), bias_ref[h * blocks : (h + 1) * blocks, :], scale)
        top = jnp.max(s, axis=0, keepdims=True)
        e = jnp.exp(s - top)
        total = jnp.sum(e, axis=0, keepdims=True)
        lse_ref[h : h + 1, :] = top + jnp.log(total)
        p_scr[h * rows : (h + 1) * rows, :] = (e * (1.0 / total)).astype(jnp.bfloat16)
        v_scr[h * rows : (h + 1) * rows, :] = only(v, mask)
    o_ref[...] = mul(p_scr[...], v_scr[...], 0, 0).astype(jnp.bfloat16)


def split_rows(value_of, mine_ref, theirs_ref):
    half = mine_ref.shape[0]
    t = lax.axis_index("tp")
    theirs_ref[...] = value_of(pl.ds((1 - t) * half, half)).astype(theirs_ref.dtype)
    mine_ref[...] = value_of(pl.ds(t * half, half))


def project_body(ways, window, o_ref, *refs):
    *pieces, mine_ref, theirs_ref, w_ref = refs
    place(pieces, w_ref, ways, window)
    split_rows(lambda rows: mul(o_ref[rows, :], w_ref[...], 1, 1), mine_ref, theirs_ref)


def add_tp_body(mine_ref, both_ref, sum_ref):
    sum_ref[...] = (mine_ref[...] + both_ref[1 - lax.axis_index("tp")].astype(jnp.float32)).astype(jnp.bfloat16)


def norm_parts(z):
    centred = z - jnp.mean(z, axis=1, keepdims=True)
    r = lax.rsqrt(jnp.mean(centred * centred, axis=1, keepdims=True) + eps)
    return centred * r, r


def norm_back(e2, n, r):
    return r * (e2 - jnp.mean(e2, axis=1, keepdims=True) - n * jnp.mean(e2 * n, axis=1, keepdims=True))


def norm_one_body(x_ref, a_ref, far_ref, vec_ref, n_ref, r_ref, low_ref):
    half = n_ref.shape[0]
    z = x_ref[pl.ds(lax.axis_index("tp") * half, half), :].astype(jnp.float32)
    z = z + (a_ref[...].astype(jnp.float32) + far_ref[...].astype(jnp.float32))
    n, r = norm_parts(z)
    n_ref[...] = n
    r_ref[...] = jnp.broadcast_to(r, r_ref.shape)
    low_ref[...] = (n * vec_ref[0:1, :] + vec_ref[2:3, :]).astype(jnp.bfloat16)


def ffn_body(y_ref, w0, w1, w2, w3, u_ref, slope_ref, up_ref):
    place((w0, w1, w2, w3), up_ref, UP_WAYS)
    hid = mul(y_ref[...], up_ref[...], 1, 0)
    root = math.sqrt(2.0 / math.pi)
    square = hid * hid
    bent = jnp.tanh(root * (hid + 0.044715 * (square * hid)))
    u_ref[...] = (0.5 * hid * (1.0 + bent)).astype(jnp.bfloat16)
    slope = 0.5 * (1.0 + bent) + 0.5 * hid * (1.0 - bent * bent) * (root * (1.0 + 3 * 0.044715 * square))
    slope_ref[...] = slope.astype(jnp.bfloat16)


def norm_two_body(n1_ref, m_ref, far_ref, e_ref, e_far_ref, vec_ref, out_ref, dz_ref, low_ref, grad_ref, e_scr, out_scr):
    part = out_ref.shape[0]
    c, t = lax.axis_index("ctx"), lax.axis_index("tp")
    e_scr[pl.ds(c * part, part), :] = e_ref[pl.ds(t * part, part), :].astype(jnp.float32)
    e_scr[pl.ds((1 - c) * part, part), :] = e_far_ref[pl.ds(t * part, part), :].astype(jnp.float32)
    y1 = n1_ref[...] * vec_ref[0:1, :] + vec_ref[2:3, :]
    z = y1 + (m_ref[...].astype(jnp.float32) + far_ref[...].astype(jnp.float32))
    n, r = norm_parts(z)
    out_scr[...] = n * vec_ref[1:2, :] + vec_ref[3:4, :]
    out_ref[...] = out_scr[pl.ds(c * part, part), :].astype(jnp.bfloat16)
    e = e_scr[...]
    dz = norm_back(e * vec_ref[1:2, :], n, r)
    dz_ref[...] = dz
    low_ref[...] = dz.astype(jnp.bfloat16)
    grad_ref[...] = jnp.zeros_like(grad_ref)
    grad_ref[1:2, :] = jnp.sum(e * n, axis=0, keepdims=True)
    grad_ref[3:4, :] = jnp.sum(e, axis=0, keepdims=True)


def ffn_back_body(dm_ref, slope_ref, down_ref, up_ref, dhid_ref, mine_ref, theirs_ref):
    du = mul(dm_ref[...], down_ref[...], 1, 0)
    dhid_ref[...] = (du * slope_ref[...].astype(jnp.float32)).astype(jnp.bfloat16)
    split_rows(lambda rows: mul(dhid_ref[rows, :], up_ref[...], 1, 1), mine_ref, theirs_ref)


def deal(own_ref, away_ref, scr, order, start=0):
    one, two, three = order
    shard, width = own_ref.shape[1:]
    dp = lax.axis_index("dp")
    for i, bits in enumerate((0, three, two, two ^ three)):
        for ref, owner in ((own_ref, dp ^ bits), (away_ref, dp ^ bits ^ one)):
            part = scr[pl.ds(pl.multiple_of(owner * shard, 32), shard), start : start + width]
            ref[i] = part.astype(ref.dtype)


def grad_body(order, left_ref, right_ref, own_ref, away_ref, scr):
    scr[...] = mul(left_ref[...], right_ref[...], 0, 0)
    deal(own_ref, away_ref, scr, order)


def fold_pair(own_ref, got_ref, keep_ref, send_ref):
    half = keep_ref.shape[0]
    keep_ref[...] = own_ref[0:half] + got_ref[0:half].astype(jnp.float32)
    send_ref[...] = (own_ref[half:] + got_ref[half:].astype(jnp.float32)).astype(jnp.bfloat16)


def fold_body(own_ref, got_ref, keep_ref, send_ref):
    fold_pair(own_ref, got_ref, keep_ref, send_ref)


def fold_two_body(own_ref, got_ref, own2_ref, got2_ref, keep_ref, send_ref, keep2_ref, send2_ref):
    fold_pair(own_ref, got_ref, keep_ref, send_ref)
    fold_pair(own2_ref, got2_ref, keep2_ref, send2_ref)


def fold_join_body(own_ref, got_ref, own2_ref, got2_ref, keep_ref, send_ref):
    width = own_ref.shape[2]
    for own, got, lanes in ((own_ref, got_ref, slice(0, width)), (own2_ref, got2_ref, slice(width, keep_ref.shape[2]))):
        keep_ref[0, :, lanes] = own[0] + got[0].astype(jnp.float32)
        send_ref[0, :, lanes] = (own[1] + got[1].astype(jnp.float32)).astype(jnp.bfloat16)


def fold_last_body(own_ref, got_ref, sum_ref):
    sum_ref[...] = (own_ref[0] + got_ref[0].astype(jnp.float32)).astype(jnp.bfloat16)


def norm_one_back_body(dz2_ref, d_ref, far_ref, n_ref, r_ref, vec_ref, grad2_ref, dz_ref, low_ref):
    dy = dz2_ref[...] + (d_ref[...].astype(jnp.float32) + far_ref[...].astype(jnp.float32))
    n = n_ref[...]
    dz = norm_back(dy * vec_ref[0:1, :], n, r_ref[:, 0:1])
    dz_ref[...] = dz
    half = dz.shape[0]
    low_ref[0:half, :] = dz.astype(jnp.bfloat16)
    sums = [
        jnp.sum(dy * n, axis=0, keepdims=True), grad2_ref[1:2, :],
        jnp.sum(dy, axis=0, keepdims=True), grad2_ref[3:4, :], jnp.zeros((12, dz.shape[1]), jnp.float32),
    ]
    low_ref[half : half + 16, :] = jnp.concatenate(sums, axis=0).astype(jnp.bfloat16)


def attend_back_body(
    da_ref, w_out_ref, w_ref, qkv_ref, o_ref, lse_ref, bias_ref, x_ref,
    own_ref, away_ref, own2_ref, away2_ref, mine_ref, theirs_ref,
    p_scr, dr_scr, q_scr, do_scr, all_scr, grad_scr,
):
    width = o_ref.shape[1]
    rows = x_ref.shape[0]
    scale = 1.0 / math.sqrt(HD)
    half = rows // 2
    da = jnp.concatenate([da_ref[0, 0:half, :], da_ref[1, 0:half, :]], axis=0)
    do = mul(da, w_out_ref[...], 1, 0).astype(jnp.bfloat16)
    q, k, v = [qkv_ref[:, i * width : (i + 1) * width] for i in range(3)]
    blocks = bias_ref.shape[0] // (width // HD)
    dq = jnp.zeros((rows, width), jnp.float32)
    for h, mask in enumerate(head_masks(width)):
        q_h, do_h = only(q, mask), only(do, mask)
        s = biased(mul(k, q_h, 1, 1), bias_ref[h * blocks : (h + 1) * blocks, :], scale)
        p = jnp.exp(s - lse_ref[h : h + 1, :])
        dp = mul(v, do_h, 1, 1)
        pd = p * dp
        ds = pd - p * jnp.sum(pd, axis=0, keepdims=True)
        dr = (ds * scale).astype(jnp.bfloat16)
        p_scr[:, h * rows : (h + 1) * rows] = p.astype(jnp.bfloat16)
        dr_scr[:, h * rows : (h + 1) * rows] = dr
        q_scr[h * rows : (h + 1) * rows, :] = q_h
        do_scr[h * rows : (h + 1) * rows, :] = do_h
        dq = dq + mul(dr, only(k, mask), 0, 0)
    all_scr[:, 0:width] = dq.astype(jnp.bfloat16)
    all_scr[:, width : 2 * width] = mul(dr_scr[...], q_scr[...], 1, 0).astype(jnp.bfloat16)
    all_scr[:, 2 * width : 3 * width] = mul(p_scr[...], do_scr[...], 1, 0).astype(jnp.bfloat16)
    vec = sum(da_ref[i, half : half + 16, :].astype(jnp.float32) for i in range(2)).astype(jnp.bfloat16)
    extra = w_ref.shape[1] - 3 * width
    unit = (
        lax.broadcasted_iota(jnp.int32, (16, extra), 0) == lax.broadcasted_iota(jnp.int32, (16, extra), 1)
    ).astype(jnp.bfloat16)
    grad_scr[...] = jnp.concatenate(
        [mul(x_ref[...], all_scr[...], 0, 0), mul(vec, unit, 0, 0), mul(da, o_ref[...], 0, 0)], axis=1
    )
    deal(own_ref, away_ref, grad_scr, (1, 2, 4))
    deal(own2_ref, away2_ref, grad_scr, (2, 1, 4), own_ref.shape[2])
    w = w_ref[:, 0 : 3 * width]
    split_rows(lambda r: mul(all_scr[r, :], w, 1, 1), mine_ref, theirs_ref)


def fold_input_body(mine_ref, both_ref, dz_ref, keep_ref, send_ref):
    part = keep_ref.shape[0]
    c, far = lax.axis_index("ctx"), 1 - lax.axis_index("tp")
    own, other = pl.ds(c * part, part), pl.ds((1 - c) * part, part)
    send_ref[...] = (mine_ref[other, :] + both_ref[far, other, :].astype(jnp.float32)).astype(jnp.bfloat16)
    keep_ref[...] = dz_ref[own, :] + (mine_ref[own, :] + both_ref[far, own, :].astype(jnp.float32))


def last_input_body(keep_ref, got_ref, out_ref):
    out_ref[...] = (keep_ref[...] + got_ref[...].astype(jnp.float32)).astype(jnp.bfloat16)


def copy_body(in_ref, out_ref):
    out_ref[...] = in_ref[...]


def finish_body(near_ref, far_ref, qkv_ref, out_ref, gain_ref, bias_ref):
    c = lax.axis_index("ctx")
    n = qkv_ref.shape[2] // 2
    m = out_ref.shape[1] // 2
    near, far = near_ref[...].astype(jnp.float32), far_ref[...].astype(jnp.float32)
    low, high = jnp.where(c == 0, near, far), jnp.where(c == 0, far, near)
    for i in range(3):
        qkv_ref[i] = jnp.concatenate([low[:, i * n : (i + 1) * n], high[:, i * n : (i + 1) * n]], axis=1)
    out_ref[...] = jnp.concatenate([low[:, low.shape[1] - m :], high[:, high.shape[1] - m :]], axis=1)
    vec = near_ref[:, 3 * n : near_ref.shape[1] - m]
    row = lax.broadcasted_iota(jnp.int32, (2, vec.shape[1]), 0)
    lane = lax.broadcasted_iota(jnp.int32, (2, vec.shape[1]), 1)
    gain_ref[...] = mul((row == lane).astype(jnp.bfloat16), vec, 1, 1)
    bias_ref[...] = mul((row + 2 == lane).astype(jnp.bfloat16), vec, 1, 1)


def rows_device(
    dims,
    inputs,
    qkv_weight,
    out_weight,
    up_weight,
    down_weight,
    norm_gains,
    norm_biases,
    lengths,
    random_blocks,
    out_grad,
):
    n_dp = dims["dp"]
    n_out = n_dp // 2
    c = lax.axis_index("ctx")
    f32, bf16 = jnp.float32, jnp.bfloat16
    pair = [(0, 1), (1, 0)]

    def both_tp(v, tiled=False):
        return lax.all_gather(v, "tp", axis=0, tiled=tiled)

    def swap_ctx(v):
        return lax.ppermute(v, "ctx", pair)

    def swap_dp(v, bits):
        return lax.ppermute(v, "dp", [(i, i ^ bits) for i in range(n_dp)])

    def after(v, *others):
        return lax.optimization_barrier((v,) + others)[0]

    def all_after(vs, *others):
        return list(lax.optimization_barrier(tuple(vs) + others)[: len(vs)])

    rows, width = inputs.shape
    part = rows // 2
    shard = qkv_weight.shape[1]
    cols = qkv_weight.shape[2] // 2
    units = up_weight.shape[1] // 2
    heads = cols // HD
    own_blocks = rows // BLOCK
    per = own_blocks // 2
    total_rows = 2 * rows
    first = 3 * cols + 4 + (-(3 * cols + 4)) % 128

    half = ((part, width), bf16)
    hbm = pl.BlockSpec(memory_space=pltpu.HBM)

    def packed(body, widths, *given):
        return call(
            body, [((shard, n), bf16) for n in widths], *given,
            scratch=[(w.shape, bf16) for w in given], copies=len(given), spec=hbm, room=60,
        )

    x_far = swap_ctx(inputs)
    w1, pack_one = packed(
        pack_first_body, (first, first + cols), qkv_weight, norm_gains, norm_biases, out_weight.T
    )
    w1_near = [swap_dp(w1, 2 * k) for k in range(1, n_out)]
    far_one = swap_dp(pack_one, 1)
    w_up, w_down = packed(pack_second_body, (units, units), up_weight, down_weight.T)
    picks_far = swap_ctx(random_blocks)
    w1_near = all_after(w1_near, far_one)
    w1_pieces = [w1, *w1_near, far_one, swap_dp(jnp.stack(w1_near), 1)]
    out_pieces = [jnp.stack([pack_one[:, first:], far_one[:, first:]])]
    out_pieces[0] = after(out_pieces[0], *w1_near)
    out_pieces.append(swap_dp(out_pieces[0], 4))
    out_pieces.append(swap_dp(jnp.concatenate(out_pieces), 2))
    up_pieces, down_pieces = all_after([w_up[None], w_down[None]], out_pieces[1])
    up_pieces = [up_pieces, swap_dp(up_pieces, 4)]
    down_pieces = [down_pieces, swap_dp(down_pieces, 4)]
    e_far = swap_ctx(after(out_grad, *w1_near))

    picks = jnp.where(c == 0, jnp.stack([random_blocks, picks_far]), jnp.stack([picks_far, random_blocks]))
    picks = lax.dynamic_slice_in_dim(picks.reshape(2 * own_blocks, 2 * heads, 3), c * heads, heads, 1)
    blocks = jnp.arange(2 * own_blocks, dtype=jnp.int32)
    table, usable = block_table(blocks, lengths[0], picks)
    named = (table[..., None] == blocks) & usable[:, None, :, None]
    counts = jnp.sum(named.astype(f32), axis=2)
    counts = counts.reshape(2, 2, per, heads, 2, 2, per).transpose(3, 5, 4, 6, 1, 0, 2)
    bias = jnp.where(counts > 0, jnp.log(jnp.maximum(counts, 1.0)), -1e30)
    bias = bias.reshape(heads * 2 * own_blocks, 2 * own_blocks, 1)
    bias = jnp.broadcast_to(bias, bias.shape[:2] + (BLOCK,)).reshape(-1, total_rows)

    low = [((rows, width), bf16)]
    wide = [((rows, width), f32)]
    small = [((8, width), f32)]
    o, qkv, lse, vecs, x_all, w1_all = call(
        attend_body,
        [
            ((total_rows, cols), bf16), ((total_rows, 3 * cols), bf16), ((8, total_rows), f32), ((8, width), f32),
            ((total_rows, width), bf16), ((width, first), bf16),
        ],
        inputs, x_far, *w1_pieces, bias,
        scratch=[((heads * total_rows, total_rows), bf16), ((heads * total_rows, cols), bf16)],
        flops=0,
    )

    def sum_tp(mine, theirs):
        return call(add_tp_body, low, mine, both_tp(theirs))[0]

    mine, theirs, w_out_all = call(
        functools.partial(project_body, OUT_WAYS, 0), wide + low + [((width, cols), bf16)], o, *out_pieces
    )
    theirs, up_pieces[1], down_pieces[1] = all_after([theirs, up_pieces[1], down_pieces[1]])
    up_pieces.append(swap_dp(jnp.concatenate(up_pieces), 2))
    down_pieces.append(swap_dp(jnp.concatenate(down_pieces), 1))
    a = after(sum_tp(mine, theirs), e_far)
    a_far = swap_ctx(a)
    up_pieces.append(swap_dp(jnp.concatenate(up_pieces), 1))
    down_pieces.append(swap_dp(jnp.concatenate(down_pieces), 2))
    n1, r1, y_low = call(norm_one_body, wide + [((rows, 128), f32)] + low, x_all, a, a_far, vecs)
    flat = [((total_rows, units), bf16)]
    square = [((width, units), bf16)]
    y_all = both_tp(y_low, True)
    u, slope, w_up_all = call(ffn_body, flat * 2 + square, y_all, *up_pieces)
    mine, theirs, w_down_all = call(functools.partial(project_body, DOWN_WAYS, 0), wide + low + square, u, *down_pieces)
    m = sum_tp(mine, theirs)
    m_far = swap_ctx(m)
    out, dz2, dm_low, grad2 = call(
        norm_two_body,
        [((part, width), bf16)] + wide + low + small,
        n1, m, m_far, out_grad, e_far, vecs,
        scratch=wide * 2,
    )

    def dealt(n):
        return [((n_out, shard, n), f32), ((n_out, shard, n), bf16)]

    def kept(k, n):
        return [((k, shard, n), f32), ((k, shard, n), bf16)]

    def fold(own, got):
        return call(fold_body, kept(own.shape[0] // 2, own.shape[2]), own, got)

    def last_sum(keep, send, bits):
        total = call(fold_last_body, [(keep.shape[1:], bf16)], keep, swap_dp(send, bits))[0]
        return total, swap_ctx(total)

    down_order, up_order = (2, 1, 4), (1, 2, 4)
    dm_all = both_tp(dm_low, True)
    down_own, down_away = call(functools.partial(grad_body, down_order), dealt(units), dm_all, u, scratch=[((width, units), f32)])
    dm_all = after(dm_all, down_away)
    dhid, mine, theirs = call(
        ffn_back_body, flat + wide + low, dm_all, slope, w_down_all, w_up_all
    )
    d = sum_tp(mine, theirs)
    d_far = swap_ctx(d)
    y_late, dhid = lax.optimization_barrier((y_all, dhid, d))[:2]
    up_own, up_away = call(functools.partial(grad_body, up_order), dealt(units), y_late, dhid, scratch=[((width, units), f32)])
    dz1, da_low = call(
        norm_one_back_body, wide + [((rows + 16, width), bf16)], dz2, d, after(d_far, up_away), n1, r1, vecs, grad2
    )
    down_keep, down_send = fold(down_own, swap_dp(down_away, down_order[0]))
    last = first + cols
    left = last // 256 * 128
    own, away, own2, away2, mine, theirs = call(
        attend_back_body,
        dealt(left) + dealt(last - left) + wide + low,
        after(both_tp(da_low), down_send), w_out_all, w1_all, qkv, o, lse, bias, x_all,
        scratch=[
            ((total_rows, heads * total_rows), bf16),
            ((total_rows, heads * total_rows), bf16),
            ((heads * total_rows, cols), bf16),
            ((heads * total_rows, cols), bf16),
            ((total_rows, 3 * cols), bf16),
            ((width, last), f32),
        ],
    )
    up_own = after(up_own, theirs)
    keep, send = call(fold_input_body, [((part, width), f32), half], mine, both_tp(theirs), dz1)
    down_keep, down_send = fold(down_keep, swap_dp(down_send, down_order[1]))
    keep1, send1, keep2, send2 = call(
        fold_two_body, kept(2, left) + kept(2, last - left),
        own, swap_dp(away, 1), own2, swap_dp(away2, 2),
    )
    up_keep, up_send = fold(after(up_own, keep1), swap_dp(up_away, up_order[0]))
    keep1, send1 = call(
        fold_join_body, kept(1, last), keep1, swap_dp(send1, 2), keep2, swap_dp(send2, 1)
    )
    up_keep, up_send = fold(after(up_keep, keep1), swap_dp(up_send, up_order[1]))
    grad_down, down_far = last_sum(down_keep, down_send, 4)
    grad_up, up_far = last_sum(up_keep, up_send, 4)
    grad_1, far_1 = last_sum(keep1, send1, 4)
    dx = call(last_input_body, [half], keep, swap_ctx(send))[0]
    output, input_grad = [call(copy_body, low, both_tp(v, True))[0] for v in (out, dx)]

    def both_ctx(g, far):
        return jnp.where(c == 0, jnp.concatenate([g, far], 1), jnp.concatenate([far, g], 1)).astype(f32)

    grad_qkv, grad_out, gains, biases = call(
        finish_body,
        [((3, shard, 2 * cols), f32), ((shard, 2 * cols), f32), ((2, shard), f32), ((2, shard), f32)],
        grad_1, far_1,
    )
    return (
        output, input_grad, grad_qkv, grad_out.T, both_ctx(grad_up, up_far), both_ctx(grad_down, down_far).T, gains, biases
    )


def solution(mesh):
    dims = dict(mesh.shape)
    fast = dims["ctx"] == 2 and dims["tp"] == 2 and dims["dp"] == 8
    step = functools.partial(rows_device, dims) if fast else per_device
    return jax.shard_map(
        step,
        mesh=mesh,
        in_specs=(
            P(("dp", "ctx"), None),
            P(None, "dp", "tp"),
            P("tp", "dp"),
            P("dp", "tp"),
            P("tp", "dp"),
            P(None, "dp"),
            P(None, "dp"),
            P("dp", None),
            P(("dp", "ctx"), "tp", None),
            P(("dp", "ctx"), None),
        ),
        out_specs=(
            P(("dp", "ctx"), None),
            P(("dp", "ctx"), None),
            P(None, "dp", "tp"),
            P("tp", "dp"),
            P("dp", "tp"),
            P("tp", "dp"),
            P(None, "dp"),
            P(None, "dp"),
        ),
        check_vma=False,
    )
```

```python
import functools
import math

import jax
import jax.numpy as jnp
from jax import lax
from jax.experimental import pallas as pl
from jax.experimental.pallas import tpu as pltpu
from jax.sharding import PartitionSpec as P

HD = 64
BLOCK = 64


eps = 1e-06


def layer_norm(values, gain, shift):
    row_mean = jnp.mean(values, axis=-1, keepdims=True)
    centred = values - row_mean
    spread = jnp.mean(centred * centred, axis=-1, keepdims=True)
    return centred * lax.rsqrt(spread + eps) * gain + shift


def gelu_tanh(values):
    return jax.nn.gelu(values, approximate=True)


def contract(form, left, right):
    return jnp.einsum(form, left, right, preferred_element_type=jnp.float32)


def block_table(blocks, lengths_row, offsets):
    seq_ends = jnp.cumsum(lengths_row)
    starts = seq_ends - lengths_row
    inside = ((blocks[:, None] >= starts[None, :]) & (blocks[:, None] < seq_ends[None, :])).astype(
        jnp.int32
    )
    seq_first = jnp.sum(inside * starts[None, :], axis=1)
    seq_count = jnp.sum(inside * lengths_row[None, :], axis=1)
    position = blocks - seq_first
    has_before = position > 0
    has_behind = position < seq_count - 1
    before = jnp.where(has_before, blocks - 1, blocks)
    behind = jnp.where(has_behind, blocks + 1, blocks)
    fixed_ids = jnp.stack([before, blocks, behind, seq_first, seq_first + 1], axis=-1)
    random_ids = seq_first[:, None, None] + offsets % seq_count[:, None, None]
    head_count = offsets.shape[1]
    key_table = jnp.concatenate(
        [jnp.broadcast_to(fixed_ids[:, None, :], (blocks.shape[0], head_count, 5)), random_ids],
        axis=-1,
    )
    always = jnp.ones_like(has_before)
    usable = jnp.stack(
        [has_before, always, has_behind, always, always] + [always] * offsets.shape[2], axis=-1
    )
    return (key_table, usable)


def scores_of(query, key_sel, usable, scale):
    raw = contract("bqhd,bhkcd->bhqkc", query, key_sel)
    return jnp.where(usable[:, None, None, :, None], raw * scale, -1e30)


def per_device(
    inputs,
    qkv_weight,
    out_weight,
    up_weight,
    down_weight,
    norm_gains,
    norm_biases,
    lengths,
    random_blocks,
    out_grad,
):
    w_qkv, w_out, w_up, w_down, gains_low, biases_low = (
        lax.all_gather(qkv_weight, "dp", axis=1, tiled=True),
        lax.all_gather(out_weight, "dp", axis=1, tiled=True),
        lax.all_gather(up_weight, "dp", axis=0, tiled=True),
        lax.all_gather(down_weight, "dp", axis=1, tiled=True),
        lax.all_gather(norm_gains, "dp", axis=1, tiled=True),
        lax.all_gather(norm_biases, "dp", axis=1, tiled=True),
    )
    gains = gains_low.astype(jnp.float32)
    biases = biases_low.astype(jnp.float32)
    rows = inputs.shape[0]
    own_blocks = rows // BLOCK
    local_width = w_qkv.shape[2]
    local_heads = local_width // HD
    scale = 1.0 / math.sqrt(HD)
    x_float = inputs.astype(jnp.float32)
    projected = contract("td,kde->kte", inputs, w_qkv)
    q_low = projected[0].astype(jnp.bfloat16)
    k_low = projected[1].astype(jnp.bfloat16)
    v_low = projected[2].astype(jnp.bfloat16)
    key_all, value_all = (
        lax.all_gather(k_low, "ctx", axis=0, tiled=True),
        lax.all_gather(v_low, "ctx", axis=0, tiled=True),
    )
    group_blocks = key_all.shape[0] // BLOCK
    first_block = lax.axis_index("ctx") * own_blocks
    blocks = first_block + jnp.arange(own_blocks, dtype=jnp.int32)
    key_table, usable = block_table(blocks, lengths[0], random_blocks)
    head_pick = jnp.arange(local_heads, dtype=jnp.int32)[None, :, None]
    key_blocks = key_all.reshape(group_blocks, BLOCK, local_heads, HD)
    value_blocks = value_all.reshape(group_blocks, BLOCK, local_heads, HD)
    key_sel = key_blocks[key_table, :, head_pick, :]
    value_sel = value_blocks[key_table, :, head_pick, :]
    query = q_low.reshape(own_blocks, BLOCK, local_heads, HD)
    scores = scores_of(query, key_sel, usable, scale)
    top = jnp.max(scores, axis=(3, 4), keepdims=True)
    log_total = top + jnp.log(jnp.sum(jnp.exp(scores - top), axis=(3, 4), keepdims=True))
    probs = jnp.exp(scores - log_total)
    probs_low = probs.astype(jnp.bfloat16)
    attended = (
        contract("bhqkc,bhkcd->bqhd", probs_low, value_sel)
        .reshape(rows, local_width)
        .astype(jnp.bfloat16)
    )
    attn_sum = lax.psum(
        jnp.dot(attended, w_out, preferred_element_type=jnp.float32).astype(jnp.bfloat16), "tp"
    ).astype(jnp.float32)
    first_sum = x_float + attn_sum
    normed, norm_pull = jax.vjp(layer_norm, first_sum, gains[0], biases[0])
    normed_low = normed.astype(jnp.bfloat16)
    hidden = jnp.dot(normed_low, w_up, preferred_element_type=jnp.float32)
    activated, gelu_pull = jax.vjp(gelu_tanh, hidden)
    act_low = activated.astype(jnp.bfloat16)
    mlp_sum = lax.psum(
        jnp.dot(act_low, w_down, preferred_element_type=jnp.float32).astype(jnp.bfloat16), "tp"
    ).astype(jnp.float32)
    second_sum = normed + mlp_sum
    result, final_pull = jax.vjp(layer_norm, second_sum, gains[1], biases[1])
    d_second, d_gain_two, d_bias_two = final_pull(out_grad.astype(jnp.float32))
    d_mlp = d_second.astype(jnp.bfloat16)
    grad_down = contract("tf,td->fd", act_low, d_mlp)
    d_act = contract("td,fd->tf", d_mlp, w_down)
    d_hidden = gelu_pull(d_act)[0].astype(jnp.bfloat16)
    grad_up = contract("td,tf->df", normed_low, d_hidden)
    d_normed = d_second + lax.psum(
        contract("tf,df->td", d_hidden, w_up).astype(jnp.bfloat16), "tp"
    ).astype(jnp.float32)
    d_first, d_gain_one, d_bias_one = norm_pull(d_normed)
    d_attn = d_first.astype(jnp.bfloat16)
    grad_proj = contract("te,td->ed", attended, d_attn)
    d_attended = (
        contract("td,ed->te", d_attn, w_out)
        .astype(jnp.bfloat16)
        .reshape(own_blocks, BLOCK, local_heads, HD)
    )
    scores = scores_of(query, key_sel, usable, scale)
    probs = jnp.exp(scores - log_total)
    probs_low = probs.astype(jnp.bfloat16)
    d_probs = contract("bqhd,bhkcd->bhqkc", d_attended, value_sel)
    d_scores = probs * (d_probs - jnp.sum(probs * d_probs, axis=(3, 4), keepdims=True))
    d_raw = (d_scores * scale).astype(jnp.bfloat16)
    d_query = (
        contract("bhqkc,bhkcd->bqhd", d_raw, key_sel)
        .reshape(rows, local_width)
        .astype(jnp.bfloat16)
    )
    d_key_sel = contract("bhqkc,bqhd->bhkcd", d_raw, query)
    d_value_sel = contract("bhqkc,bqhd->bhkcd", probs_low, d_attended)
    empty = jnp.zeros((group_blocks, BLOCK, local_heads, HD), jnp.float32)
    d_key_all = (
        empty.at[key_table, :, head_pick, :]
        .add(d_key_sel)
        .reshape(group_blocks * BLOCK, local_width)
    )
    d_value_all = (
        empty.at[key_table, :, head_pick, :]
        .add(d_value_sel)
        .reshape(group_blocks * BLOCK, local_width)
    )
    d_key, d_value = (
        lax.psum_scatter(
            d_key_all.astype(jnp.bfloat16), "ctx", scatter_dimension=0, tiled=True
        ).astype(jnp.float32),
        lax.psum_scatter(
            d_value_all.astype(jnp.bfloat16), "ctx", scatter_dimension=0, tiled=True
        ).astype(jnp.float32),
    )
    d_projected = jnp.stack([d_query, d_key.astype(jnp.bfloat16), d_value.astype(jnp.bfloat16)])
    grad_qkv = contract("td,kte->kde", inputs, d_projected)
    d_inputs = d_first + lax.psum(
        contract("kte,kde->td", d_projected, w_qkv).astype(jnp.bfloat16), "tp"
    ).astype(jnp.float32)
    grad_gains = jnp.stack([d_gain_one, d_gain_two])
    grad_biases = jnp.stack([d_bias_one, d_bias_two])
    shared = (
        lax.psum_scatter(
            grad_qkv.astype(jnp.bfloat16), "dp", scatter_dimension=1, tiled=True
        ).astype(jnp.float32),
        lax.psum_scatter(
            grad_proj.astype(jnp.bfloat16), "dp", scatter_dimension=1, tiled=True
        ).astype(jnp.float32),
        lax.psum_scatter(
            grad_up.astype(jnp.bfloat16), "dp", scatter_dimension=0, tiled=True
        ).astype(jnp.float32),
        lax.psum_scatter(
            grad_down.astype(jnp.bfloat16), "dp", scatter_dimension=1, tiled=True
        ).astype(jnp.float32),
        lax.psum_scatter(
            grad_gains.astype(jnp.bfloat16), "dp", scatter_dimension=1, tiled=True
        ).astype(jnp.float32),
        lax.psum_scatter(
            grad_biases.astype(jnp.bfloat16), "dp", scatter_dimension=1, tiled=True
        ).astype(jnp.float32),
    )
    totals = (
        lax.psum(shared[0].astype(jnp.bfloat16), "ctx").astype(jnp.float32),
        lax.psum(shared[1].astype(jnp.bfloat16), "ctx").astype(jnp.float32),
        lax.psum(shared[2].astype(jnp.bfloat16), "ctx").astype(jnp.float32),
        lax.psum(shared[3].astype(jnp.bfloat16), "ctx").astype(jnp.float32),
        lax.psum(shared[4].astype(jnp.bfloat16), "ctx").astype(jnp.float32),
        lax.psum(shared[5].astype(jnp.bfloat16), "ctx").astype(jnp.float32),
    )
    return (
        result.astype(jnp.bfloat16),
        d_inputs.astype(jnp.bfloat16),
        totals[0],
        totals[1],
        totals[2],
        totals[3],
        totals[4],
        totals[5],
    )


def mul(left, right, left_dim, right_dim):
    dims = (((left_dim,), (right_dim,)), ((), ()))
    return lax.dot_general(left, right, dims, preferred_element_type=jnp.float32)


def call(body, outs, *args, scratch=(), copies=0, spec=None, room=32, flops=0):
    spec = spec or pl.BlockSpec(memory_space=pltpu.VMEM)
    specs = [spec] * len(args)
    shapes = [jax.ShapeDtypeStruct(shape, dtype) for shape, dtype in outs]
    return pl.pallas_call(
        body,
        out_shape=shapes,
        in_specs=specs,
        out_specs=[pl.BlockSpec(memory_space=pltpu.VMEM)] * len(shapes),
        scratch_shapes=[pltpu.VMEM(shape, dtype) for shape, dtype in scratch]
        + ([pltpu.SemaphoreType.DMA((copies,))] if copies else []),
        compiler_params=pltpu.CompilerParams(vmem_limit_bytes=room << 20),
        cost_estimate=pl.CostEstimate(flops=flops, bytes_accessed=0, transcendentals=0),
    )(*args)


def head_masks(width):
    lane = lax.broadcasted_iota(jnp.int32, (1, width), 1)
    return [(lane >= h * HD) & (lane < (h + 1) * HD) for h in range(width // HD)]


def only(values, mask):
    return jnp.where(mask, values, jnp.zeros_like(values))


def biased(raw, bias, scale):
    blocks = bias.shape[0]
    size = raw.shape[0] // blocks
    return jnp.concatenate(
        [raw[j * size : (j + 1) * size] * scale + bias[j : j + 1] for j in range(blocks)], axis=0
    )


DIRECT = (0, 2, 4, 6, 1, 3, 5, 7)
OUT_WAYS = (0, 1, 4, 5, 2, 3, 6, 7)
UP_WAYS = (0, 4, 2, 6, 1, 5, 3, 7)
DOWN_WAYS = (0, 4, 1, 5, 2, 6, 3, 7)


def place(pieces, all_ref, ways, window=0):
    width = all_ref.shape[1]
    parts = []
    for piece in pieces:
        parts += [piece] if len(piece.shape) == 2 else [piece.at[i] for i in range(piece.shape[0])]
    for part, bits in zip(parts, ways, strict=True):
        shard = part.shape[0]
        owner = lax.axis_index("dp") ^ bits
        start = window if part.shape[1] > width else 0
        all_ref[pl.ds(pl.multiple_of(owner * shard, 32), shard), :] = part[:, start : start + width]


def fetch(pairs, sems):
    copies = [pltpu.make_async_copy(src, dst, sems.at[i]) for i, (src, dst) in enumerate(pairs)]
    for copy in copies:
        copy.start()
    for copy in copies:
        copy.wait()


def own_half(src, dst):
    n = dst.shape[1]
    dst[...] = jnp.where(lax.axis_index("ctx") == 0, src[:, :n], src[:, n:])


def pack_first_body(qkv_hbm, gain_hbm, bias_hbm, out_hbm, w_ref, pack_ref, qkv, gain, bias, out, sems):
    fetch(((qkv_hbm, qkv), (gain_hbm, gain), (bias_hbm, bias), (out_hbm, out)), sems)
    c = lax.axis_index("ctx")
    n = qkv.shape[2] // 2
    for i in range(3):
        w_ref[:, i * n : (i + 1) * n] = jnp.where(c == 0, qkv[i, :, :n], qkv[i, :, n:])
    m = out.shape[1] // 2
    extra = pack_ref.shape[1] - 3 * n - m
    row = lax.broadcasted_iota(jnp.int32, (2, extra), 0)
    lane = lax.broadcasted_iota(jnp.int32, (2, extra), 1)
    cols = mul(gain[...], (row == lane).astype(jnp.bfloat16), 0, 0)
    cols = cols + mul(bias[...], (row + 2 == lane).astype(jnp.bfloat16), 0, 0)
    pack_ref[:, 0:m] = jnp.where(c == 0, out[:, :m], out[:, m:])
    pack_ref[:, m : m + extra] = cols.astype(jnp.bfloat16)
    pack_ref[:, m + extra :] = w_ref[...]


def pack_second_body(up_hbm, down_hbm, up_ref, down_ref, up, down, sems):
    fetch(((up_hbm, up), (down_hbm, down)), sems)
    own_half(up, up_ref)
    own_half(down, down_ref)


def attend_body(
    own_ref, far_ref, w0, w1, w2, w3, w4, w5, bias_ref,
    o_ref, qkv_ref, lse_ref, x_ref, w_ref, p_scr, v_scr,
):
    width = o_ref.shape[1]
    rows = x_ref.shape[0]
    part = far_ref.shape[0] // 2
    c = lax.axis_index("ctx")
    for t in range(2):
        x_ref[pl.ds((2 * t + c) * part, part), :] = own_ref[t * part : (t + 1) * part, :]
        x_ref[pl.ds((2 * t + 1 - c) * part, part), :] = far_ref[t * part : (t + 1) * part, :]
    place((w0, w1, w2, w3, w4, w5), w_ref, DIRECT, w4.shape[1] - w_ref.shape[1])
    scale = 1.0 / math.sqrt(HD)
    w = w_ref[...]
    qkv = mul(x_ref[...], w, 1, 0).astype(jnp.bfloat16)
    qkv_ref[...] = qkv
    q, k, v = [qkv[:, i * width : (i + 1) * width] for i in range(3)]
    lse_ref[...] = jnp.zeros_like(lse_ref)
    blocks = bias_ref.shape[0] // (width // HD)
    for h, mask in enumerate(head_masks(width)):
        s = biased(mul(k, only(q, mask), 1, 1), bias_ref[h * blocks : (h + 1) * blocks, :], scale)
        top = jnp.max(s, axis=0, keepdims=True)
        e = jnp.exp(s - top)
        total = jnp.sum(e, axis=0, keepdims=True)
        lse_ref[h : h + 1, :] = top + jnp.log(total)
        p_scr[h * rows : (h + 1) * rows, :] = (e * (1.0 / total)).astype(jnp.bfloat16)
        v_scr[h * rows : (h + 1) * rows, :] = only(v, mask)
    o_ref[...] = mul(p_scr[...], v_scr[...], 0, 0).astype(jnp.bfloat16)


def split_rows(value_of, mine_ref, theirs_ref):
    half = mine_ref.shape[0]
    t = lax.axis_index("tp")
    theirs_ref[...] = value_of(pl.ds((1 - t) * half, half)).astype(theirs_ref.dtype)
    mine_ref[...] = value_of(pl.ds(t * half, half))


def project_body(ways, o_ref, *refs):
    *pieces, mine_ref, theirs_ref, w_ref = refs
    place(pieces, w_ref, ways)
    split_rows(lambda rows: mul(o_ref[rows, :], w_ref[...], 1, 1), mine_ref, theirs_ref)


def project_out_body(ways, o_ref, *refs):
    *pieces, mine_ref, theirs_ref, w_ref, vec_ref, scr = refs
    place(pieces, scr, ways)
    n = w_ref.shape[1]
    w_ref[...] = scr[:, 0:n]
    extra = scr.shape[1] - n
    unit = (
        lax.broadcasted_iota(jnp.int32, (8, extra), 0) == lax.broadcasted_iota(jnp.int32, (8, extra), 1)
    ).astype(jnp.bfloat16)
    vec_ref[...] = mul(unit, scr[:, n:], 1, 1)
    split_rows(lambda rows: mul(o_ref[rows, :], w_ref[...], 1, 1), mine_ref, theirs_ref)


def add_tp_body(mine_ref, both_ref, sum_ref):
    sum_ref[...] = (mine_ref[...] + both_ref[1 - lax.axis_index("tp")].astype(jnp.float32)).astype(jnp.bfloat16)


def norm_parts(z):
    centred = z - jnp.mean(z, axis=1, keepdims=True)
    r = lax.rsqrt(jnp.mean(centred * centred, axis=1, keepdims=True) + eps)
    return centred * r, r


def norm_back(e2, n, r):
    return r * (e2 - jnp.mean(e2, axis=1, keepdims=True) - n * jnp.mean(e2 * n, axis=1, keepdims=True))


def norm_one_body(x_ref, a_ref, far_ref, vec_ref, n_ref, r_ref, low_ref):
    half = n_ref.shape[0]
    z = x_ref[pl.ds(lax.axis_index("tp") * half, half), :].astype(jnp.float32)
    z = z + (a_ref[...].astype(jnp.float32) + far_ref[...].astype(jnp.float32))
    n, r = norm_parts(z)
    n_ref[...] = n
    r_ref[...] = jnp.broadcast_to(r, r_ref.shape)
    low_ref[...] = (n * vec_ref[0:1, :] + vec_ref[2:3, :]).astype(jnp.bfloat16)


def ffn_body(y_ref, w0, w1, w2, w3, u_ref, slope_ref, up_ref):
    place((w0, w1, w2, w3), up_ref, UP_WAYS)
    hid = mul(y_ref[...], up_ref[...], 1, 0)
    root = math.sqrt(2.0 / math.pi)
    square = hid * hid
    bent = jnp.tanh(root * (hid + 0.044715 * (square * hid)))
    u_ref[...] = (0.5 * hid * (1.0 + bent)).astype(jnp.bfloat16)
    slope = 0.5 * (1.0 + bent) + 0.5 * hid * (1.0 - bent * bent) * (root * (1.0 + 3 * 0.044715 * square))
    slope_ref[...] = slope.astype(jnp.bfloat16)


def norm_two_body(n1_ref, m_ref, far_ref, e_ref, e_far_ref, vec_ref, out_ref, dz_ref, low_ref, grad_ref, e_scr, out_scr):
    part = out_ref.shape[0]
    c, t = lax.axis_index("ctx"), lax.axis_index("tp")
    e_scr[pl.ds(c * part, part), :] = e_ref[pl.ds(t * part, part), :].astype(jnp.float32)
    e_scr[pl.ds((1 - c) * part, part), :] = e_far_ref[pl.ds(t * part, part), :].astype(jnp.float32)
    y1 = n1_ref[...] * vec_ref[0:1, :] + vec_ref[2:3, :]
    z = y1 + (m_ref[...].astype(jnp.float32) + far_ref[...].astype(jnp.float32))
    n, r = norm_parts(z)
    out_scr[...] = n * vec_ref[1:2, :] + vec_ref[3:4, :]
    out_ref[...] = out_scr[pl.ds(c * part, part), :].astype(jnp.bfloat16)
    e = e_scr[...]
    dz = norm_back(e * vec_ref[1:2, :], n, r)
    dz_ref[...] = dz
    low_ref[...] = dz.astype(jnp.bfloat16)
    grad_ref[...] = jnp.zeros_like(grad_ref)
    grad_ref[1:2, :] = jnp.sum(e * n, axis=0, keepdims=True)
    grad_ref[3:4, :] = jnp.sum(e, axis=0, keepdims=True)


def ffn_back_body(dm_ref, slope_ref, down_ref, up_ref, dhid_ref, mine_ref, theirs_ref):
    du = mul(dm_ref[...], down_ref[...], 1, 0)
    dhid_ref[...] = (du * slope_ref[...].astype(jnp.float32)).astype(jnp.bfloat16)
    split_rows(lambda rows: mul(dhid_ref[rows, :], up_ref[...], 1, 1), mine_ref, theirs_ref)


def deal(own_ref, away_ref, scr, order, start=0):
    one, two, three = order
    shard, width = own_ref.shape[1:]
    dp = lax.axis_index("dp")
    for i, bits in enumerate((0, three, two, two ^ three)):
        for ref, owner in ((own_ref, dp ^ bits), (away_ref, dp ^ bits ^ one)):
            part = scr[pl.ds(pl.multiple_of(owner * shard, 32), shard), start : start + width]
            ref[i] = part.astype(ref.dtype)


def grad_body(order, left_ref, right_ref, own_ref, away_ref, scr):
    scr[...] = mul(left_ref[...], right_ref[...], 0, 0)
    deal(own_ref, away_ref, scr, order)


def deal_two(own_ref, away_ref, own2_ref, away2_ref, scr):
    deal(own_ref, away_ref, scr, (1, 2, 4))
    deal(own2_ref, away2_ref, scr, (2, 1, 4), own_ref.shape[2])


def fold_pair(own_ref, got_ref, keep_ref, send_ref):
    half = keep_ref.shape[0]
    keep_ref[...] = own_ref[0:half] + got_ref[0:half].astype(jnp.float32)
    send_ref[...] = (own_ref[half:] + got_ref[half:].astype(jnp.float32)).astype(jnp.bfloat16)


def fold_body(own_ref, got_ref, keep_ref, send_ref):
    fold_pair(own_ref, got_ref, keep_ref, send_ref)


def fold_two_body(own_ref, got_ref, own2_ref, got2_ref, keep_ref, send_ref, keep2_ref, send2_ref):
    fold_pair(own_ref, got_ref, keep_ref, send_ref)
    fold_pair(own2_ref, got2_ref, keep2_ref, send2_ref)


def fold_join_body(own_ref, got_ref, own2_ref, got2_ref, keep_ref, send_ref):
    width = own_ref.shape[2]
    for own, got, lanes in ((own_ref, got_ref, slice(0, width)), (own2_ref, got2_ref, slice(width, keep_ref.shape[2]))):
        keep_ref[0, :, lanes] = own[0] + got[0].astype(jnp.float32)
        send_ref[0, :, lanes] = (own[1] + got[1].astype(jnp.float32)).astype(jnp.bfloat16)


def fold_last_body(own_ref, got_ref, sum_ref):
    sum_ref[...] = (own_ref[0] + got_ref[0].astype(jnp.float32)).astype(jnp.bfloat16)


def norm_one_back_body(dz2_ref, d_ref, far_ref, n_ref, r_ref, vec_ref, grad2_ref, dz_ref, low_ref):
    dy = dz2_ref[...] + (d_ref[...].astype(jnp.float32) + far_ref[...].astype(jnp.float32))
    n = n_ref[...]
    dz = norm_back(dy * vec_ref[0:1, :], n, r_ref[:, 0:1])
    dz_ref[...] = dz
    half = dz.shape[0]
    low_ref[0:half, :] = dz.astype(jnp.bfloat16)
    sums = [
        jnp.sum(dy * n, axis=0, keepdims=True), grad2_ref[1:2, :],
        jnp.sum(dy, axis=0, keepdims=True), grad2_ref[3:4, :], jnp.zeros((12, dz.shape[1]), jnp.float32),
    ]
    low_ref[half : half + 16, :] = jnp.concatenate(sums, axis=0).astype(jnp.bfloat16)


def attend_back_body(
    da_ref, w_out_ref, qkv_ref, o_ref, lse_ref, bias_ref, x_ref,
    own_ref, away_ref, own2_ref, away2_ref, all_scr,
    p_scr, dr_scr, q_scr, do_scr, grad_scr,
):
    width = o_ref.shape[1]
    rows = x_ref.shape[0]
    scale = 1.0 / math.sqrt(HD)
    half = rows // 2
    da = jnp.concatenate([da_ref[0, 0:half, :], da_ref[1, 0:half, :]], axis=0)
    do = mul(da, w_out_ref[...], 1, 0).astype(jnp.bfloat16)
    q, k, v = [qkv_ref[:, i * width : (i + 1) * width] for i in range(3)]
    blocks = bias_ref.shape[0] // (width // HD)
    dq = jnp.zeros((rows, width), jnp.float32)
    for h, mask in enumerate(head_masks(width)):
        q_h, do_h = only(q, mask), only(do, mask)
        s = biased(mul(k, q_h, 1, 1), bias_ref[h * blocks : (h + 1) * blocks, :], scale)
        p = jnp.exp(s - lse_ref[h : h + 1, :])
        dp = mul(v, do_h, 1, 1)
        pd = p * dp
        ds = pd - p * jnp.sum(pd, axis=0, keepdims=True)
        dr = (ds * scale).astype(jnp.bfloat16)
        p_scr[:, h * rows : (h + 1) * rows] = p.astype(jnp.bfloat16)
        dr_scr[:, h * rows : (h + 1) * rows] = dr
        q_scr[h * rows : (h + 1) * rows, :] = q_h
        do_scr[h * rows : (h + 1) * rows, :] = do_h
        dq = dq + mul(dr, only(k, mask), 0, 0)
    all_scr[:, 0:width] = dq.astype(jnp.bfloat16)
    all_scr[:, width : 2 * width] = mul(dr_scr[...], q_scr[...], 1, 0).astype(jnp.bfloat16)
    all_scr[:, 2 * width : 3 * width] = mul(p_scr[...], do_scr[...], 1, 0).astype(jnp.bfloat16)
    vec = sum(da_ref[i, half : half + 16, :].astype(jnp.float32) for i in range(2)).astype(jnp.bfloat16)
    extra = grad_scr.shape[1] - 4 * width
    unit = (
        lax.broadcasted_iota(jnp.int32, (16, extra), 0) == lax.broadcasted_iota(jnp.int32, (16, extra), 1)
    ).astype(jnp.bfloat16)
    grad_scr[...] = jnp.concatenate(
        [mul(x_ref[...], all_scr[...], 0, 0), mul(vec, unit, 0, 0), mul(da, o_ref[...], 0, 0)], axis=1
    )
    deal_two(own_ref, away_ref, own2_ref, away2_ref, grad_scr)


def input_body(grad_ref, w_ref, mine_ref, theirs_ref):
    split_rows(lambda rows: mul(grad_ref[rows, :], w_ref[...], 1, 1), mine_ref, theirs_ref)


def fold_input_body(mine_ref, both_ref, dz_ref, keep_ref, send_ref):
    part = keep_ref.shape[0]
    c, far = lax.axis_index("ctx"), 1 - lax.axis_index("tp")
    own, other = pl.ds(c * part, part), pl.ds((1 - c) * part, part)
    send_ref[...] = (mine_ref[other, :] + both_ref[far, other, :].astype(jnp.float32)).astype(jnp.bfloat16)
    keep_ref[...] = dz_ref[own, :] + (mine_ref[own, :] + both_ref[far, own, :].astype(jnp.float32))


def last_input_body(keep_ref, got_ref, out_ref):
    out_ref[...] = (keep_ref[...] + got_ref[...].astype(jnp.float32)).astype(jnp.bfloat16)


def copy_body(in_ref, out_ref):
    out_ref[...] = in_ref[...]


def finish_body(near_ref, far_ref, qkv_ref, out_ref, gain_ref, bias_ref):
    c = lax.axis_index("ctx")
    n = qkv_ref.shape[2] // 2
    m = out_ref.shape[1] // 2
    near, far = near_ref[...].astype(jnp.float32), far_ref[...].astype(jnp.float32)
    low, high = jnp.where(c == 0, near, far), jnp.where(c == 0, far, near)
    for i in range(3):
        qkv_ref[i] = jnp.concatenate([low[:, i * n : (i + 1) * n], high[:, i * n : (i + 1) * n]], axis=1)
    out_ref[...] = jnp.concatenate([low[:, low.shape[1] - m :], high[:, high.shape[1] - m :]], axis=1)
    vec = near_ref[:, 3 * n : near_ref.shape[1] - m]
    row = lax.broadcasted_iota(jnp.int32, (2, vec.shape[1]), 0)
    lane = lax.broadcasted_iota(jnp.int32, (2, vec.shape[1]), 1)
    gain_ref[...] = mul((row == lane).astype(jnp.bfloat16), vec, 1, 1)
    bias_ref[...] = mul((row + 2 == lane).astype(jnp.bfloat16), vec, 1, 1)


def rows_device(
    dims,
    inputs,
    qkv_weight,
    out_weight,
    up_weight,
    down_weight,
    norm_gains,
    norm_biases,
    lengths,
    random_blocks,
    out_grad,
):
    n_dp = dims["dp"]
    n_out = n_dp // 2
    c = lax.axis_index("ctx")
    f32, bf16 = jnp.float32, jnp.bfloat16
    pair = [(0, 1), (1, 0)]

    def both_tp(v, tiled=False):
        return lax.all_gather(v, "tp", axis=0, tiled=tiled)

    def swap_ctx(v):
        return lax.ppermute(v, "ctx", pair)

    def swap_dp(v, bits):
        return lax.ppermute(v, "dp", [(i, i ^ bits) for i in range(n_dp)])

    def after(v, *others):
        return lax.optimization_barrier((v,) + others)[0]

    def all_after(vs, *others):
        return list(lax.optimization_barrier(tuple(vs) + others)[: len(vs)])

    rows, width = inputs.shape
    part = rows // 2
    shard = qkv_weight.shape[1]
    cols = qkv_weight.shape[2] // 2
    units = up_weight.shape[1] // 2
    heads = cols // HD
    own_blocks = rows // BLOCK
    per = own_blocks // 2
    total_rows = 2 * rows
    extra = 4 + (-(4 * cols + 4)) % 64

    half = ((part, width), bf16)
    hbm = pl.BlockSpec(memory_space=pltpu.HBM)

    def packed(body, widths, *given):
        return call(
            body, [((shard, n), bf16) for n in widths], *given,
            scratch=[(w.shape, bf16) for w in given], copies=len(given), spec=hbm, room=60,
        )

    x_far = swap_ctx(inputs)
    w1, pack_one = packed(
        pack_first_body, (3 * cols, 4 * cols + extra), qkv_weight, norm_gains, norm_biases, out_weight.T
    )
    w1_near = [swap_dp(w1, 2 * k) for k in range(1, n_out)]
    far_one = swap_dp(pack_one, 1)
    w_up, w_down = packed(pack_second_body, (units, units), up_weight, down_weight.T)
    picks_far = swap_ctx(random_blocks)
    w1_near = all_after(w1_near, far_one)
    w1_rest = jnp.stack(w1_near)
    w1_pieces = [w1, *w1_near, far_one, swap_dp(w1_rest, 1)]
    out_pieces = [jnp.stack([pack_one[:, : cols + extra], far_one[:, : cols + extra]])]
    out_pieces[0] = after(out_pieces[0], w1_rest)
    out_pieces.append(swap_dp(out_pieces[0], 4))
    out_pieces.append(swap_dp(jnp.concatenate(out_pieces), 2))
    up_pieces, down_pieces = all_after([w_up[None], w_down[None]], out_pieces[1])
    up_pieces = [up_pieces, swap_dp(up_pieces, 4)]
    down_pieces = [down_pieces, swap_dp(down_pieces, 4)]
    e_far = swap_ctx(after(out_grad, *w1_near))

    picks = jnp.where(c == 0, jnp.stack([random_blocks, picks_far]), jnp.stack([picks_far, random_blocks]))
    picks = lax.dynamic_slice_in_dim(picks.reshape(2 * own_blocks, 2 * heads, 3), c * heads, heads, 1)
    blocks = jnp.arange(2 * own_blocks, dtype=jnp.int32)
    table, usable = block_table(blocks, lengths[0], picks)
    named = (table[..., None] == blocks) & usable[:, None, :, None]
    counts = jnp.sum(named.astype(f32), axis=2)
    counts = counts.reshape(2, 2, per, heads, 2, 2, per).transpose(3, 5, 4, 6, 1, 0, 2)
    bias = jnp.where(counts > 0, jnp.log(jnp.maximum(counts, 1.0)), -1e30)
    bias = bias.reshape(heads * 2 * own_blocks, 2 * own_blocks, 1)
    bias = jnp.broadcast_to(bias, bias.shape[:2] + (BLOCK,)).reshape(-1, total_rows)

    low = [((rows, width), bf16)]
    wide = [((rows, width), f32)]
    small = [((8, width), f32)]
    o, qkv, lse, x_all, w1_all = call(
        attend_body,
        [
            ((total_rows, cols), bf16), ((total_rows, 3 * cols), bf16), ((8, total_rows), f32),
            ((total_rows, width), bf16), ((width, 3 * cols), bf16),
        ],
        inputs, x_far, *w1_pieces, bias,
        scratch=[((heads * total_rows, total_rows), bf16), ((heads * total_rows, cols), bf16)],
        flops=0,
    )

    def sum_tp(mine, theirs):
        return call(add_tp_body, low, mine, both_tp(theirs))[0]

    mine, theirs, w_out_all, vecs = call(
        functools.partial(project_out_body, OUT_WAYS), wide + low + [((width, cols), bf16)] + small, o, *out_pieces,
        scratch=[((width, cols + extra), bf16)],
    )
    theirs, up_pieces[1], down_pieces[1] = all_after([theirs, up_pieces[1], down_pieces[1]])
    up_pieces.append(swap_dp(jnp.concatenate(up_pieces), 2))
    down_pieces.append(swap_dp(jnp.concatenate(down_pieces), 1))
    a = after(sum_tp(mine, theirs), e_far)
    a_far = swap_ctx(a)
    up_pieces.append(swap_dp(jnp.concatenate(up_pieces), 1))
    down_pieces.append(swap_dp(jnp.concatenate(down_pieces), 2))
    n1, r1, y_low = call(norm_one_body, wide + [((rows, 128), f32)] + low, x_all, a, a_far, vecs)
    flat = [((total_rows, units), bf16)]
    square = [((width, units), bf16)]
    y_all = both_tp(y_low, True)
    u, slope, w_up_all = call(ffn_body, flat * 2 + square, y_all, *up_pieces)
    mine, theirs, w_down_all = call(functools.partial(project_body, DOWN_WAYS), wide + low + square, u, *down_pieces)
    m = sum_tp(mine, theirs)
    m_far = swap_ctx(m)
    out, dz2, dm_low, grad2 = call(
        norm_two_body,
        [((part, width), bf16)] + wide + low + small,
        n1, m, m_far, out_grad, e_far, vecs,
        scratch=wide * 2,
    )

    def pairs(k, *widths):
        return [((k, shard, n), dtype) for n in widths for dtype in (f32, bf16)]

    def cut(n):
        most = n * 2 // 3 // 128 * 128
        return most, n - most

    def fold(own, got):
        return call(fold_body, pairs(own.shape[0] // 2, own.shape[2]), own, got)

    def fold_first(own, away, own2, away2):
        return call(fold_two_body, pairs(2, own.shape[2], own2.shape[2]), own, swap_dp(away, 1), own2, swap_dp(away2, 2))

    def fold_third(keep, send, bits):
        total = call(fold_last_body, [(keep.shape[1:], bf16)], keep, swap_dp(send, bits))[0]
        return total, swap_ctx(total)

    dm_all = both_tp(dm_low, True)
    down_own, down_away = call(
        functools.partial(grad_body, (2, 1, 4)), pairs(n_out, units), dm_all, u, scratch=[((width, units), f32)]
    )
    dm_all = after(dm_all, down_away)
    dhid, mine, theirs = call(
        ffn_back_body, flat + wide + low, dm_all, slope, w_down_all, w_up_all
    )
    d = sum_tp(mine, theirs)
    d_far = swap_ctx(d)
    y_late, dhid = lax.optimization_barrier((y_all, dhid, d))[:2]
    up = call(
        functools.partial(grad_body, (1, 4, 2)), pairs(n_out, units), y_late, dhid, scratch=[((width, units), f32)]
    )
    down_keep, down_send = fold(down_own, swap_dp(down_away, 2))
    output = call(copy_body, low, both_tp(after(out, up[1]), True))[0]
    dz1, da_low = call(
        norm_one_back_body, wide + [((rows + 16, width), bf16)], dz2, d, after(d_far, up[1], down_send, output), n1, r1, vecs, grad2
    )
    last = 4 * cols + extra
    *tail, dqkv = call(
        attend_back_body,
        pairs(n_out, *cut(last)) + [((total_rows, 3 * cols), bf16)],
        after(both_tp(da_low), down_send), w_out_all, qkv, o, lse, bias, x_all,
        flops=2 * 10**10,
        scratch=[
            ((total_rows, heads * total_rows), bf16),
            ((total_rows, heads * total_rows), bf16),
            ((heads * total_rows, cols), bf16),
            ((heads * total_rows, cols), bf16),
            ((width, last), f32),
        ],
    )
    mine, theirs = call(input_body, wide + low, dqkv, w1_all)
    down = fold(after(down_keep, theirs), swap_dp(down_send, 1))
    theirs = after(theirs, down[1])
    keep, send = call(fold_input_body, [((part, width), f32), half], mine, both_tp(theirs), dz1)
    up = fold(after(up[0], mine), swap_dp(up[1], 1))
    keep1, send1, keep2, send2 = fold_first(*all_after(tail[:1], send), *tail[1:])
    got1, got2 = swap_dp(send1, 2), swap_dp(send2, 1)
    dx_far = swap_ctx(send)
    up = fold(after(up[0], keep1), swap_dp(up[1], 4))
    grad_down, down_far = fold_third(*all_after(down[:1], keep1), down[1], 4)
    keep1 = after(keep1, dx_far, up[1], grad_down)
    tail = call(fold_join_body, pairs(1, last), keep1, got1, keep2, got2)
    grad_1, far_1 = fold_third(*tail, 4)
    grad_up, up_far = fold_third(*all_after(up[:1], grad_1), up[1], 2)
    dx = call(last_input_body, [half], keep, after(dx_far, grad_1))[0]
    input_grad = call(copy_body, low, both_tp(dx, True))[0]
    grad_1 = after(grad_1, input_grad)

    def both_ctx(g, far):
        return jnp.where(c == 0, jnp.concatenate([g, far], 1), jnp.concatenate([far, g], 1)).astype(f32)

    grad_qkv, grad_out, gains, biases = call(
        finish_body,
        [((3, shard, 2 * cols), f32), ((shard, 2 * cols), f32), ((2, shard), f32), ((2, shard), f32)],
        grad_1, far_1,
    )
    return (
        output, input_grad, grad_qkv, grad_out.T, both_ctx(grad_up, up_far), both_ctx(grad_down, down_far).T, gains, biases
    )


def solution(mesh):
    dims = dict(mesh.shape)
    fast = dims["ctx"] == 2 and dims["tp"] == 2 and dims["dp"] == 8
    step = functools.partial(rows_device, dims) if fast else per_device
    return jax.shard_map(
        step,
        mesh=mesh,
        in_specs=(
            P(("dp", "ctx"), None),
            P(None, "dp", "tp"),
            P("tp", "dp"),
            P("dp", "tp"),
            P("tp", "dp"),
            P(None, "dp"),
            P(None, "dp"),
            P("dp", None),
            P(("dp", "ctx"), "tp", None),
            P(("dp", "ctx"), None),
        ),
        out_specs=(
            P(("dp", "ctx"), None),
            P(("dp", "ctx"), None),
            P(None, "dp", "tp"),
            P("tp", "dp"),
            P("dp", "tp"),
            P("tp", "dp"),
            P(None, "dp"),
            P(None, "dp"),
        ),
        check_vma=False,
    )
```

```python
import functools
import math

import jax
import jax.numpy as jnp
from jax import lax
from jax.experimental import pallas as pl
from jax.experimental.pallas import tpu as pltpu
from jax.sharding import PartitionSpec as P

HD = 64
BLOCK = 64


eps = 1e-06


def layer_norm(values, gain, shift):
    row_mean = jnp.mean(values, axis=-1, keepdims=True)
    centred = values - row_mean
    spread = jnp.mean(centred * centred, axis=-1, keepdims=True)
    return centred * lax.rsqrt(spread + eps) * gain + shift


def gelu_tanh(values):
    return jax.nn.gelu(values, approximate=True)


def contract(form, left, right):
    return jnp.einsum(form, left, right, preferred_element_type=jnp.float32)


def block_table(blocks, lengths_row, offsets):
    seq_ends = jnp.cumsum(lengths_row)
    starts = seq_ends - lengths_row
    inside = ((blocks[:, None] >= starts[None, :]) & (blocks[:, None] < seq_ends[None, :])).astype(
        jnp.int32
    )
    seq_first = jnp.sum(inside * starts[None, :], axis=1)
    seq_count = jnp.sum(inside * lengths_row[None, :], axis=1)
    position = blocks - seq_first
    has_before = position > 0
    has_behind = position < seq_count - 1
    before = jnp.where(has_before, blocks - 1, blocks)
    behind = jnp.where(has_behind, blocks + 1, blocks)
    fixed_ids = jnp.stack([before, blocks, behind, seq_first, seq_first + 1], axis=-1)
    random_ids = seq_first[:, None, None] + offsets % seq_count[:, None, None]
    head_count = offsets.shape[1]
    key_table = jnp.concatenate(
        [jnp.broadcast_to(fixed_ids[:, None, :], (blocks.shape[0], head_count, 5)), random_ids],
        axis=-1,
    )
    always = jnp.ones_like(has_before)
    usable = jnp.stack(
        [has_before, always, has_behind, always, always] + [always] * offsets.shape[2], axis=-1
    )
    return (key_table, usable)


def scores_of(query, key_sel, usable, scale):
    raw = contract("bqhd,bhkcd->bhqkc", query, key_sel)
    return jnp.where(usable[:, None, None, :, None], raw * scale, -1e30)


def per_device(
    inputs,
    qkv_weight,
    out_weight,
    up_weight,
    down_weight,
    norm_gains,
    norm_biases,
    lengths,
    random_blocks,
    out_grad,
):
    w_qkv, w_out, w_up, w_down, gains_low, biases_low = (
        lax.all_gather(qkv_weight, "dp", axis=1, tiled=True),
        lax.all_gather(out_weight, "dp", axis=1, tiled=True),
        lax.all_gather(up_weight, "dp", axis=0, tiled=True),
        lax.all_gather(down_weight, "dp", axis=1, tiled=True),
        lax.all_gather(norm_gains, "dp", axis=1, tiled=True),
        lax.all_gather(norm_biases, "dp", axis=1, tiled=True),
    )
    gains = gains_low.astype(jnp.float32)
    biases = biases_low.astype(jnp.float32)
    rows = inputs.shape[0]
    own_blocks = rows // BLOCK
    local_width = w_qkv.shape[2]
    local_heads = local_width // HD
    scale = 1.0 / math.sqrt(HD)
    x_float = inputs.astype(jnp.float32)
    projected = contract("td,kde->kte", inputs, w_qkv)
    q_low = projected[0].astype(jnp.bfloat16)
    k_low = projected[1].astype(jnp.bfloat16)
    v_low = projected[2].astype(jnp.bfloat16)
    key_all, value_all = (
        lax.all_gather(k_low, "ctx", axis=0, tiled=True),
        lax.all_gather(v_low, "ctx", axis=0, tiled=True),
    )
    group_blocks = key_all.shape[0] // BLOCK
    first_block = lax.axis_index("ctx") * own_blocks
    blocks = first_block + jnp.arange(own_blocks, dtype=jnp.int32)
    key_table, usable = block_table(blocks, lengths[0], random_blocks)
    head_pick = jnp.arange(local_heads, dtype=jnp.int32)[None, :, None]
    key_blocks = key_all.reshape(group_blocks, BLOCK, local_heads, HD)
    value_blocks = value_all.reshape(group_blocks, BLOCK, local_heads, HD)
    key_sel = key_blocks[key_table, :, head_pick, :]
    value_sel = value_blocks[key_table, :, head_pick, :]
    query = q_low.reshape(own_blocks, BLOCK, local_heads, HD)
    scores = scores_of(query, key_sel, usable, scale)
    top = jnp.max(scores, axis=(3, 4), keepdims=True)
    log_total = top + jnp.log(jnp.sum(jnp.exp(scores - top), axis=(3, 4), keepdims=True))
    probs = jnp.exp(scores - log_total)
    probs_low = probs.astype(jnp.bfloat16)
    attended = (
        contract("bhqkc,bhkcd->bqhd", probs_low, value_sel)
        .reshape(rows, local_width)
        .astype(jnp.bfloat16)
    )
    attn_sum = lax.psum(
        jnp.dot(attended, w_out, preferred_element_type=jnp.float32).astype(jnp.bfloat16), "tp"
    ).astype(jnp.float32)
    first_sum = x_float + attn_sum
    normed, norm_pull = jax.vjp(layer_norm, first_sum, gains[0], biases[0])
    normed_low = normed.astype(jnp.bfloat16)
    hidden = jnp.dot(normed_low, w_up, preferred_element_type=jnp.float32)
    activated, gelu_pull = jax.vjp(gelu_tanh, hidden)
    act_low = activated.astype(jnp.bfloat16)
    mlp_sum = lax.psum(
        jnp.dot(act_low, w_down, preferred_element_type=jnp.float32).astype(jnp.bfloat16), "tp"
    ).astype(jnp.float32)
    second_sum = normed + mlp_sum
    result, final_pull = jax.vjp(layer_norm, second_sum, gains[1], biases[1])
    d_second, d_gain_two, d_bias_two = final_pull(out_grad.astype(jnp.float32))
    d_mlp = d_second.astype(jnp.bfloat16)
    grad_down = contract("tf,td->fd", act_low, d_mlp)
    d_act = contract("td,fd->tf", d_mlp, w_down)
    d_hidden = gelu_pull(d_act)[0].astype(jnp.bfloat16)
    grad_up = contract("td,tf->df", normed_low, d_hidden)
    d_normed = d_second + lax.psum(
        contract("tf,df->td", d_hidden, w_up).astype(jnp.bfloat16), "tp"
    ).astype(jnp.float32)
    d_first, d_gain_one, d_bias_one = norm_pull(d_normed)
    d_attn = d_first.astype(jnp.bfloat16)
    grad_proj = contract("te,td->ed", attended, d_attn)
    d_attended = (
        contract("td,ed->te", d_attn, w_out)
        .astype(jnp.bfloat16)
        .reshape(own_blocks, BLOCK, local_heads, HD)
    )
    scores = scores_of(query, key_sel, usable, scale)
    probs = jnp.exp(scores - log_total)
    probs_low = probs.astype(jnp.bfloat16)
    d_probs = contract("bqhd,bhkcd->bhqkc", d_attended, value_sel)
    d_scores = probs * (d_probs - jnp.sum(probs * d_probs, axis=(3, 4), keepdims=True))
    d_raw = (d_scores * scale).astype(jnp.bfloat16)
    d_query = (
        contract("bhqkc,bhkcd->bqhd", d_raw, key_sel)
        .reshape(rows, local_width)
        .astype(jnp.bfloat16)
    )
    d_key_sel = contract("bhqkc,bqhd->bhkcd", d_raw, query)
    d_value_sel = contract("bhqkc,bqhd->bhkcd", probs_low, d_attended)
    empty = jnp.zeros((group_blocks, BLOCK, local_heads, HD), jnp.float32)
    d_key_all = (
        empty.at[key_table, :, head_pick, :]
        .add(d_key_sel)
        .reshape(group_blocks * BLOCK, local_width)
    )
    d_value_all = (
        empty.at[key_table, :, head_pick, :]
        .add(d_value_sel)
        .reshape(group_blocks * BLOCK, local_width)
    )
    d_key, d_value = (
        lax.psum_scatter(
            d_key_all.astype(jnp.bfloat16), "ctx", scatter_dimension=0, tiled=True
        ).astype(jnp.float32),
        lax.psum_scatter(
            d_value_all.astype(jnp.bfloat16), "ctx", scatter_dimension=0, tiled=True
        ).astype(jnp.float32),
    )
    d_projected = jnp.stack([d_query, d_key.astype(jnp.bfloat16), d_value.astype(jnp.bfloat16)])
    grad_qkv = contract("td,kte->kde", inputs, d_projected)
    d_inputs = d_first + lax.psum(
        contract("kte,kde->td", d_projected, w_qkv).astype(jnp.bfloat16), "tp"
    ).astype(jnp.float32)
    grad_gains = jnp.stack([d_gain_one, d_gain_two])
    grad_biases = jnp.stack([d_bias_one, d_bias_two])
    shared = (
        lax.psum_scatter(
            grad_qkv.astype(jnp.bfloat16), "dp", scatter_dimension=1, tiled=True
        ).astype(jnp.float32),
        lax.psum_scatter(
            grad_proj.astype(jnp.bfloat16), "dp", scatter_dimension=1, tiled=True
        ).astype(jnp.float32),
        lax.psum_scatter(
            grad_up.astype(jnp.bfloat16), "dp", scatter_dimension=0, tiled=True
        ).astype(jnp.float32),
        lax.psum_scatter(
            grad_down.astype(jnp.bfloat16), "dp", scatter_dimension=1, tiled=True
        ).astype(jnp.float32),
        lax.psum_scatter(
            grad_gains.astype(jnp.bfloat16), "dp", scatter_dimension=1, tiled=True
        ).astype(jnp.float32),
        lax.psum_scatter(
            grad_biases.astype(jnp.bfloat16), "dp", scatter_dimension=1, tiled=True
        ).astype(jnp.float32),
    )
    totals = (
        lax.psum(shared[0].astype(jnp.bfloat16), "ctx").astype(jnp.float32),
        lax.psum(shared[1].astype(jnp.bfloat16), "ctx").astype(jnp.float32),
        lax.psum(shared[2].astype(jnp.bfloat16), "ctx").astype(jnp.float32),
        lax.psum(shared[3].astype(jnp.bfloat16), "ctx").astype(jnp.float32),
        lax.psum(shared[4].astype(jnp.bfloat16), "ctx").astype(jnp.float32),
        lax.psum(shared[5].astype(jnp.bfloat16), "ctx").astype(jnp.float32),
    )
    return (
        result.astype(jnp.bfloat16),
        d_inputs.astype(jnp.bfloat16),
        totals[0],
        totals[1],
        totals[2],
        totals[3],
        totals[4],
        totals[5],
    )


def mul(left, right, left_dim, right_dim):
    dims = (((left_dim,), (right_dim,)), ((), ()))
    return lax.dot_general(left, right, dims, preferred_element_type=jnp.float32)


def call(body, outs, *args, scratch=(), copies=0, spec=None, room=32, flops=0):
    spec = spec or pl.BlockSpec(memory_space=pltpu.VMEM)
    specs = [spec] * len(args)
    shapes = [jax.ShapeDtypeStruct(shape, dtype) for shape, dtype in outs]
    return pl.pallas_call(
        body,
        out_shape=shapes,
        in_specs=specs,
        out_specs=[pl.BlockSpec(memory_space=pltpu.VMEM)] * len(shapes),
        scratch_shapes=[pltpu.VMEM(shape, dtype) for shape, dtype in scratch]
        + ([pltpu.SemaphoreType.DMA((copies,))] if copies else []),
        compiler_params=pltpu.CompilerParams(vmem_limit_bytes=room << 20),
        cost_estimate=pl.CostEstimate(flops=flops, bytes_accessed=0, transcendentals=0),
    )(*args)


def head_masks(width):
    lane = lax.broadcasted_iota(jnp.int32, (1, width), 1)
    return [(lane >= h * HD) & (lane < (h + 1) * HD) for h in range(width // HD)]


def only(values, mask):
    return jnp.where(mask, values, jnp.zeros_like(values))


def biased(raw, bias):
    blocks = bias.shape[0]
    size = raw.shape[0] // blocks
    return jnp.concatenate([raw[j * size : (j + 1) * size] + bias[j : j + 1] for j in range(blocks)], axis=0)


DIRECT = (0, 2, 4, 6, 1, 3, 5, 7)
OUT_WAYS = (0, 1, 4, 5, 2, 3, 6, 7)
UP_WAYS = (0, 4, 2, 6, 1, 5, 3, 7)
DOWN_WAYS = (0, 4, 1, 5, 2, 6, 3, 7)


def place(pieces, all_ref, ways, window=0):
    width = all_ref.shape[1]
    parts = []
    for piece in pieces:
        parts += [piece] if len(piece.shape) == 2 else [piece.at[i] for i in range(piece.shape[0])]
    for part, bits in zip(parts, ways, strict=True):
        shard = part.shape[0]
        owner = lax.axis_index("dp") ^ bits
        start = window if part.shape[1] > width else 0
        all_ref[pl.ds(pl.multiple_of(owner * shard, 32), shard), :] = part[:, start : start + width]


def fetch(pairs, sems):
    copies = [pltpu.make_async_copy(src, dst, sems.at[i]) for i, (src, dst) in enumerate(pairs)]
    for copy in copies:
        copy.start()
    for copy in copies:
        copy.wait()


def own_half(src, dst):
    n = dst.shape[1]
    dst[...] = jnp.where(lax.axis_index("ctx") == 0, src[:, :n], src[:, n:])


def pack_first_body(qkv_hbm, gain_hbm, bias_hbm, out_hbm, w_ref, pack_ref, qkv, gain, bias, out, sems):
    fetch(((qkv_hbm, qkv), (gain_hbm, gain), (bias_hbm, bias), (out_hbm, out)), sems)
    c = lax.axis_index("ctx")
    n = qkv.shape[2] // 2
    for i in range(3):
        w_ref[:, i * n : (i + 1) * n] = jnp.where(c == 0, qkv[i, :, :n], qkv[i, :, n:])
    m = out.shape[1] // 2
    extra = pack_ref.shape[1] - 3 * n - m
    row = lax.broadcasted_iota(jnp.int32, (2, extra), 0)
    lane = lax.broadcasted_iota(jnp.int32, (2, extra), 1)
    cols = mul(gain[...], (row == lane).astype(jnp.bfloat16), 0, 0)
    cols = cols + mul(bias[...], (row + 2 == lane).astype(jnp.bfloat16), 0, 0)
    pack_ref[:, 0:m] = jnp.where(c == 0, out[:, :m], out[:, m:])
    pack_ref[:, m : m + extra] = cols.astype(jnp.bfloat16)
    pack_ref[:, m + extra :] = w_ref[...]


def pack_second_body(up_hbm, down_hbm, up_ref, down_ref, up, down, sems):
    fetch(((up_hbm, up), (down_hbm, down)), sems)
    own_half(up, up_ref)
    own_half(down, down_ref)


def attend_body(
    own_ref, far_ref, w0, w1, w2, w3, w4, w5, bias_ref,
    o_ref, qkv_ref, lse_ref, x_ref, w_ref, p_scr, v_scr,
):
    width = o_ref.shape[1]
    rows = x_ref.shape[0]
    part = far_ref.shape[0] // 2
    c = lax.axis_index("ctx")
    for t in range(2):
        x_ref[pl.ds((2 * t + c) * part, part), :] = own_ref[t * part : (t + 1) * part, :]
        x_ref[pl.ds((2 * t + 1 - c) * part, part), :] = far_ref[t * part : (t + 1) * part, :]
    place((w0, w1, w2, w3, w4, w5), w_ref, DIRECT, w4.shape[1] - w_ref.shape[1])
    scale = jnp.bfloat16(1.0 / math.sqrt(HD))
    w = w_ref[...]
    qkv = mul(x_ref[...], w, 1, 0).astype(jnp.bfloat16)
    qkv_ref[...] = qkv
    q, k, v = [qkv[:, i * width : (i + 1) * width] for i in range(3)]
    q = q * scale
    lse_ref[...] = jnp.zeros_like(lse_ref)
    blocks = bias_ref.shape[0] // (width // HD)
    for h, mask in enumerate(head_masks(width)):
        s = biased(mul(k, only(q, mask), 1, 1), bias_ref[h * blocks : (h + 1) * blocks, :])
        top = jnp.max(s, axis=0, keepdims=True)
        e = jnp.exp(s - top)
        total = jnp.sum(e, axis=0, keepdims=True)
        lse_ref[h : h + 1, :] = top + jnp.log(total)
        p_scr[h * rows : (h + 1) * rows, :] = (e * (1.0 / total)).astype(jnp.bfloat16)
        v_scr[h * rows : (h + 1) * rows, :] = only(v, mask)
    o_ref[...] = mul(p_scr[...], v_scr[...], 0, 0).astype(jnp.bfloat16)


def split_rows(value_of, mine_ref, theirs_ref):
    half = mine_ref.shape[0]
    t = lax.axis_index("tp")
    theirs_ref[...] = value_of(pl.ds((1 - t) * half, half)).astype(theirs_ref.dtype)
    mine_ref[...] = value_of(pl.ds(t * half, half))


def project_body(ways, o_ref, *refs):
    *pieces, theirs_ref, w_ref = refs
    place(pieces, w_ref, ways)
    rows = part_rows(theirs_ref.shape[0], False)
    theirs_ref[...] = mul(o_ref[rows, :], w_ref[...], 1, 1).astype(jnp.bfloat16)


def project_out_body(ways, o_ref, *refs):
    *pieces, mine_ref, theirs_ref, w_ref, vec_ref, scr = refs
    place(pieces, scr, ways)
    n = w_ref.shape[1]
    w_ref[...] = scr[:, 0:n]
    extra = scr.shape[1] - n
    unit = (
        lax.broadcasted_iota(jnp.int32, (8, extra), 0) == lax.broadcasted_iota(jnp.int32, (8, extra), 1)
    ).astype(jnp.bfloat16)
    vec_ref[...] = mul(unit, scr[:, n:], 1, 1)
    split_rows(lambda rows: mul(o_ref[rows, :], w_ref[...], 1, 1), mine_ref, theirs_ref)


def add_tp_body(mine_ref, both_ref, sum_ref):
    sum_ref[...] = (mine_ref[...] + both_ref[1 - lax.axis_index("tp")].astype(jnp.float32)).astype(jnp.bfloat16)


def norm_parts(z):
    centred = z - jnp.mean(z, axis=1, keepdims=True)
    r = lax.rsqrt(jnp.mean(centred * centred, axis=1, keepdims=True) + eps)
    return centred * r, r


def norm_back(e2, n, r):
    return r * (e2 - jnp.mean(e2, axis=1, keepdims=True) - n * jnp.mean(e2 * n, axis=1, keepdims=True))


def norm_one_body(x_ref, a_ref, far_ref, vec_ref, n_ref, r_ref, low_ref):
    half = n_ref.shape[0]
    z = x_ref[pl.ds(lax.axis_index("tp") * half, half), :].astype(jnp.float32)
    z = z + (a_ref[...].astype(jnp.float32) + far_ref[...].astype(jnp.float32))
    n, r = norm_parts(z)
    n_ref[...] = n
    r_ref[...] = jnp.broadcast_to(r, r_ref.shape)
    low_ref[...] = (n * vec_ref[0:1, :] + vec_ref[2:3, :]).astype(jnp.bfloat16)


def ffn_body(y_ref, w0, w1, w2, w3, u_ref, slope_ref, up_ref):
    place((w0, w1, w2, w3), up_ref, UP_WAYS)
    hid = mul(y_ref[...], up_ref[...], 1, 0)
    root = math.sqrt(2.0 / math.pi)
    square = hid * hid
    bent = jnp.tanh(root * (hid + 0.044715 * (square * hid)))
    u_ref[...] = (0.5 * hid * (1.0 + bent)).astype(jnp.bfloat16)
    slope = 0.5 * (1.0 + bent) + 0.5 * hid * (1.0 - bent * bent) * (root * (1.0 + 3 * 0.044715 * square))
    slope_ref[...] = slope.astype(jnp.bfloat16)


def norm_two_body(n1_ref, m_ref, far_ref, e_ref, e_far_ref, vec_ref, out_ref, dz_ref, low_ref, grad_ref, e_scr, out_scr):
    part = out_ref.shape[0]
    c, t = lax.axis_index("ctx"), lax.axis_index("tp")
    e_scr[pl.ds(c * part, part), :] = e_ref[pl.ds(t * part, part), :].astype(jnp.float32)
    e_scr[pl.ds((1 - c) * part, part), :] = e_far_ref[pl.ds(t * part, part), :].astype(jnp.float32)
    y1 = n1_ref[...] * vec_ref[0:1, :] + vec_ref[2:3, :]
    z = y1 + (m_ref[...].astype(jnp.float32) + far_ref[...].astype(jnp.float32))
    n, r = norm_parts(z)
    out_scr[...] = n * vec_ref[1:2, :] + vec_ref[3:4, :]
    out_ref[...] = out_scr[pl.ds(c * part, part), :].astype(jnp.bfloat16)
    e = e_scr[...]
    dz = norm_back(e * vec_ref[1:2, :], n, r)
    dz_ref[...] = dz
    low_ref[...] = dz.astype(jnp.bfloat16)
    grad_ref[...] = jnp.zeros_like(grad_ref)
    grad_ref[1:2, :] = jnp.sum(e * n, axis=0, keepdims=True)
    grad_ref[3:4, :] = jnp.sum(e, axis=0, keepdims=True)


def join(near_ref, far_ref, all_ref):
    half = near_ref.shape[0]
    t = lax.axis_index("tp")
    all_ref[pl.ds(t * half, half), :] = near_ref[...]
    all_ref[pl.ds((1 - t) * half, half), :] = far_ref[...]


def part_rows(half, mine):
    t = lax.axis_index("tp")
    return pl.ds((t if mine else 1 - t) * half, half)


def ffn_back_body(near_ref, far_ref, slope_ref, down_ref, up_ref, dm_ref, dhid_ref, theirs_ref):
    join(near_ref, far_ref, dm_ref)
    du = mul(dm_ref[...], down_ref[...], 1, 0)
    dhid_ref[...] = (du * slope_ref[...].astype(jnp.float32)).astype(jnp.bfloat16)
    theirs_ref[...] = mul(dhid_ref[part_rows(near_ref.shape[0], False), :], up_ref[...], 1, 1).astype(jnp.bfloat16)


def part_body(rows_ref, w_ref, mine_ref):
    mine_ref[...] = mul(rows_ref[part_rows(mine_ref.shape[0], True), :], w_ref[...], 1, 1)


def add_far_body(mine_ref, far_ref, sum_ref):
    sum_ref[...] = (mine_ref[...] + far_ref[...].astype(jnp.float32)).astype(jnp.bfloat16)


def deal(own_ref, away_ref, scr, order, start=0):
    one, two, three = order
    shard, width = own_ref.shape[1:]
    dp = lax.axis_index("dp")
    for i, bits in enumerate((0, three, two, two ^ three)):
        for ref, owner in ((own_ref, dp ^ bits), (away_ref, dp ^ bits ^ one)):
            part = scr[pl.ds(pl.multiple_of(owner * shard, 32), shard), start : start + width]
            ref[i] = part.astype(ref.dtype)


def grad_body(order, left_ref, right_ref, own_ref, away_ref, scr):
    scr[...] = mul(left_ref[...], right_ref[...], 0, 0).astype(scr.dtype)
    deal(own_ref, away_ref, scr, order)


def deal_two(own_ref, away_ref, own2_ref, away2_ref, scr):
    deal(own_ref, away_ref, scr, (1, 2, 4))
    deal(own2_ref, away2_ref, scr, (2, 1, 4), own_ref.shape[2])


def fold_pair(own_ref, got_ref, keep_ref, send_ref):
    half = keep_ref.shape[0]
    keep_ref[...] = own_ref[0:half].astype(jnp.float32) + got_ref[0:half].astype(jnp.float32)
    send_ref[...] = (own_ref[half:].astype(jnp.float32) + got_ref[half:].astype(jnp.float32)).astype(jnp.bfloat16)


def fold_body(own_ref, got_ref, keep_ref, send_ref):
    fold_pair(own_ref, got_ref, keep_ref, send_ref)


def fold_two_body(own_ref, got_ref, own2_ref, got2_ref, keep_ref, send_ref, keep2_ref, send2_ref):
    fold_pair(own_ref, got_ref, keep_ref, send_ref)
    fold_pair(own2_ref, got2_ref, keep2_ref, send2_ref)


def fold_join_body(own_ref, got_ref, own2_ref, got2_ref, keep_ref, send_ref):
    width = own_ref.shape[2]
    for own, got, lanes in ((own_ref, got_ref, slice(0, width)), (own2_ref, got2_ref, slice(width, keep_ref.shape[2]))):
        keep_ref[0, :, lanes] = own[0] + got[0].astype(jnp.float32)
        send_ref[0, :, lanes] = (own[1] + got[1].astype(jnp.float32)).astype(jnp.bfloat16)


def fold_last_body(own_ref, got_ref, sum_ref):
    sum_ref[...] = (own_ref[0] + got_ref[0].astype(jnp.float32)).astype(jnp.bfloat16)


def norm_one_back_body(dz2_ref, d_ref, far_ref, n_ref, r_ref, vec_ref, grad2_ref, dz_ref, low_ref):
    dy = dz2_ref[...] + (d_ref[...].astype(jnp.float32) + far_ref[...].astype(jnp.float32))
    n = n_ref[...]
    dz = norm_back(dy * vec_ref[0:1, :], n, r_ref[:, 0:1])
    dz_ref[...] = dz
    half = dz.shape[0]
    low_ref[0:half, :] = dz.astype(jnp.bfloat16)
    sums = [
        jnp.sum(dy * n, axis=0, keepdims=True), grad2_ref[1:2, :],
        jnp.sum(dy, axis=0, keepdims=True), grad2_ref[3:4, :], jnp.zeros((12, dz.shape[1]), jnp.float32),
    ]
    low_ref[half : half + 16, :] = jnp.concatenate(sums, axis=0).astype(jnp.bfloat16)


def attend_back_body(
    da_ref, w_out_ref, qkv_ref, o_ref, lse_ref, bias_ref, x_ref,
    own_ref, away_ref, own2_ref, away2_ref, all_scr,
    p_scr, dr_scr, q_scr, do_scr, grad_scr,
):
    width = o_ref.shape[1]
    rows = x_ref.shape[0]
    scale = jnp.bfloat16(1.0 / math.sqrt(HD))
    half = rows // 2
    da = jnp.concatenate([da_ref[0, 0:half, :], da_ref[1, 0:half, :]], axis=0)
    do = mul(da, w_out_ref[...], 1, 0).astype(jnp.bfloat16)
    q, k, v = [qkv_ref[:, i * width : (i + 1) * width] for i in range(3)]
    q = q * scale
    k_scaled = k * scale
    blocks = bias_ref.shape[0] // (width // HD)
    dq = jnp.zeros((rows, width), jnp.float32)
    for h, mask in enumerate(head_masks(width)):
        q_h, do_h = only(q, mask), only(do, mask)
        s = biased(mul(k, q_h, 1, 1), bias_ref[h * blocks : (h + 1) * blocks, :])
        p = jnp.exp(s - lse_ref[h : h + 1, :])
        dp = mul(v, do_h, 1, 1)
        pd = p * dp
        ds = pd - p * jnp.sum(pd, axis=0, keepdims=True)
        dr = ds.astype(jnp.bfloat16)
        p_scr[:, h * rows : (h + 1) * rows] = p.astype(jnp.bfloat16)
        dr_scr[:, h * rows : (h + 1) * rows] = dr
        q_scr[h * rows : (h + 1) * rows, :] = q_h
        do_scr[h * rows : (h + 1) * rows, :] = do_h
        dq = dq + mul(dr, only(k_scaled, mask), 0, 0)
    all_scr[:, 0:width] = dq.astype(jnp.bfloat16)
    all_scr[:, width : 2 * width] = mul(dr_scr[...], q_scr[...], 1, 0).astype(jnp.bfloat16)
    all_scr[:, 2 * width : 3 * width] = mul(p_scr[...], do_scr[...], 1, 0).astype(jnp.bfloat16)
    vec = sum(da_ref[i, half : half + 16, :].astype(jnp.float32) for i in range(2)).astype(jnp.bfloat16)
    extra = grad_scr.shape[1] - 4 * width
    unit = (
        lax.broadcasted_iota(jnp.int32, (16, extra), 0) == lax.broadcasted_iota(jnp.int32, (16, extra), 1)
    ).astype(jnp.bfloat16)
    grad_scr[...] = jnp.concatenate(
        [mul(x_ref[...], all_scr[...], 0, 0), mul(vec, unit, 0, 0), mul(da, o_ref[...], 0, 0)], axis=1
    ).astype(grad_scr.dtype)
    deal_two(own_ref, away_ref, own2_ref, away2_ref, grad_scr)


def input_body(grad_ref, w_ref, mine_ref, theirs_ref):
    split_rows(lambda rows: mul(grad_ref[rows, :], w_ref[...], 1, 1), mine_ref, theirs_ref)


def fold_input_body(mine_ref, both_ref, dz_ref, keep_ref, send_ref):
    part = keep_ref.shape[0]
    c, far = lax.axis_index("ctx"), 1 - lax.axis_index("tp")
    own, other = pl.ds(c * part, part), pl.ds((1 - c) * part, part)
    send_ref[...] = (mine_ref[other, :] + both_ref[far, other, :].astype(jnp.float32)).astype(jnp.bfloat16)
    keep_ref[...] = dz_ref[own, :] + (mine_ref[own, :] + both_ref[far, own, :].astype(jnp.float32))


def last_input_body(keep_ref, got_ref, out_ref):
    out_ref[...] = (keep_ref[...] + got_ref[...].astype(jnp.float32)).astype(jnp.bfloat16)


def copy_body(in_ref, out_ref):
    out_ref[...] = in_ref[...]


def finish_body(near_ref, far_ref, qkv_ref, out_ref, gain_ref, bias_ref):
    c = lax.axis_index("ctx")
    n = qkv_ref.shape[2] // 2
    m = out_ref.shape[1] // 2
    near, far = near_ref[...].astype(jnp.float32), far_ref[...].astype(jnp.float32)
    low, high = jnp.where(c == 0, near, far), jnp.where(c == 0, far, near)
    for i in range(3):
        qkv_ref[i] = jnp.concatenate([low[:, i * n : (i + 1) * n], high[:, i * n : (i + 1) * n]], axis=1)
    out_ref[...] = jnp.concatenate([low[:, low.shape[1] - m :], high[:, high.shape[1] - m :]], axis=1)
    vec = near_ref[:, 3 * n : near_ref.shape[1] - m]
    row = lax.broadcasted_iota(jnp.int32, (2, vec.shape[1]), 0)
    lane = lax.broadcasted_iota(jnp.int32, (2, vec.shape[1]), 1)
    gain_ref[...] = mul((row == lane).astype(jnp.bfloat16), vec, 1, 1)
    bias_ref[...] = mul((row + 2 == lane).astype(jnp.bfloat16), vec, 1, 1)


def rows_device(
    dims,
    inputs,
    qkv_weight,
    out_weight,
    up_weight,
    down_weight,
    norm_gains,
    norm_biases,
    lengths,
    random_blocks,
    out_grad,
):
    n_dp = dims["dp"]
    n_out = n_dp // 2
    c = lax.axis_index("ctx")
    f32, bf16 = jnp.float32, jnp.bfloat16
    pair = [(0, 1), (1, 0)]

    def swap_tp(v):
        return lax.ppermute(v, "tp", pair)

    def both_tp(v, tiled=False):
        return lax.all_gather(v, "tp", axis=0, tiled=tiled)

    def swap_ctx(v):
        return lax.ppermute(v, "ctx", pair)

    def swap_dp(v, bits):
        return lax.ppermute(v, "dp", [(i, i ^ bits) for i in range(n_dp)])

    def after(v, *others):
        return lax.optimization_barrier((v,) + others)[0]

    def all_after(vs, *others):
        return list(lax.optimization_barrier(tuple(vs) + others)[: len(vs)])

    rows, width = inputs.shape
    part = rows // 2
    shard = qkv_weight.shape[1]
    cols = qkv_weight.shape[2] // 2
    units = up_weight.shape[1] // 2
    heads = cols // HD
    own_blocks = rows // BLOCK
    per = own_blocks // 2
    total_rows = 2 * rows
    extra = 4 + (-(4 * cols + 4)) % 64

    half = ((part, width), bf16)
    hbm = pl.BlockSpec(memory_space=pltpu.HBM)

    def packed(body, widths, *given):
        return call(
            body, [((shard, n), bf16) for n in widths], *given,
            scratch=[(w.shape, bf16) for w in given], copies=len(given), spec=hbm, room=60,
        )

    x_far = swap_ctx(inputs)
    w1, pack_one = packed(
        pack_first_body, (3 * cols, 4 * cols + extra), qkv_weight, norm_gains, norm_biases, out_weight.T
    )
    w1_near = [swap_dp(w1, 2 * k) for k in range(1, n_out)]
    far_one = swap_dp(pack_one, 1)
    w_up, w_down = packed(pack_second_body, (units, units), up_weight, down_weight.T)
    picks_far = swap_ctx(random_blocks)
    out_first = jnp.stack([pack_one[:, : cols + extra], far_one[:, : cols + extra]])
    out_next = swap_dp(out_first, 4)
    w1_near = all_after(w1_near, far_one, out_first)
    w1_rest = jnp.stack(w1_near)
    w1_pieces = [w1, *w1_near, far_one, swap_dp(w1_rest, 1)]
    out_pieces = [out_first, out_next]
    out_pieces.append(swap_dp(jnp.concatenate(out_pieces), 2))
    up_pieces, down_pieces = all_after([w_up[None], w_down[None]], w1_rest)
    up_pieces = [up_pieces, swap_dp(up_pieces, 4)]
    down_pieces = [down_pieces, swap_dp(down_pieces, 4)]
    e_far = swap_ctx(after(out_grad, *w1_near))

    picks = jnp.where(c == 0, jnp.stack([random_blocks, picks_far]), jnp.stack([picks_far, random_blocks]))
    picks = lax.dynamic_slice_in_dim(picks.reshape(2 * own_blocks, 2 * heads, 3), c * heads, heads, 1)
    blocks = jnp.arange(2 * own_blocks, dtype=jnp.int32)
    table, usable = block_table(blocks, lengths[0], picks)
    named = (table[..., None] == blocks) & usable[:, None, :, None]
    counts = jnp.sum(named.astype(f32), axis=2)
    counts = counts.reshape(2, 2, per, heads, 2, 2, per).transpose(3, 5, 4, 6, 1, 0, 2)
    bias = jnp.where(counts > 0, jnp.log(jnp.maximum(counts, 1.0)), -1e30)
    bias = bias.reshape(heads * 2 * own_blocks, 2 * own_blocks, 1)
    bias = jnp.broadcast_to(bias, bias.shape[:2] + (BLOCK,)).reshape(-1, total_rows)

    low = [((rows, width), bf16)]
    wide = [((rows, width), f32)]
    small = [((8, width), f32)]
    o, qkv, lse, x_all, w1_all = call(
        attend_body,
        [
            ((total_rows, cols), bf16), ((total_rows, 3 * cols), bf16), ((8, total_rows), f32),
            ((total_rows, width), bf16), ((width, 3 * cols), bf16),
        ],
        inputs, x_far, *w1_pieces, bias,
        scratch=[((heads * total_rows, total_rows), bf16), ((heads * total_rows, cols), bf16)],
        flops=0,
    )

    def sum_tp(mine, theirs):
        return call(add_tp_body, low, mine, both_tp(theirs))[0]

    mine, theirs, w_out_all, vecs = call(
        functools.partial(project_out_body, OUT_WAYS), wide + low + [((width, cols), bf16)] + small, o, *out_pieces,
        scratch=[((width, cols + extra), bf16)],
    )
    theirs, up_pieces[1], down_pieces[1] = all_after([theirs, up_pieces[1], down_pieces[1]])
    up_pieces.append(swap_dp(jnp.concatenate(up_pieces), 2))
    down_pieces.append(swap_dp(jnp.concatenate(down_pieces), 1))
    a = after(sum_tp(mine, theirs), e_far)
    a_far = swap_ctx(a)
    up_pieces.append(swap_dp(jnp.concatenate(up_pieces), 1))
    down_pieces.append(swap_dp(jnp.concatenate(down_pieces), 2))
    n1, r1, y_low = call(norm_one_body, wide + [((rows, 128), f32)] + low, x_all, a, a_far, vecs)
    flat = [((total_rows, units), bf16)]
    square = [((width, units), bf16)]
    y_all = both_tp(y_low, True)
    u, slope, w_up_all = call(ffn_body, flat * 2 + square, y_all, *up_pieces)
    theirs, w_down_all = call(functools.partial(project_body, DOWN_WAYS), low + square, u, *down_pieces)
    mine = call(part_body, wide, u, w_down_all)[0]
    m = call(add_far_body, low, mine, swap_tp(theirs))[0]
    m_far = swap_ctx(m)
    out, dz2, dm_low, grad2 = call(
        norm_two_body,
        [((part, width), bf16)] + wide + low + small,
        n1, m, m_far, out_grad, e_far, vecs,
        scratch=wide * 2,
    )

    def pairs(k, *widths):
        return [((k, shard, n), dtype) for n in widths for dtype in (f32, bf16)]

    def cut(n):
        most = n * 2 // 3 // 128 * 128
        return most, n - most

    def fold(own, got):
        return call(fold_body, pairs(own.shape[0] // 2, own.shape[2]), own, got)

    def fold_first(own, away, own2, away2):
        return call(fold_two_body, pairs(2, own.shape[2], own2.shape[2]), own, swap_dp(away, 1), own2, swap_dp(away2, 2))

    def fold_third(keep, send, bits):
        total = call(fold_last_body, [(keep.shape[1:], bf16)], keep, swap_dp(send, bits))[0]
        return total, swap_ctx(total)

    dm_all, dhid, theirs = call(
        ffn_back_body, [((total_rows, width), bf16)] + flat + low, dm_low, swap_tp(dm_low), slope, w_down_all, w_up_all
    )
    down_own, down_away = call(
        functools.partial(grad_body, (2, 1, 4)), [((n_out, shard, units), bf16)] * 2, dm_all, u, scratch=[((width, units), bf16)]
    )
    mine = call(part_body, wide, dhid, w_up_all)[0]
    d = call(add_far_body, low, after(mine, down_away), swap_tp(theirs))[0]
    d_far = swap_ctx(d)
    y_late, dhid = lax.optimization_barrier((y_all, dhid, d))[:2]
    up = call(
        functools.partial(grad_body, (1, 4, 2)), [((n_out, shard, units), bf16)] * 2, y_late, dhid, scratch=[((width, units), bf16)]
    )
    output = call(copy_body, low, both_tp(after(out, up[1]), True))[0]
    dz1, da_low = call(
        norm_one_back_body, wide + [((rows + 16, width), bf16)], dz2, d, after(d_far, up[1], output), n1, r1, vecs, grad2
    )
    down_keep, down_send = fold(after(down_own, da_low), swap_dp(down_away, 2))
    last = 4 * cols + extra
    *tail, dqkv = call(
        attend_back_body,
        [((n_out, shard, n), bf16) for n in cut(last) for _ in range(2)] + [((total_rows, 3 * cols), bf16)],
        after(both_tp(da_low), down_send), w_out_all, qkv, o, lse, bias, x_all,
        flops=2 * 10**10,
        scratch=[
            ((total_rows, heads * total_rows), bf16),
            ((total_rows, heads * total_rows), bf16),
            ((heads * total_rows, cols), bf16),
            ((heads * total_rows, cols), bf16),
            ((width, last), bf16),
        ],
    )
    mine, theirs = call(input_body, wide + low, dqkv, w1_all)
    down = fold(after(down_keep, theirs), swap_dp(down_send, 1))
    theirs = after(theirs, down[1])
    keep, send = call(fold_input_body, [((part, width), f32), half], mine, both_tp(theirs), dz1)
    up = fold(after(up[0], mine), swap_dp(up[1], 1))
    keep1, send1, keep2, send2 = fold_first(*all_after(tail[:1], send), *tail[1:])
    got1, got2 = swap_dp(send1, 2), swap_dp(send2, 1)
    dx_far = swap_ctx(send)
    up = fold(after(up[0], keep1), swap_dp(up[1], 4))
    keep1 = after(keep1, dx_far, up[1])
    tail = call(fold_join_body, pairs(1, last), keep1, got1, keep2, got2)
    grad_down, down_far = fold_third(*all_after(down[:1], tail[0]), down[1], 4)
    grad_1, far_1 = fold_third(after(tail[0], grad_down), tail[1], 4)
    grad_up, up_far = fold_third(*all_after(up[:1], grad_1), up[1], 2)
    down_far = after(down_far, grad_up)
    dx = call(last_input_body, [half], keep, after(dx_far, grad_up))[0]
    input_grad = call(copy_body, low, both_tp(dx, True))[0]
    grad_1 = after(grad_1, input_grad)

    def both_ctx(g, far):
        return jnp.where(c == 0, jnp.concatenate([g, far], 1), jnp.concatenate([far, g], 1)).astype(f32)

    grad_qkv, grad_out, gains, biases = call(
        finish_body,
        [((3, shard, 2 * cols), f32), ((shard, 2 * cols), f32), ((2, shard), f32), ((2, shard), f32)],
        grad_1, far_1,
    )
    return (
        output, input_grad, grad_qkv, grad_out.T, both_ctx(grad_up, up_far), both_ctx(grad_down, down_far).T, gains, biases
    )


def solution(mesh):
    dims = dict(mesh.shape)
    fast = dims["ctx"] == 2 and dims["tp"] == 2 and dims["dp"] == 8
    step = functools.partial(rows_device, dims) if fast else per_device
    return jax.shard_map(
        step,
        mesh=mesh,
        in_specs=(
            P(("dp", "ctx"), None),
            P(None, "dp", "tp"),
            P("tp", "dp"),
            P("dp", "tp"),
            P("tp", "dp"),
            P(None, "dp"),
            P(None, "dp"),
            P("dp", None),
            P(("dp", "ctx"), "tp", None),
            P(("dp", "ctx"), None),
        ),
        out_specs=(
            P(("dp", "ctx"), None),
            P(("dp", "ctx"), None),
            P(None, "dp", "tp"),
            P("tp", "dp"),
            P("dp", "tp"),
            P("tp", "dp"),
            P(None, "dp"),
            P(None, "dp"),
        ),
        check_vma=False,
    )
```

```python
import functools
import math

import jax
import jax.numpy as jnp
from jax import lax
from jax.experimental import pallas as pl
from jax.experimental.pallas import tpu as pltpu
from jax.sharding import PartitionSpec as P

HD = 64
BLOCK = 64


eps = 1e-06


def layer_norm(values, gain, shift):
    row_mean = jnp.mean(values, axis=-1, keepdims=True)
    centred = values - row_mean
    spread = jnp.mean(centred * centred, axis=-1, keepdims=True)
    return centred * lax.rsqrt(spread + eps) * gain + shift


def gelu_tanh(values):
    return jax.nn.gelu(values, approximate=True)


def contract(form, left, right):
    return jnp.einsum(form, left, right, preferred_element_type=jnp.float32)


def block_table(blocks, lengths_row, offsets):
    seq_ends = jnp.cumsum(lengths_row)
    starts = seq_ends - lengths_row
    inside = ((blocks[:, None] >= starts[None, :]) & (blocks[:, None] < seq_ends[None, :])).astype(
        jnp.int32
    )
    seq_first = jnp.sum(inside * starts[None, :], axis=1)
    seq_count = jnp.sum(inside * lengths_row[None, :], axis=1)
    position = blocks - seq_first
    has_before = position > 0
    has_behind = position < seq_count - 1
    before = jnp.where(has_before, blocks - 1, blocks)
    behind = jnp.where(has_behind, blocks + 1, blocks)
    fixed_ids = jnp.stack([before, blocks, behind, seq_first, seq_first + 1], axis=-1)
    random_ids = seq_first[:, None, None] + offsets % seq_count[:, None, None]
    head_count = offsets.shape[1]
    key_table = jnp.concatenate(
        [jnp.broadcast_to(fixed_ids[:, None, :], (blocks.shape[0], head_count, 5)), random_ids],
        axis=-1,
    )
    always = jnp.ones_like(has_before)
    usable = jnp.stack(
        [has_before, always, has_behind, always, always] + [always] * offsets.shape[2], axis=-1
    )
    return (key_table, usable)


def scores_of(query, key_sel, usable, scale):
    raw = contract("bqhd,bhkcd->bhqkc", query, key_sel)
    return jnp.where(usable[:, None, None, :, None], raw * scale, -1e30)


def per_device(
    inputs,
    qkv_weight,
    out_weight,
    up_weight,
    down_weight,
    norm_gains,
    norm_biases,
    lengths,
    random_blocks,
    out_grad,
):
    w_qkv, w_out, w_up, w_down, gains_low, biases_low = (
        lax.all_gather(qkv_weight, "dp", axis=1, tiled=True),
        lax.all_gather(out_weight, "dp", axis=1, tiled=True),
        lax.all_gather(up_weight, "dp", axis=0, tiled=True),
        lax.all_gather(down_weight, "dp", axis=1, tiled=True),
        lax.all_gather(norm_gains, "dp", axis=1, tiled=True),
        lax.all_gather(norm_biases, "dp", axis=1, tiled=True),
    )
    gains = gains_low.astype(jnp.float32)
    biases = biases_low.astype(jnp.float32)
    rows = inputs.shape[0]
    own_blocks = rows // BLOCK
    local_width = w_qkv.shape[2]
    local_heads = local_width // HD
    scale = 1.0 / math.sqrt(HD)
    x_float = inputs.astype(jnp.float32)
    projected = contract("td,kde->kte", inputs, w_qkv)
    q_low = projected[0].astype(jnp.bfloat16)
    k_low = projected[1].astype(jnp.bfloat16)
    v_low = projected[2].astype(jnp.bfloat16)
    key_all, value_all = (
        lax.all_gather(k_low, "ctx", axis=0, tiled=True),
        lax.all_gather(v_low, "ctx", axis=0, tiled=True),
    )
    group_blocks = key_all.shape[0] // BLOCK
    first_block = lax.axis_index("ctx") * own_blocks
    blocks = first_block + jnp.arange(own_blocks, dtype=jnp.int32)
    key_table, usable = block_table(blocks, lengths[0], random_blocks)
    head_pick = jnp.arange(local_heads, dtype=jnp.int32)[None, :, None]
    key_blocks = key_all.reshape(group_blocks, BLOCK, local_heads, HD)
    value_blocks = value_all.reshape(group_blocks, BLOCK, local_heads, HD)
    key_sel = key_blocks[key_table, :, head_pick, :]
    value_sel = value_blocks[key_table, :, head_pick, :]
    query = q_low.reshape(own_blocks, BLOCK, local_heads, HD)
    scores = scores_of(query, key_sel, usable, scale)
    top = jnp.max(scores, axis=(3, 4), keepdims=True)
    log_total = top + jnp.log(jnp.sum(jnp.exp(scores - top), axis=(3, 4), keepdims=True))
    probs = jnp.exp(scores - log_total)
    probs_low = probs.astype(jnp.bfloat16)
    attended = (
        contract("bhqkc,bhkcd->bqhd", probs_low, value_sel)
        .reshape(rows, local_width)
        .astype(jnp.bfloat16)
    )
    attn_sum = lax.psum(
        jnp.dot(attended, w_out, preferred_element_type=jnp.float32).astype(jnp.bfloat16), "tp"
    ).astype(jnp.float32)
    first_sum = x_float + attn_sum
    normed, norm_pull = jax.vjp(layer_norm, first_sum, gains[0], biases[0])
    normed_low = normed.astype(jnp.bfloat16)
    hidden = jnp.dot(normed_low, w_up, preferred_element_type=jnp.float32)
    activated, gelu_pull = jax.vjp(gelu_tanh, hidden)
    act_low = activated.astype(jnp.bfloat16)
    mlp_sum = lax.psum(
        jnp.dot(act_low, w_down, preferred_element_type=jnp.float32).astype(jnp.bfloat16), "tp"
    ).astype(jnp.float32)
    second_sum = normed + mlp_sum
    result, final_pull = jax.vjp(layer_norm, second_sum, gains[1], biases[1])
    d_second, d_gain_two, d_bias_two = final_pull(out_grad.astype(jnp.float32))
    d_mlp = d_second.astype(jnp.bfloat16)
    grad_down = contract("tf,td->fd", act_low, d_mlp)
    d_act = contract("td,fd->tf", d_mlp, w_down)
    d_hidden = gelu_pull(d_act)[0].astype(jnp.bfloat16)
    grad_up = contract("td,tf->df", normed_low, d_hidden)
    d_normed = d_second + lax.psum(
        contract("tf,df->td", d_hidden, w_up).astype(jnp.bfloat16), "tp"
    ).astype(jnp.float32)
    d_first, d_gain_one, d_bias_one = norm_pull(d_normed)
    d_attn = d_first.astype(jnp.bfloat16)
    grad_proj = contract("te,td->ed", attended, d_attn)
    d_attended = (
        contract("td,ed->te", d_attn, w_out)
        .astype(jnp.bfloat16)
        .reshape(own_blocks, BLOCK, local_heads, HD)
    )
    scores = scores_of(query, key_sel, usable, scale)
    probs = jnp.exp(scores - log_total)
    probs_low = probs.astype(jnp.bfloat16)
    d_probs = contract("bqhd,bhkcd->bhqkc", d_attended, value_sel)
    d_scores = probs * (d_probs - jnp.sum(probs * d_probs, axis=(3, 4), keepdims=True))
    d_raw = (d_scores * scale).astype(jnp.bfloat16)
    d_query = (
        contract("bhqkc,bhkcd->bqhd", d_raw, key_sel)
        .reshape(rows, local_width)
        .astype(jnp.bfloat16)
    )
    d_key_sel = contract("bhqkc,bqhd->bhkcd", d_raw, query)
    d_value_sel = contract("bhqkc,bqhd->bhkcd", probs_low, d_attended)
    empty = jnp.zeros((group_blocks, BLOCK, local_heads, HD), jnp.float32)
    d_key_all = (
        empty.at[key_table, :, head_pick, :]
        .add(d_key_sel)
        .reshape(group_blocks * BLOCK, local_width)
    )
    d_value_all = (
        empty.at[key_table, :, head_pick, :]
        .add(d_value_sel)
        .reshape(group_blocks * BLOCK, local_width)
    )
    d_key, d_value = (
        lax.psum_scatter(
            d_key_all.astype(jnp.bfloat16), "ctx", scatter_dimension=0, tiled=True
        ).astype(jnp.float32),
        lax.psum_scatter(
            d_value_all.astype(jnp.bfloat16), "ctx", scatter_dimension=0, tiled=True
        ).astype(jnp.float32),
    )
    d_projected = jnp.stack([d_query, d_key.astype(jnp.bfloat16), d_value.astype(jnp.bfloat16)])
    grad_qkv = contract("td,kte->kde", inputs, d_projected)
    d_inputs = d_first + lax.psum(
        contract("kte,kde->td", d_projected, w_qkv).astype(jnp.bfloat16), "tp"
    ).astype(jnp.float32)
    grad_gains = jnp.stack([d_gain_one, d_gain_two])
    grad_biases = jnp.stack([d_bias_one, d_bias_two])
    shared = (
        lax.psum_scatter(
            grad_qkv.astype(jnp.bfloat16), "dp", scatter_dimension=1, tiled=True
        ).astype(jnp.float32),
        lax.psum_scatter(
            grad_proj.astype(jnp.bfloat16), "dp", scatter_dimension=1, tiled=True
        ).astype(jnp.float32),
        lax.psum_scatter(
            grad_up.astype(jnp.bfloat16), "dp", scatter_dimension=0, tiled=True
        ).astype(jnp.float32),
        lax.psum_scatter(
            grad_down.astype(jnp.bfloat16), "dp", scatter_dimension=1, tiled=True
        ).astype(jnp.float32),
        lax.psum_scatter(
            grad_gains.astype(jnp.bfloat16), "dp", scatter_dimension=1, tiled=True
        ).astype(jnp.float32),
        lax.psum_scatter(
            grad_biases.astype(jnp.bfloat16), "dp", scatter_dimension=1, tiled=True
        ).astype(jnp.float32),
    )
    totals = (
        lax.psum(shared[0].astype(jnp.bfloat16), "ctx").astype(jnp.float32),
        lax.psum(shared[1].astype(jnp.bfloat16), "ctx").astype(jnp.float32),
        lax.psum(shared[2].astype(jnp.bfloat16), "ctx").astype(jnp.float32),
        lax.psum(shared[3].astype(jnp.bfloat16), "ctx").astype(jnp.float32),
        lax.psum(shared[4].astype(jnp.bfloat16), "ctx").astype(jnp.float32),
        lax.psum(shared[5].astype(jnp.bfloat16), "ctx").astype(jnp.float32),
    )
    return (
        result.astype(jnp.bfloat16),
        d_inputs.astype(jnp.bfloat16),
        totals[0],
        totals[1],
        totals[2],
        totals[3],
        totals[4],
        totals[5],
    )


def mul(left, right, left_dim, right_dim):
    dims = (((left_dim,), (right_dim,)), ((), ()))
    return lax.dot_general(left, right, dims, preferred_element_type=jnp.float32)


def call(body, outs, *args, scratch=(), copies=0, spec=None, room=32, flops=0):
    spec = spec or pl.BlockSpec(memory_space=pltpu.VMEM)
    specs = [spec] * len(args)
    shapes = [jax.ShapeDtypeStruct(shape, dtype) for shape, dtype in outs]
    return pl.pallas_call(
        body,
        out_shape=shapes,
        in_specs=specs,
        out_specs=[pl.BlockSpec(memory_space=pltpu.VMEM)] * len(shapes),
        scratch_shapes=[pltpu.VMEM(shape, dtype) for shape, dtype in scratch]
        + ([pltpu.SemaphoreType.DMA((copies,))] if copies else []),
        compiler_params=pltpu.CompilerParams(vmem_limit_bytes=room << 20),
        cost_estimate=pl.CostEstimate(flops=flops, bytes_accessed=0, transcendentals=0),
    )(*args)


def head_masks(width):
    lane = lax.broadcasted_iota(jnp.int32, (1, width), 1)
    return [(lane >= h * HD) & (lane < (h + 1) * HD) for h in range(width // HD)]


def only(values, mask):
    return jnp.where(mask, values, jnp.zeros_like(values))


def biased(raw, bias):
    blocks = bias.shape[0]
    size = raw.shape[0] // blocks
    return jnp.concatenate([raw[j * size : (j + 1) * size] + bias[j : j + 1] for j in range(blocks)], axis=0)


DIRECT = (0, 2, 4, 6, 1, 3, 5, 7)
OUT_WAYS = (0, 1, 4, 5, 2, 3, 6, 7)
UP_WAYS = (0, 4, 2, 6, 1, 5, 3, 7)
DOWN_WAYS = (0, 4, 1, 5, 2, 6, 3, 7)


def place(pieces, all_ref, ways, window=0):
    width = all_ref.shape[1]
    parts = []
    for piece in pieces:
        parts += [piece] if len(piece.shape) == 2 else [piece.at[i] for i in range(piece.shape[0])]
    for part, bits in zip(parts, ways, strict=True):
        shard = part.shape[0]
        owner = lax.axis_index("dp") ^ bits
        start = window if part.shape[1] > width else 0
        all_ref[pl.ds(pl.multiple_of(owner * shard, 32), shard), :] = part[:, start : start + width]


def fetch(pairs, sems):
    copies = [pltpu.make_async_copy(src, dst, sems.at[i]) for i, (src, dst) in enumerate(pairs)]
    for copy in copies:
        copy.start()
    for copy in copies:
        copy.wait()


def own_half(src, dst):
    n = dst.shape[1]
    dst[...] = jnp.where(lax.axis_index("ctx") == 0, src[:, :n], src[:, n:])


def pack_first_body(qkv_hbm, gain_hbm, bias_hbm, out_hbm, w_ref, pack_ref, qkv, gain, bias, out, sems):
    fetch(((qkv_hbm, qkv), (gain_hbm, gain), (bias_hbm, bias), (out_hbm, out)), sems)
    c = lax.axis_index("ctx")
    n = qkv.shape[2] // 2
    for i in range(3):
        w_ref[:, i * n : (i + 1) * n] = jnp.where(c == 0, qkv[i, :, :n], qkv[i, :, n:])
    m = out.shape[1] // 2
    extra = pack_ref.shape[1] - 3 * n - m
    row = lax.broadcasted_iota(jnp.int32, (2, extra), 0)
    lane = lax.broadcasted_iota(jnp.int32, (2, extra), 1)
    cols = mul(gain[...], (row == lane).astype(jnp.bfloat16), 0, 0)
    cols = cols + mul(bias[...], (row + 2 == lane).astype(jnp.bfloat16), 0, 0)
    pack_ref[:, 0:m] = jnp.where(c == 0, out[:, :m], out[:, m:])
    pack_ref[:, m : m + extra] = cols.astype(jnp.bfloat16)
    pack_ref[:, m + extra :] = w_ref[...]


def pack_second_body(up_hbm, down_hbm, up_ref, down_ref, up, down, sems):
    fetch(((up_hbm, up), (down_hbm, down)), sems)
    own_half(up, up_ref)
    own_half(down, down_ref)


def attend_body(
    own_ref, far_ref, w0, w1, w2, w3, w4, w5, bias_ref,
    o_ref, qkv_ref, lse_ref, x_ref, w_ref, p_scr, v_scr,
):
    width = o_ref.shape[1]
    rows = x_ref.shape[0]
    part = far_ref.shape[0] // 2
    c = lax.axis_index("ctx")
    for t in range(2):
        x_ref[pl.ds((2 * t + c) * part, part), :] = own_ref[t * part : (t + 1) * part, :]
        x_ref[pl.ds((2 * t + 1 - c) * part, part), :] = far_ref[t * part : (t + 1) * part, :]
    place((w0, w1, w2, w3, w4, w5), w_ref, DIRECT, w4.shape[1] - w_ref.shape[1])
    scale = jnp.bfloat16(1.0 / math.sqrt(HD))
    w = w_ref[...]
    qkv = mul(x_ref[...], w, 1, 0).astype(jnp.bfloat16)
    qkv_ref[...] = qkv
    q, k, v = [qkv[:, i * width : (i + 1) * width] for i in range(3)]
    q = q * scale
    lse_ref[...] = jnp.zeros_like(lse_ref)
    blocks = bias_ref.shape[0] // (width // HD)
    for h, mask in enumerate(head_masks(width)):
        s = biased(mul(k, only(q, mask), 1, 1), bias_ref[h * blocks : (h + 1) * blocks, :])
        top = jnp.max(s, axis=0, keepdims=True)
        e = jnp.exp(s - top)
        total = jnp.sum(e, axis=0, keepdims=True)
        lse_ref[h : h + 1, :] = top + jnp.log(total)
        p_scr[h * rows : (h + 1) * rows, :] = (e * (1.0 / total)).astype(jnp.bfloat16)
        v_scr[h * rows : (h + 1) * rows, :] = only(v, mask)
    o_ref[...] = mul(p_scr[...], v_scr[...], 0, 0).astype(jnp.bfloat16)


def split_rows(value_of, mine_ref, theirs_ref):
    half = mine_ref.shape[0]
    t = lax.axis_index("tp")
    theirs_ref[...] = value_of(pl.ds((1 - t) * half, half)).astype(theirs_ref.dtype)
    mine_ref[...] = value_of(pl.ds(t * half, half))


def project_body(ways, o_ref, *refs):
    *pieces, theirs_ref, w_ref = refs
    place(pieces, w_ref, ways)
    rows = part_rows(theirs_ref.shape[0], False)
    theirs_ref[...] = mul(o_ref[rows, :], w_ref[...], 1, 1).astype(jnp.bfloat16)


def project_out_body(ways, o_ref, *refs):
    *pieces, mine_ref, theirs_ref, w_ref, vec_ref, scr = refs
    place(pieces, scr, ways)
    n = w_ref.shape[1]
    w_ref[...] = scr[:, 0:n]
    extra = scr.shape[1] - n
    unit = (
        lax.broadcasted_iota(jnp.int32, (8, extra), 0) == lax.broadcasted_iota(jnp.int32, (8, extra), 1)
    ).astype(jnp.bfloat16)
    vec_ref[...] = mul(unit, scr[:, n:], 1, 1)
    split_rows(lambda rows: mul(o_ref[rows, :], w_ref[...], 1, 1), mine_ref, theirs_ref)


def add_tp_body(mine_ref, both_ref, sum_ref):
    sum_ref[...] = (mine_ref[...] + both_ref[1 - lax.axis_index("tp")].astype(jnp.float32)).astype(jnp.bfloat16)


def norm_parts(z):
    centred = z - jnp.mean(z, axis=1, keepdims=True)
    r = lax.rsqrt(jnp.mean(centred * centred, axis=1, keepdims=True) + eps)
    return centred * r, r


def norm_back(e2, n, r):
    return r * (e2 - jnp.mean(e2, axis=1, keepdims=True) - n * jnp.mean(e2 * n, axis=1, keepdims=True))


def norm_one_body(x_ref, a_ref, far_ref, vec_ref, n_ref, r_ref, low_ref):
    half = n_ref.shape[0]
    z = x_ref[pl.ds(lax.axis_index("tp") * half, half), :].astype(jnp.float32)
    z = z + (a_ref[...].astype(jnp.float32) + far_ref[...].astype(jnp.float32))
    n, r = norm_parts(z)
    n_ref[...] = n
    r_ref[...] = jnp.broadcast_to(r, r_ref.shape)
    low_ref[...] = (n * vec_ref[0:1, :] + vec_ref[2:3, :]).astype(jnp.bfloat16)


def ffn_body(y_ref, w0, w1, w2, w3, u_ref, slope_ref, up_ref):
    place((w0, w1, w2, w3), up_ref, UP_WAYS)
    hid = mul(y_ref[...], up_ref[...], 1, 0)
    root = math.sqrt(2.0 / math.pi)
    square = hid * hid
    bent = jnp.tanh(root * (hid + 0.044715 * (square * hid)))
    u_ref[...] = (0.5 * hid * (1.0 + bent)).astype(jnp.bfloat16)
    slope = 0.5 * (1.0 + bent) + 0.5 * hid * (1.0 - bent * bent) * (root * (1.0 + 3 * 0.044715 * square))
    slope_ref[...] = slope.astype(jnp.bfloat16)


def norm_two_body(n1_ref, m_ref, far_ref, e_ref, e_far_ref, vec_ref, out_ref, dz_ref, low_ref, grad_ref, e_scr, out_scr):
    part = out_ref.shape[0]
    c, t = lax.axis_index("ctx"), lax.axis_index("tp")
    e_scr[pl.ds(c * part, part), :] = e_ref[pl.ds(t * part, part), :].astype(jnp.float32)
    e_scr[pl.ds((1 - c) * part, part), :] = e_far_ref[pl.ds(t * part, part), :].astype(jnp.float32)
    y1 = n1_ref[...] * vec_ref[0:1, :] + vec_ref[2:3, :]
    z = y1 + (m_ref[...].astype(jnp.float32) + far_ref[...].astype(jnp.float32))
    n, r = norm_parts(z)
    out_scr[...] = n * vec_ref[1:2, :] + vec_ref[3:4, :]
    out_ref[...] = out_scr[pl.ds(c * part, part), :].astype(jnp.bfloat16)
    e = e_scr[...]
    dz = norm_back(e * vec_ref[1:2, :], n, r)
    dz_ref[...] = dz
    low_ref[...] = dz.astype(jnp.bfloat16)
    grad_ref[...] = jnp.zeros_like(grad_ref)
    grad_ref[1:2, :] = jnp.sum(e * n, axis=0, keepdims=True)
    grad_ref[3:4, :] = jnp.sum(e, axis=0, keepdims=True)


def join(near_ref, far_ref, all_ref):
    half = near_ref.shape[0]
    t = lax.axis_index("tp")
    all_ref[pl.ds(t * half, half), :] = near_ref[...]
    all_ref[pl.ds((1 - t) * half, half), :] = far_ref[...]


def part_rows(half, mine):
    t = lax.axis_index("tp")
    return pl.ds((t if mine else 1 - t) * half, half)


def ffn_back_body(near_ref, far_ref, slope_ref, down_ref, up_ref, dm_ref, dhid_ref, theirs_ref):
    join(near_ref, far_ref, dm_ref)
    du = mul(dm_ref[...], down_ref[...], 1, 0)
    dhid_ref[...] = (du * slope_ref[...].astype(jnp.float32)).astype(jnp.bfloat16)
    theirs_ref[...] = mul(dhid_ref[part_rows(near_ref.shape[0], False), :], up_ref[...], 1, 1).astype(jnp.bfloat16)


def part_body(rows_ref, w_ref, mine_ref):
    mine_ref[...] = mul(rows_ref[part_rows(mine_ref.shape[0], True), :], w_ref[...], 1, 1)


def add_far_body(mine_ref, far_ref, sum_ref):
    sum_ref[...] = (mine_ref[...] + far_ref[...].astype(jnp.float32)).astype(jnp.bfloat16)


def deal(own_ref, away_ref, scr, order, start=0):
    one, two, three = order
    shard, width = own_ref.shape[1:]
    dp = lax.axis_index("dp")
    for i, bits in enumerate((0, three, two, two ^ three)):
        for ref, owner in ((own_ref, dp ^ bits), (away_ref, dp ^ bits ^ one)):
            part = scr[pl.ds(pl.multiple_of(owner * shard, 32), shard), start : start + width]
            ref[i] = part.astype(ref.dtype)


def grad_body(order, left_ref, right_ref, own_ref, away_ref, scr):
    scr[...] = mul(left_ref[...], right_ref[...], 0, 0).astype(scr.dtype)
    deal(own_ref, away_ref, scr, order)


def deal_two(own_ref, away_ref, own2_ref, away2_ref, scr):
    deal(own_ref, away_ref, scr, (1, 2, 4))
    deal(own2_ref, away2_ref, scr, (2, 1, 4), own_ref.shape[2])


def fold_pair(own_ref, got_ref, keep_ref, send_ref):
    half = keep_ref.shape[0]
    keep_ref[...] = own_ref[0:half].astype(jnp.float32) + got_ref[0:half].astype(jnp.float32)
    send_ref[...] = (own_ref[half:].astype(jnp.float32) + got_ref[half:].astype(jnp.float32)).astype(jnp.bfloat16)


def fold_body(own_ref, got_ref, keep_ref, send_ref):
    fold_pair(own_ref, got_ref, keep_ref, send_ref)


def fold_two_body(own_ref, got_ref, own2_ref, got2_ref, keep_ref, send_ref, keep2_ref, send2_ref):
    fold_pair(own_ref, got_ref, keep_ref, send_ref)
    fold_pair(own2_ref, got2_ref, keep2_ref, send2_ref)


def fold_join_body(own_ref, got_ref, own2_ref, got2_ref, keep_ref, send_ref):
    width = own_ref.shape[2]
    for own, got, lanes in ((own_ref, got_ref, slice(0, width)), (own2_ref, got2_ref, slice(width, keep_ref.shape[2]))):
        keep_ref[0, :, lanes] = own[0] + got[0].astype(jnp.float32)
        send_ref[0, :, lanes] = (own[1] + got[1].astype(jnp.float32)).astype(jnp.bfloat16)


def fold_last_body(own_ref, got_ref, sum_ref):
    sum_ref[...] = (own_ref[0] + got_ref[0].astype(jnp.float32)).astype(jnp.bfloat16)


def norm_one_back_body(dz2_ref, d_ref, far_ref, n_ref, r_ref, vec_ref, grad2_ref, dz_ref, low_ref):
    dy = dz2_ref[...] + (d_ref[...].astype(jnp.float32) + far_ref[...].astype(jnp.float32))
    n = n_ref[...]
    dz = norm_back(dy * vec_ref[0:1, :], n, r_ref[:, 0:1])
    dz_ref[...] = dz
    half = dz.shape[0]
    low_ref[0:half, :] = dz.astype(jnp.bfloat16)
    sums = [
        jnp.sum(dy * n, axis=0, keepdims=True), grad2_ref[1:2, :],
        jnp.sum(dy, axis=0, keepdims=True), grad2_ref[3:4, :], jnp.zeros((12, dz.shape[1]), jnp.float32),
    ]
    low_ref[half : half + 16, :] = jnp.concatenate(sums, axis=0).astype(jnp.bfloat16)


def attend_back_body(
    da_ref, w_out_ref, qkv_ref, o_ref, lse_ref, bias_ref, x_ref,
    own_ref, away_ref, own2_ref, away2_ref, all_scr,
    p_scr, dr_scr, q_scr, do_scr, grad_scr,
):
    width = o_ref.shape[1]
    rows = x_ref.shape[0]
    scale = jnp.bfloat16(1.0 / math.sqrt(HD))
    half = rows // 2
    da = jnp.concatenate([da_ref[0, 0:half, :], da_ref[1, 0:half, :]], axis=0)
    do = mul(da, w_out_ref[...], 1, 0).astype(jnp.bfloat16)
    q, k, v = [qkv_ref[:, i * width : (i + 1) * width] for i in range(3)]
    q = q * scale
    k_scaled = k * scale
    blocks = bias_ref.shape[0] // (width // HD)
    dq = jnp.zeros((rows, width), jnp.float32)
    for h, mask in enumerate(head_masks(width)):
        q_h, do_h = only(q, mask), only(do, mask)
        s = biased(mul(k, q_h, 1, 1), bias_ref[h * blocks : (h + 1) * blocks, :])
        p = jnp.exp(s - lse_ref[h : h + 1, :])
        dp = mul(v, do_h, 1, 1)
        pd = p * dp
        ds = pd - p * jnp.sum(pd, axis=0, keepdims=True)
        dr = ds.astype(jnp.bfloat16)
        p_scr[:, h * rows : (h + 1) * rows] = p.astype(jnp.bfloat16)
        dr_scr[:, h * rows : (h + 1) * rows] = dr
        q_scr[h * rows : (h + 1) * rows, :] = q_h
        do_scr[h * rows : (h + 1) * rows, :] = do_h
        dq = dq + mul(dr, only(k_scaled, mask), 0, 0)
    all_scr[:, 0:width] = dq.astype(jnp.bfloat16)
    all_scr[:, width : 2 * width] = mul(dr_scr[...], q_scr[...], 1, 0).astype(jnp.bfloat16)
    all_scr[:, 2 * width : 3 * width] = mul(p_scr[...], do_scr[...], 1, 0).astype(jnp.bfloat16)
    vec = sum(da_ref[i, half : half + 16, :].astype(jnp.float32) for i in range(2)).astype(jnp.bfloat16)
    extra = grad_scr.shape[1] - 4 * width
    unit = (
        lax.broadcasted_iota(jnp.int32, (16, extra), 0) == lax.broadcasted_iota(jnp.int32, (16, extra), 1)
    ).astype(jnp.bfloat16)
    grad_scr[...] = jnp.concatenate(
        [mul(x_ref[...], all_scr[...], 0, 0), mul(vec, unit, 0, 0), mul(da, o_ref[...], 0, 0)], axis=1
    ).astype(grad_scr.dtype)
    deal_two(own_ref, away_ref, own2_ref, away2_ref, grad_scr)


def input_body(grad_ref, w_ref, mine_ref, theirs_ref):
    split_rows(lambda rows: mul(grad_ref[rows, :], w_ref[...], 1, 1), mine_ref, theirs_ref)


def fold_input_body(mine_ref, both_ref, dz_ref, keep_ref, send_ref):
    part = keep_ref.shape[0]
    c, far = lax.axis_index("ctx"), 1 - lax.axis_index("tp")
    own, other = pl.ds(c * part, part), pl.ds((1 - c) * part, part)
    send_ref[...] = (mine_ref[other, :] + both_ref[far, other, :].astype(jnp.float32)).astype(jnp.bfloat16)
    keep_ref[...] = dz_ref[own, :] + (mine_ref[own, :] + both_ref[far, own, :].astype(jnp.float32))


def last_input_body(keep_ref, got_ref, out_ref):
    out_ref[...] = (keep_ref[...] + got_ref[...].astype(jnp.float32)).astype(jnp.bfloat16)


def copy_body(in_ref, out_ref):
    out_ref[...] = in_ref[...]


def finish_body(near_ref, far_ref, qkv_ref, out_ref, gain_ref, bias_ref):
    c = lax.axis_index("ctx")
    n = qkv_ref.shape[2] // 2
    m = out_ref.shape[1] // 2
    near, far = near_ref[...].astype(jnp.float32), far_ref[...].astype(jnp.float32)
    low, high = jnp.where(c == 0, near, far), jnp.where(c == 0, far, near)
    for i in range(3):
        qkv_ref[i] = jnp.concatenate([low[:, i * n : (i + 1) * n], high[:, i * n : (i + 1) * n]], axis=1)
    out_ref[...] = jnp.concatenate([low[:, low.shape[1] - m :], high[:, high.shape[1] - m :]], axis=1)
    vec = near_ref[:, 3 * n : near_ref.shape[1] - m]
    row = lax.broadcasted_iota(jnp.int32, (2, vec.shape[1]), 0)
    lane = lax.broadcasted_iota(jnp.int32, (2, vec.shape[1]), 1)
    gain_ref[...] = mul((row == lane).astype(jnp.bfloat16), vec, 1, 1)
    bias_ref[...] = mul((row + 2 == lane).astype(jnp.bfloat16), vec, 1, 1)


def rows_device(
    dims,
    inputs,
    qkv_weight,
    out_weight,
    up_weight,
    down_weight,
    norm_gains,
    norm_biases,
    lengths,
    random_blocks,
    out_grad,
):
    n_dp = dims["dp"]
    n_out = n_dp // 2
    c = lax.axis_index("ctx")
    f32, bf16 = jnp.float32, jnp.bfloat16
    pair = [(0, 1), (1, 0)]

    def swap_tp(v):
        return lax.ppermute(v, "tp", pair)

    def both_tp(v, tiled=False):
        return lax.all_gather(v, "tp", axis=0, tiled=tiled)

    def swap_ctx(v):
        return lax.ppermute(v, "ctx", pair)

    def swap_dp(v, bits):
        return lax.ppermute(v, "dp", [(i, i ^ bits) for i in range(n_dp)])

    def after(v, *others):
        return lax.optimization_barrier((v,) + others)[0]

    def all_after(vs, *others):
        return list(lax.optimization_barrier(tuple(vs) + others)[: len(vs)])

    rows, width = inputs.shape
    part = rows // 2
    shard = qkv_weight.shape[1]
    cols = qkv_weight.shape[2] // 2
    units = up_weight.shape[1] // 2
    heads = cols // HD
    own_blocks = rows // BLOCK
    per = own_blocks // 2
    total_rows = 2 * rows
    extra = 4 + (-(4 * cols + 4)) % 64

    half = ((part, width), bf16)
    hbm = pl.BlockSpec(memory_space=pltpu.HBM)

    def packed(body, widths, *given):
        return call(
            body, [((shard, n), bf16) for n in widths], *given,
            scratch=[(w.shape, bf16) for w in given], copies=len(given), spec=hbm, room=60,
        )

    x_far = swap_ctx(inputs)
    w1, pack_one = packed(
        pack_first_body, (3 * cols, 4 * cols + extra), qkv_weight, norm_gains, norm_biases, out_weight.T
    )
    w1_near = [swap_dp(w1, 2 * k) for k in range(1, n_out)]
    far_one = swap_dp(pack_one, 1)
    w_up, w_down = packed(pack_second_body, (units, units), up_weight, down_weight.T)
    picks_far = swap_ctx(random_blocks)
    out_first = jnp.stack([pack_one[:, : cols + extra], far_one[:, : cols + extra]])
    out_next = swap_dp(out_first, 4)
    w1_near = all_after(w1_near, far_one, out_first)
    w1_rest = jnp.stack(w1_near)
    w1_pieces = [w1, *w1_near, far_one, swap_dp(w1_rest, 1)]
    out_pieces = [out_first, out_next]
    out_pieces.append(swap_dp(jnp.concatenate(out_pieces), 2))
    up_pieces, down_pieces = all_after([w_up[None], w_down[None]], w1_rest)
    up_pieces = [up_pieces, swap_dp(up_pieces, 4)]
    down_pieces = [down_pieces, swap_dp(down_pieces, 4)]
    e_far = swap_ctx(after(out_grad, *w1_near))

    picks = jnp.where(c == 0, jnp.stack([random_blocks, picks_far]), jnp.stack([picks_far, random_blocks]))
    picks = lax.dynamic_slice_in_dim(picks.reshape(2 * own_blocks, 2 * heads, 3), c * heads, heads, 1)
    blocks = jnp.arange(2 * own_blocks, dtype=jnp.int32)
    table, usable = block_table(blocks, lengths[0], picks)
    named = (table[..., None] == blocks) & usable[:, None, :, None]
    counts = jnp.sum(named.astype(f32), axis=2)
    counts = counts.reshape(2, 2, per, heads, 2, 2, per).transpose(3, 5, 4, 6, 1, 0, 2)
    bias = jnp.where(counts > 0, jnp.log(jnp.maximum(counts, 1.0)), -1e30)
    bias = bias.reshape(heads * 2 * own_blocks, 2 * own_blocks, 1)
    bias = jnp.broadcast_to(bias, bias.shape[:2] + (BLOCK,)).reshape(-1, total_rows)

    low = [((rows, width), bf16)]
    wide = [((rows, width), f32)]
    small = [((8, width), f32)]
    o, qkv, lse, x_all, w1_all = call(
        attend_body,
        [
            ((total_rows, cols), bf16), ((total_rows, 3 * cols), bf16), ((8, total_rows), f32),
            ((total_rows, width), bf16), ((width, 3 * cols), bf16),
        ],
        inputs, x_far, *w1_pieces, bias,
        scratch=[((heads * total_rows, total_rows), bf16), ((heads * total_rows, cols), bf16)],
        flops=0,
    )

    def sum_tp(mine, theirs):
        return call(add_tp_body, low, mine, both_tp(theirs))[0]

    mine, theirs, w_out_all, vecs = call(
        functools.partial(project_out_body, OUT_WAYS), wide + low + [((width, cols), bf16)] + small, o, *out_pieces,
        scratch=[((width, cols + extra), bf16)],
    )
    theirs, up_pieces[1], down_pieces[1] = all_after([theirs, up_pieces[1], down_pieces[1]])
    up_pieces.append(swap_dp(jnp.concatenate(up_pieces), 2))
    down_pieces.append(swap_dp(jnp.concatenate(down_pieces), 1))
    a = after(sum_tp(mine, theirs), e_far)
    a_far = swap_ctx(a)
    up_pieces.append(swap_dp(jnp.concatenate(up_pieces), 1))
    down_pieces.append(swap_dp(jnp.concatenate(down_pieces), 2))
    n1, r1, y_low = call(norm_one_body, wide + [((rows, 128), f32)] + low, x_all, a, a_far, vecs)
    flat = [((total_rows, units), bf16)]
    square = [((width, units), bf16)]
    y_all = both_tp(y_low, True)
    u, slope, w_up_all = call(ffn_body, flat * 2 + square, y_all, *up_pieces)
    theirs, w_down_all = call(functools.partial(project_body, DOWN_WAYS), low + square, u, *down_pieces)
    mine = call(part_body, wide, u, w_down_all)[0]
    m = call(add_far_body, low, mine, swap_tp(theirs))[0]
    m_far = swap_ctx(m)
    out, dz2, dm_low, grad2 = call(
        norm_two_body,
        [((part, width), bf16)] + wide + low + small,
        n1, m, m_far, out_grad, e_far, vecs,
        scratch=wide * 2,
    )

    def pairs(k, *widths):
        return [((k, shard, n), dtype) for n in widths for dtype in (f32, bf16)]

    def cut(n):
        most = n * 2 // 3 // 128 * 128
        return most, n - most

    def fold(own, got):
        return call(fold_body, pairs(own.shape[0] // 2, own.shape[2]), own, got)

    def fold_first(own, away, own2, away2):
        return call(fold_two_body, pairs(2, own.shape[2], own2.shape[2]), own, swap_dp(away, 1), own2, swap_dp(away2, 2))

    def fold_third(keep, send, bits):
        total = call(fold_last_body, [(keep.shape[1:], bf16)], keep, swap_dp(send, bits))[0]
        return total, swap_ctx(total)

    dm_all, dhid, theirs = call(
        ffn_back_body, [((total_rows, width), bf16)] + flat + low, dm_low, swap_tp(dm_low), slope, w_down_all, w_up_all
    )
    down_own, down_away = call(
        functools.partial(grad_body, (2, 1, 4)), [((n_out, shard, units), bf16)] * 2, dm_all, u, scratch=[((width, units), bf16)]
    )
    mine = call(part_body, wide, dhid, w_up_all)[0]
    d = call(add_far_body, low, after(mine, down_away), swap_tp(theirs))[0]
    d_far = swap_ctx(d)
    y_late, dhid = lax.optimization_barrier((y_all, dhid, d))[:2]
    up = call(
        functools.partial(grad_body, (1, 4, 2)), [((n_out, shard, units), bf16)] * 2, y_late, dhid, scratch=[((width, units), bf16)]
    )
    output = call(copy_body, low, both_tp(after(out, up[1]), True))[0]
    dz1, da_low = call(
        norm_one_back_body, wide + [((rows + 16, width), bf16)], dz2, d, after(d_far, up[1], output), n1, r1, vecs, grad2
    )
    last = 4 * cols + extra
    *tail, dqkv = call(
        attend_back_body,
        [((n_out, shard, n), bf16) for n in cut(last) for _ in range(2)] + [((total_rows, 3 * cols), bf16)],
        both_tp(da_low), w_out_all, qkv, o, lse, bias, x_all,
        flops=2 * 10**10,
        scratch=[
            ((total_rows, heads * total_rows), bf16),
            ((total_rows, heads * total_rows), bf16),
            ((heads * total_rows, cols), bf16),
            ((heads * total_rows, cols), bf16),
            ((width, last), bf16),
        ],
    )
    mine, theirs = call(input_body, wide + low, dqkv, w1_all)
    down_keep, down_send = fold(after(down_own, tail[0]), swap_dp(down_away, 2))
    down = fold(after(down_keep, theirs), swap_dp(down_send, 1))
    keep, send = call(fold_input_body, [((part, width), f32), half], mine, both_tp(theirs), dz1)
    up = fold(after(up[0], mine), swap_dp(up[1], 1))
    keep1, send1, keep2, send2 = fold_first(*all_after(tail[:1], send), *tail[1:])
    got1, got2 = swap_dp(send1, 2), swap_dp(send2, 1)
    dx_far = swap_ctx(send)
    keep1 = after(keep1, dx_far)
    tail = call(fold_join_body, pairs(1, last), keep1, got1, keep2, got2)
    up = fold(after(up[0], tail[0]), swap_dp(up[1], 4))
    grad_down, down_far = fold_third(*all_after(down[:1], tail[0]), down[1], 4)
    grad_up, up_far = fold_third(*up, 2)
    grad_1, far_1 = fold_third(after(tail[0], grad_down, grad_up), tail[1], 4)
    down_far = after(down_far, grad_1)
    dx = call(last_input_body, [half], keep, after(dx_far, grad_1))[0]
    input_grad = call(copy_body, low, both_tp(dx, True))[0]
    grad_1 = after(grad_1, input_grad)

    def both_ctx(g, far):
        return jnp.where(c == 0, jnp.concatenate([g, far], 1), jnp.concatenate([far, g], 1)).astype(f32)

    grad_qkv, grad_out, gains, biases = call(
        finish_body,
        [((3, shard, 2 * cols), f32), ((shard, 2 * cols), f32), ((2, shard), f32), ((2, shard), f32)],
        grad_1, far_1,
    )
    return (
        output, input_grad, grad_qkv, grad_out.T, both_ctx(grad_up, up_far), both_ctx(grad_down, down_far).T, gains, biases
    )


def solution(mesh):
    dims = dict(mesh.shape)
    fast = dims["ctx"] == 2 and dims["tp"] == 2 and dims["dp"] == 8
    step = functools.partial(rows_device, dims) if fast else per_device
    return jax.shard_map(
        step,
        mesh=mesh,
        in_specs=(
            P(("dp", "ctx"), None),
            P(None, "dp", "tp"),
            P("tp", "dp"),
            P("dp", "tp"),
            P("tp", "dp"),
            P(None, "dp"),
            P(None, "dp"),
            P("dp", None),
            P(("dp", "ctx"), "tp", None),
            P(("dp", "ctx"), None),
        ),
        out_specs=(
            P(("dp", "ctx"), None),
            P(("dp", "ctx"), None),
            P(None, "dp", "tp"),
            P("tp", "dp"),
            P("dp", "tp"),
            P("tp", "dp"),
            P(None, "dp"),
            P(None, "dp"),
        ),
        check_vma=False,
    )
```

```python
import functools
import math

import jax
import jax.numpy as jnp
from jax import lax
from jax.experimental import pallas as pl
from jax.experimental.pallas import tpu as pltpu
from jax.sharding import PartitionSpec as P

HD = 64
BLOCK = 64


eps = 1e-06


def layer_norm(values, gain, shift):
    row_mean = jnp.mean(values, axis=-1, keepdims=True)
    centred = values - row_mean
    spread = jnp.mean(centred * centred, axis=-1, keepdims=True)
    return centred * lax.rsqrt(spread + eps) * gain + shift


def gelu_tanh(values):
    return jax.nn.gelu(values, approximate=True)


def contract(form, left, right):
    return jnp.einsum(form, left, right, preferred_element_type=jnp.float32)


def block_table(blocks, lengths_row, offsets):
    seq_ends = jnp.cumsum(lengths_row)
    starts = seq_ends - lengths_row
    inside = ((blocks[:, None] >= starts[None, :]) & (blocks[:, None] < seq_ends[None, :])).astype(
        jnp.int32
    )
    seq_first = jnp.sum(inside * starts[None, :], axis=1)
    seq_count = jnp.sum(inside * lengths_row[None, :], axis=1)
    position = blocks - seq_first
    has_before = position > 0
    has_behind = position < seq_count - 1
    before = jnp.where(has_before, blocks - 1, blocks)
    behind = jnp.where(has_behind, blocks + 1, blocks)
    fixed_ids = jnp.stack([before, blocks, behind, seq_first, seq_first + 1], axis=-1)
    random_ids = seq_first[:, None, None] + offsets % seq_count[:, None, None]
    head_count = offsets.shape[1]
    key_table = jnp.concatenate(
        [jnp.broadcast_to(fixed_ids[:, None, :], (blocks.shape[0], head_count, 5)), random_ids],
        axis=-1,
    )
    always = jnp.ones_like(has_before)
    usable = jnp.stack(
        [has_before, always, has_behind, always, always] + [always] * offsets.shape[2], axis=-1
    )
    return (key_table, usable)


def scores_of(query, key_sel, usable, scale):
    raw = contract("bqhd,bhkcd->bhqkc", query, key_sel)
    return jnp.where(usable[:, None, None, :, None], raw * scale, -1e30)


def per_device(
    inputs,
    qkv_weight,
    out_weight,
    up_weight,
    down_weight,
    norm_gains,
    norm_biases,
    lengths,
    random_blocks,
    out_grad,
):
    w_qkv, w_out, w_up, w_down, gains_low, biases_low = (
        lax.all_gather(qkv_weight, "dp", axis=1, tiled=True),
        lax.all_gather(out_weight, "dp", axis=1, tiled=True),
        lax.all_gather(up_weight, "dp", axis=0, tiled=True),
        lax.all_gather(down_weight, "dp", axis=1, tiled=True),
        lax.all_gather(norm_gains, "dp", axis=1, tiled=True),
        lax.all_gather(norm_biases, "dp", axis=1, tiled=True),
    )
    gains = gains_low.astype(jnp.float32)
    biases = biases_low.astype(jnp.float32)
    rows = inputs.shape[0]
    own_blocks = rows // BLOCK
    local_width = w_qkv.shape[2]
    local_heads = local_width // HD
    scale = 1.0 / math.sqrt(HD)
    x_float = inputs.astype(jnp.float32)
    projected = contract("td,kde->kte", inputs, w_qkv)
    q_low = projected[0].astype(jnp.bfloat16)
    k_low = projected[1].astype(jnp.bfloat16)
    v_low = projected[2].astype(jnp.bfloat16)
    key_all, value_all = (
        lax.all_gather(k_low, "ctx", axis=0, tiled=True),
        lax.all_gather(v_low, "ctx", axis=0, tiled=True),
    )
    group_blocks = key_all.shape[0] // BLOCK
    first_block = lax.axis_index("ctx") * own_blocks
    blocks = first_block + jnp.arange(own_blocks, dtype=jnp.int32)
    key_table, usable = block_table(blocks, lengths[0], random_blocks)
    head_pick = jnp.arange(local_heads, dtype=jnp.int32)[None, :, None]
    key_blocks = key_all.reshape(group_blocks, BLOCK, local_heads, HD)
    value_blocks = value_all.reshape(group_blocks, BLOCK, local_heads, HD)
    key_sel = key_blocks[key_table, :, head_pick, :]
    value_sel = value_blocks[key_table, :, head_pick, :]
    query = q_low.reshape(own_blocks, BLOCK, local_heads, HD)
    scores = scores_of(query, key_sel, usable, scale)
    top = jnp.max(scores, axis=(3, 4), keepdims=True)
    log_total = top + jnp.log(jnp.sum(jnp.exp(scores - top), axis=(3, 4), keepdims=True))
    probs = jnp.exp(scores - log_total)
    probs_low = probs.astype(jnp.bfloat16)
    attended = (
        contract("bhqkc,bhkcd->bqhd", probs_low, value_sel)
        .reshape(rows, local_width)
        .astype(jnp.bfloat16)
    )
    attn_sum = lax.psum(
        jnp.dot(attended, w_out, preferred_element_type=jnp.float32).astype(jnp.bfloat16), "tp"
    ).astype(jnp.float32)
    first_sum = x_float + attn_sum
    normed, norm_pull = jax.vjp(layer_norm, first_sum, gains[0], biases[0])
    normed_low = normed.astype(jnp.bfloat16)
    hidden = jnp.dot(normed_low, w_up, preferred_element_type=jnp.float32)
    activated, gelu_pull = jax.vjp(gelu_tanh, hidden)
    act_low = activated.astype(jnp.bfloat16)
    mlp_sum = lax.psum(
        jnp.dot(act_low, w_down, preferred_element_type=jnp.float32).astype(jnp.bfloat16), "tp"
    ).astype(jnp.float32)
    second_sum = normed + mlp_sum
    result, final_pull = jax.vjp(layer_norm, second_sum, gains[1], biases[1])
    d_second, d_gain_two, d_bias_two = final_pull(out_grad.astype(jnp.float32))
    d_mlp = d_second.astype(jnp.bfloat16)
    grad_down = contract("tf,td->fd", act_low, d_mlp)
    d_act = contract("td,fd->tf", d_mlp, w_down)
    d_hidden = gelu_pull(d_act)[0].astype(jnp.bfloat16)
    grad_up = contract("td,tf->df", normed_low, d_hidden)
    d_normed = d_second + lax.psum(
        contract("tf,df->td", d_hidden, w_up).astype(jnp.bfloat16), "tp"
    ).astype(jnp.float32)
    d_first, d_gain_one, d_bias_one = norm_pull(d_normed)
    d_attn = d_first.astype(jnp.bfloat16)
    grad_proj = contract("te,td->ed", attended, d_attn)
    d_attended = (
        contract("td,ed->te", d_attn, w_out)
        .astype(jnp.bfloat16)
        .reshape(own_blocks, BLOCK, local_heads, HD)
    )
    scores = scores_of(query, key_sel, usable, scale)
    probs = jnp.exp(scores - log_total)
    probs_low = probs.astype(jnp.bfloat16)
    d_probs = contract("bqhd,bhkcd->bhqkc", d_attended, value_sel)
    d_scores = probs * (d_probs - jnp.sum(probs * d_probs, axis=(3, 4), keepdims=True))
    d_raw = (d_scores * scale).astype(jnp.bfloat16)
    d_query = (
        contract("bhqkc,bhkcd->bqhd", d_raw, key_sel)
        .reshape(rows, local_width)
        .astype(jnp.bfloat16)
    )
    d_key_sel = contract("bhqkc,bqhd->bhkcd", d_raw, query)
    d_value_sel = contract("bhqkc,bqhd->bhkcd", probs_low, d_attended)
    empty = jnp.zeros((group_blocks, BLOCK, local_heads, HD), jnp.float32)
    d_key_all = (
        empty.at[key_table, :, head_pick, :]
        .add(d_key_sel)
        .reshape(group_blocks * BLOCK, local_width)
    )
    d_value_all = (
        empty.at[key_table, :, head_pick, :]
        .add(d_value_sel)
        .reshape(group_blocks * BLOCK, local_width)
    )
    d_key, d_value = (
        lax.psum_scatter(
            d_key_all.astype(jnp.bfloat16), "ctx", scatter_dimension=0, tiled=True
        ).astype(jnp.float32),
        lax.psum_scatter(
            d_value_all.astype(jnp.bfloat16), "ctx", scatter_dimension=0, tiled=True
        ).astype(jnp.float32),
    )
    d_projected = jnp.stack([d_query, d_key.astype(jnp.bfloat16), d_value.astype(jnp.bfloat16)])
    grad_qkv = contract("td,kte->kde", inputs, d_projected)
    d_inputs = d_first + lax.psum(
        contract("kte,kde->td", d_projected, w_qkv).astype(jnp.bfloat16), "tp"
    ).astype(jnp.float32)
    grad_gains = jnp.stack([d_gain_one, d_gain_two])
    grad_biases = jnp.stack([d_bias_one, d_bias_two])
    shared = (
        lax.psum_scatter(
            grad_qkv.astype(jnp.bfloat16), "dp", scatter_dimension=1, tiled=True
        ).astype(jnp.float32),
        lax.psum_scatter(
            grad_proj.astype(jnp.bfloat16), "dp", scatter_dimension=1, tiled=True
        ).astype(jnp.float32),
        lax.psum_scatter(
            grad_up.astype(jnp.bfloat16), "dp", scatter_dimension=0, tiled=True
        ).astype(jnp.float32),
        lax.psum_scatter(
            grad_down.astype(jnp.bfloat16), "dp", scatter_dimension=1, tiled=True
        ).astype(jnp.float32),
        lax.psum_scatter(
            grad_gains.astype(jnp.bfloat16), "dp", scatter_dimension=1, tiled=True
        ).astype(jnp.float32),
        lax.psum_scatter(
            grad_biases.astype(jnp.bfloat16), "dp", scatter_dimension=1, tiled=True
        ).astype(jnp.float32),
    )
    totals = (
        lax.psum(shared[0].astype(jnp.bfloat16), "ctx").astype(jnp.float32),
        lax.psum(shared[1].astype(jnp.bfloat16), "ctx").astype(jnp.float32),
        lax.psum(shared[2].astype(jnp.bfloat16), "ctx").astype(jnp.float32),
        lax.psum(shared[3].astype(jnp.bfloat16), "ctx").astype(jnp.float32),
        lax.psum(shared[4].astype(jnp.bfloat16), "ctx").astype(jnp.float32),
        lax.psum(shared[5].astype(jnp.bfloat16), "ctx").astype(jnp.float32),
    )
    return (
        result.astype(jnp.bfloat16),
        d_inputs.astype(jnp.bfloat16),
        totals[0],
        totals[1],
        totals[2],
        totals[3],
        totals[4],
        totals[5],
    )


def mul(left, right, left_dim, right_dim):
    dims = (((left_dim,), (right_dim,)), ((), ()))
    return lax.dot_general(left, right, dims, preferred_element_type=jnp.float32)


def call(body, outs, *args, scratch=(), copies=0, spec=None, room=32, flops=0):
    spec = spec or pl.BlockSpec(memory_space=pltpu.VMEM)
    specs = [spec] * len(args)
    shapes = [jax.ShapeDtypeStruct(shape, dtype) for shape, dtype in outs]
    return pl.pallas_call(
        body,
        out_shape=shapes,
        in_specs=specs,
        out_specs=[pl.BlockSpec(memory_space=pltpu.VMEM)] * len(shapes),
        scratch_shapes=[pltpu.VMEM(shape, dtype) for shape, dtype in scratch]
        + ([pltpu.SemaphoreType.DMA((copies,))] if copies else []),
        compiler_params=pltpu.CompilerParams(vmem_limit_bytes=room << 20),
        cost_estimate=pl.CostEstimate(flops=flops, bytes_accessed=0, transcendentals=0),
    )(*args)


def head_masks(width):
    lane = lax.broadcasted_iota(jnp.int32, (1, width), 1)
    return [(lane >= h * HD) & (lane < (h + 1) * HD) for h in range(width // HD)]


def only(values, mask):
    return jnp.where(mask, values, jnp.zeros_like(values))


def biased(raw, bias):
    blocks = bias.shape[0]
    size = raw.shape[0] // blocks
    return jnp.concatenate([raw[j * size : (j + 1) * size] + bias[j : j + 1] for j in range(blocks)], axis=0)


DIRECT = (0, 2, 4, 6, 1, 3, 5, 7)
OUT_WAYS = (0, 1, 4, 5, 2, 3, 6, 7)
UP_WAYS = (0, 4, 2, 6, 1, 5, 3, 7)
DOWN_WAYS = (0, 4, 1, 5, 2, 6, 3, 7)


def place(pieces, all_ref, ways, window=0):
    width = all_ref.shape[1]
    parts = []
    for piece in pieces:
        parts += [piece] if len(piece.shape) == 2 else [piece.at[i] for i in range(piece.shape[0])]
    for part, bits in zip(parts, ways, strict=True):
        shard = part.shape[0]
        owner = lax.axis_index("dp") ^ bits
        start = window if part.shape[1] > width else 0
        all_ref[pl.ds(pl.multiple_of(owner * shard, 32), shard), :] = part[:, start : start + width]


def fetch(pairs, sems):
    copies = [pltpu.make_async_copy(src, dst, sems.at[i]) for i, (src, dst) in enumerate(pairs)]
    for copy in copies:
        copy.start()
    for copy in copies:
        copy.wait()


def own_half(src, dst):
    n = dst.shape[1]
    dst[...] = jnp.where(lax.axis_index("ctx") == 0, src[:, :n], src[:, n:])


def pack_first_body(qkv_hbm, gain_hbm, bias_hbm, out_hbm, w_ref, pack_ref, qkv, gain, bias, out, sems):
    fetch(((qkv_hbm, qkv), (gain_hbm, gain), (bias_hbm, bias), (out_hbm, out)), sems)
    c = lax.axis_index("ctx")
    n = qkv.shape[2] // 2
    for i in range(3):
        w_ref[:, i * n : (i + 1) * n] = jnp.where(c == 0, qkv[i, :, :n], qkv[i, :, n:])
    m = out.shape[1] // 2
    extra = pack_ref.shape[1] - 3 * n - m
    row = lax.broadcasted_iota(jnp.int32, (2, extra), 0)
    lane = lax.broadcasted_iota(jnp.int32, (2, extra), 1)
    cols = mul(gain[...], (row == lane).astype(jnp.bfloat16), 0, 0)
    cols = cols + mul(bias[...], (row + 2 == lane).astype(jnp.bfloat16), 0, 0)
    pack_ref[:, 0:m] = jnp.where(c == 0, out[:, :m], out[:, m:])
    pack_ref[:, m : m + extra] = cols.astype(jnp.bfloat16)
    pack_ref[:, m + extra :] = w_ref[...]


def pack_second_body(up_hbm, down_hbm, up_ref, down_ref, up, down, sems):
    fetch(((up_hbm, up), (down_hbm, down)), sems)
    own_half(up, up_ref)
    own_half(down, down_ref)


def attend_body(
    own_ref, far_ref, w0, w1, w2, w3, w4, w5, bias_ref,
    o_ref, qkv_ref, lse_ref, x_ref, w_ref, p_scr, v_scr,
):
    width = o_ref.shape[1]
    rows = x_ref.shape[0]
    part = far_ref.shape[0] // 2
    c = lax.axis_index("ctx")
    for t in range(2):
        x_ref[pl.ds((2 * t + c) * part, part), :] = own_ref[t * part : (t + 1) * part, :]
        x_ref[pl.ds((2 * t + 1 - c) * part, part), :] = far_ref[t * part : (t + 1) * part, :]
    place((w0, w1, w2, w3, w4, w5), w_ref, DIRECT, w4.shape[1] - w_ref.shape[1])
    scale = jnp.bfloat16(1.0 / math.sqrt(HD))
    w = w_ref[...]
    qkv = mul(x_ref[...], w, 1, 0).astype(jnp.bfloat16)
    qkv_ref[...] = qkv
    q, k, v = [qkv[:, i * width : (i + 1) * width] for i in range(3)]
    q = q * scale
    lse_ref[...] = jnp.zeros_like(lse_ref)
    blocks = bias_ref.shape[0] // (width // HD)
    for h, mask in enumerate(head_masks(width)):
        s = biased(mul(k, only(q, mask), 1, 1), bias_ref[h * blocks : (h + 1) * blocks, :])
        top = jnp.max(s, axis=0, keepdims=True)
        e = jnp.exp(s - top)
        total = jnp.sum(e, axis=0, keepdims=True)
        lse_ref[h : h + 1, :] = top + jnp.log(total)
        p_scr[h * rows : (h + 1) * rows, :] = (e * (1.0 / total)).astype(jnp.bfloat16)
        v_scr[h * rows : (h + 1) * rows, :] = only(v, mask)
    o_ref[...] = mul(p_scr[...], v_scr[...], 0, 0).astype(jnp.bfloat16)


def split_rows(value_of, mine_ref, theirs_ref):
    half = mine_ref.shape[0]
    t = lax.axis_index("tp")
    theirs_ref[...] = value_of(pl.ds((1 - t) * half, half)).astype(theirs_ref.dtype)
    mine_ref[...] = value_of(pl.ds(t * half, half))


def project_body(ways, o_ref, *refs):
    *pieces, theirs_ref, w_ref = refs
    place(pieces, w_ref, ways)
    rows = part_rows(theirs_ref.shape[0], False)
    theirs_ref[...] = mul(o_ref[rows, :], w_ref[...], 1, 1).astype(jnp.bfloat16)


def project_out_body(ways, o_ref, *refs):
    *pieces, mine_ref, theirs_ref, w_ref, vec_ref, scr = refs
    place(pieces, scr, ways)
    n = w_ref.shape[1]
    w_ref[...] = scr[:, 0:n]
    extra = scr.shape[1] - n
    unit = (
        lax.broadcasted_iota(jnp.int32, (8, extra), 0) == lax.broadcasted_iota(jnp.int32, (8, extra), 1)
    ).astype(jnp.bfloat16)
    vec_ref[...] = mul(unit, scr[:, n:], 1, 1)
    split_rows(lambda rows: mul(o_ref[rows, :], w_ref[...], 1, 1), mine_ref, theirs_ref)


def add_tp_body(mine_ref, both_ref, sum_ref):
    sum_ref[...] = (mine_ref[...] + both_ref[1 - lax.axis_index("tp")].astype(jnp.float32)).astype(jnp.bfloat16)


def norm_parts(z):
    centred = z - jnp.mean(z, axis=1, keepdims=True)
    r = lax.rsqrt(jnp.mean(centred * centred, axis=1, keepdims=True) + eps)
    return centred * r, r


def norm_back(e2, n, r):
    return r * (e2 - jnp.mean(e2, axis=1, keepdims=True) - n * jnp.mean(e2 * n, axis=1, keepdims=True))


def norm_one_body(x_ref, a_ref, far_ref, vec_ref, n_ref, r_ref, low_ref):
    half = n_ref.shape[0]
    z = x_ref[pl.ds(lax.axis_index("tp") * half, half), :].astype(jnp.float32)
    z = z + (a_ref[...].astype(jnp.float32) + far_ref[...].astype(jnp.float32))
    n, r = norm_parts(z)
    n_ref[...] = n
    r_ref[...] = jnp.broadcast_to(r, r_ref.shape)
    low_ref[...] = (n * vec_ref[0:1, :] + vec_ref[2:3, :]).astype(jnp.bfloat16)


def ffn_body(y_ref, w0, w1, w2, w3, u_ref, slope_ref, up_ref):
    place((w0, w1, w2, w3), up_ref, UP_WAYS)
    hid = mul(y_ref[...], up_ref[...], 1, 0)
    root = math.sqrt(2.0 / math.pi)
    square = hid * hid
    bent = jnp.tanh(root * (hid + 0.044715 * (square * hid)))
    u_ref[...] = (0.5 * hid * (1.0 + bent)).astype(jnp.bfloat16)
    slope = 0.5 * (1.0 + bent) + 0.5 * hid * (1.0 - bent * bent) * (root * (1.0 + 3 * 0.044715 * square))
    slope_ref[...] = slope.astype(jnp.bfloat16)


def norm_two_body(n1_ref, m_ref, far_ref, e_ref, e_far_ref, vec_ref, out_ref, dz_ref, low_ref, grad_ref, e_scr, out_scr):
    part = out_ref.shape[0]
    c, t = lax.axis_index("ctx"), lax.axis_index("tp")
    e_scr[pl.ds(c * part, part), :] = e_ref[pl.ds(t * part, part), :].astype(jnp.float32)
    e_scr[pl.ds((1 - c) * part, part), :] = e_far_ref[pl.ds(t * part, part), :].astype(jnp.float32)
    y1 = n1_ref[...] * vec_ref[0:1, :] + vec_ref[2:3, :]
    z = y1 + (m_ref[...].astype(jnp.float32) + far_ref[...].astype(jnp.float32))
    n, r = norm_parts(z)
    out_scr[...] = n * vec_ref[1:2, :] + vec_ref[3:4, :]
    out_ref[...] = out_scr[pl.ds(c * part, part), :].astype(jnp.bfloat16)
    e = e_scr[...]
    dz = norm_back(e * vec_ref[1:2, :], n, r)
    dz_ref[...] = dz
    low_ref[...] = dz.astype(jnp.bfloat16)
    grad_ref[...] = jnp.zeros_like(grad_ref)
    grad_ref[1:2, :] = jnp.sum(e * n, axis=0, keepdims=True)
    grad_ref[3:4, :] = jnp.sum(e, axis=0, keepdims=True)


def join(near_ref, far_ref, all_ref):
    half = near_ref.shape[0]
    t = lax.axis_index("tp")
    all_ref[pl.ds(t * half, half), :] = near_ref[...]
    all_ref[pl.ds((1 - t) * half, half), :] = far_ref[...]


def part_rows(half, mine):
    t = lax.axis_index("tp")
    return pl.ds((t if mine else 1 - t) * half, half)


def ffn_back_body(near_ref, far_ref, slope_ref, down_ref, up_ref, dm_ref, dhid_ref, theirs_ref):
    join(near_ref, far_ref, dm_ref)
    du = mul(dm_ref[...], down_ref[...], 1, 0)
    dhid_ref[...] = (du * slope_ref[...].astype(jnp.float32)).astype(jnp.bfloat16)
    theirs_ref[...] = mul(dhid_ref[part_rows(near_ref.shape[0], False), :], up_ref[...], 1, 1).astype(jnp.bfloat16)


def part_body(rows_ref, w_ref, mine_ref):
    mine_ref[...] = mul(rows_ref[part_rows(mine_ref.shape[0], True), :], w_ref[...], 1, 1)


def add_far_body(mine_ref, far_ref, sum_ref):
    sum_ref[...] = (mine_ref[...] + far_ref[...].astype(jnp.float32)).astype(jnp.bfloat16)


def deal(own_ref, away_ref, scr, order, start=0):
    one, two, three = order
    shard, width = own_ref.shape[1:]
    dp = lax.axis_index("dp")
    for i, bits in enumerate((0, three, two, two ^ three)):
        for ref, owner in ((own_ref, dp ^ bits), (away_ref, dp ^ bits ^ one)):
            part = scr[pl.ds(pl.multiple_of(owner * shard, 32), shard), start : start + width]
            ref[i] = part.astype(ref.dtype)


def grad_body(order, left_ref, right_ref, own_ref, away_ref, scr):
    scr[...] = mul(left_ref[...], right_ref[...], 0, 0).astype(scr.dtype)
    deal(own_ref, away_ref, scr, order)


def deal_two(own_ref, away_ref, own2_ref, away2_ref, scr):
    deal(own_ref, away_ref, scr, (1, 2, 4))
    deal(own2_ref, away2_ref, scr, (2, 1, 4), own_ref.shape[2])


def fold_pair(own_ref, got_ref, keep_ref, send_ref):
    half = keep_ref.shape[0]
    keep_ref[...] = own_ref[0:half].astype(jnp.float32) + got_ref[0:half].astype(jnp.float32)
    send_ref[...] = (own_ref[half:].astype(jnp.float32) + got_ref[half:].astype(jnp.float32)).astype(jnp.bfloat16)


def fold_body(own_ref, got_ref, keep_ref, send_ref):
    fold_pair(own_ref, got_ref, keep_ref, send_ref)


def fold_two_body(own_ref, got_ref, own2_ref, got2_ref, keep_ref, send_ref, keep2_ref, send2_ref):
    fold_pair(own_ref, got_ref, keep_ref, send_ref)
    fold_pair(own2_ref, got2_ref, keep2_ref, send2_ref)


def fold_join_body(own_ref, got_ref, own2_ref, got2_ref, keep_ref, send_ref):
    width = own_ref.shape[2]
    for own, got, lanes in ((own_ref, got_ref, slice(0, width)), (own2_ref, got2_ref, slice(width, keep_ref.shape[2]))):
        keep_ref[0, :, lanes] = own[0] + got[0].astype(jnp.float32)
        send_ref[0, :, lanes] = (own[1] + got[1].astype(jnp.float32)).astype(jnp.bfloat16)


def fold_last_body(own_ref, got_ref, sum_ref):
    sum_ref[...] = (own_ref[0] + got_ref[0].astype(jnp.float32)).astype(jnp.bfloat16)


def norm_one_back_body(dz2_ref, d_ref, far_ref, n_ref, r_ref, vec_ref, grad2_ref, dz_ref, low_ref):
    dy = dz2_ref[...] + (d_ref[...].astype(jnp.float32) + far_ref[...].astype(jnp.float32))
    n = n_ref[...]
    dz = norm_back(dy * vec_ref[0:1, :], n, r_ref[:, 0:1])
    dz_ref[...] = dz
    half = dz.shape[0]
    low_ref[0:half, :] = dz.astype(jnp.bfloat16)
    sums = [
        jnp.sum(dy * n, axis=0, keepdims=True), grad2_ref[1:2, :],
        jnp.sum(dy, axis=0, keepdims=True), grad2_ref[3:4, :], jnp.zeros((12, dz.shape[1]), jnp.float32),
    ]
    low_ref[half : half + 16, :] = jnp.concatenate(sums, axis=0).astype(jnp.bfloat16)


def attend_back_body(
    da_ref, w_out_ref, qkv_ref, o_ref, lse_ref, bias_ref, x_ref,
    own_ref, away_ref, own2_ref, away2_ref, all_scr,
    p_scr, dr_scr, q_scr, do_scr, grad_scr,
):
    width = o_ref.shape[1]
    rows = x_ref.shape[0]
    scale = jnp.bfloat16(1.0 / math.sqrt(HD))
    half = rows // 2
    da = jnp.concatenate([da_ref[0, 0:half, :], da_ref[1, 0:half, :]], axis=0)
    do = mul(da, w_out_ref[...], 1, 0).astype(jnp.bfloat16)
    q, k, v = [qkv_ref[:, i * width : (i + 1) * width] for i in range(3)]
    q = q * scale
    k_scaled = k * scale
    blocks = bias_ref.shape[0] // (width // HD)
    dq = jnp.zeros((rows, width), jnp.float32)
    for h, mask in enumerate(head_masks(width)):
        q_h, do_h = only(q, mask), only(do, mask)
        s = biased(mul(k, q_h, 1, 1), bias_ref[h * blocks : (h + 1) * blocks, :])
        p = jnp.exp(s - lse_ref[h : h + 1, :])
        dp = mul(v, do_h, 1, 1)
        pd = p * dp
        ds = pd - p * jnp.sum(pd, axis=0, keepdims=True)
        dr = ds.astype(jnp.bfloat16)
        p_scr[:, h * rows : (h + 1) * rows] = p.astype(jnp.bfloat16)
        dr_scr[:, h * rows : (h + 1) * rows] = dr
        q_scr[h * rows : (h + 1) * rows, :] = q_h
        do_scr[h * rows : (h + 1) * rows, :] = do_h
        dq = dq + mul(dr, only(k_scaled, mask), 0, 0)
    all_scr[:, 0:width] = dq.astype(jnp.bfloat16)
    all_scr[:, width : 2 * width] = mul(dr_scr[...], q_scr[...], 1, 0).astype(jnp.bfloat16)
    all_scr[:, 2 * width : 3 * width] = mul(p_scr[...], do_scr[...], 1, 0).astype(jnp.bfloat16)
    vec = sum(da_ref[i, half : half + 16, :].astype(jnp.float32) for i in range(2)).astype(jnp.bfloat16)
    extra = grad_scr.shape[1] - 4 * width
    unit = (
        lax.broadcasted_iota(jnp.int32, (16, extra), 0) == lax.broadcasted_iota(jnp.int32, (16, extra), 1)
    ).astype(jnp.bfloat16)
    grad_scr[...] = jnp.concatenate(
        [mul(x_ref[...], all_scr[...], 0, 0), mul(vec, unit, 0, 0), mul(da, o_ref[...], 0, 0)], axis=1
    ).astype(grad_scr.dtype)
    deal_two(own_ref, away_ref, own2_ref, away2_ref, grad_scr)


def input_body(grad_ref, w_ref, mine_ref, theirs_ref):
    split_rows(lambda rows: mul(grad_ref[rows, :], w_ref[...], 1, 1), mine_ref, theirs_ref)


def fold_input_body(mine_ref, both_ref, dz_ref, keep_ref, send_ref):
    part = keep_ref.shape[0]
    c, far = lax.axis_index("ctx"), 1 - lax.axis_index("tp")
    own, other = pl.ds(c * part, part), pl.ds((1 - c) * part, part)
    send_ref[...] = (mine_ref[other, :] + both_ref[far, other, :].astype(jnp.float32)).astype(jnp.bfloat16)
    keep_ref[...] = dz_ref[own, :] + (mine_ref[own, :] + both_ref[far, own, :].astype(jnp.float32))


def last_input_body(keep_ref, got_ref, out_ref):
    out_ref[...] = (keep_ref[...] + got_ref[...].astype(jnp.float32)).astype(jnp.bfloat16)


def copy_body(in_ref, out_ref):
    out_ref[...] = in_ref[...]


def finish_body(near_ref, far_ref, qkv_ref, out_ref, gain_ref, bias_ref):
    c = lax.axis_index("ctx")
    n = qkv_ref.shape[2] // 2
    m = out_ref.shape[1] // 2
    near, far = near_ref[...].astype(jnp.float32), far_ref[...].astype(jnp.float32)
    low, high = jnp.where(c == 0, near, far), jnp.where(c == 0, far, near)
    for i in range(3):
        qkv_ref[i] = jnp.concatenate([low[:, i * n : (i + 1) * n], high[:, i * n : (i + 1) * n]], axis=1)
    out_ref[...] = jnp.concatenate([low[:, low.shape[1] - m :], high[:, high.shape[1] - m :]], axis=1)
    vec = near_ref[:, 3 * n : near_ref.shape[1] - m]
    row = lax.broadcasted_iota(jnp.int32, (2, vec.shape[1]), 0)
    lane = lax.broadcasted_iota(jnp.int32, (2, vec.shape[1]), 1)
    gain_ref[...] = mul((row == lane).astype(jnp.bfloat16), vec, 1, 1)
    bias_ref[...] = mul((row + 2 == lane).astype(jnp.bfloat16), vec, 1, 1)


def rows_device(
    dims,
    inputs,
    qkv_weight,
    out_weight,
    up_weight,
    down_weight,
    norm_gains,
    norm_biases,
    lengths,
    random_blocks,
    out_grad,
):
    n_dp = dims["dp"]
    n_out = n_dp // 2
    c = lax.axis_index("ctx")
    f32, bf16 = jnp.float32, jnp.bfloat16
    pair = [(0, 1), (1, 0)]

    def swap_tp(v):
        return lax.ppermute(v, "tp", pair)

    def both_tp(v, tiled=False):
        return lax.all_gather(v, "tp", axis=0, tiled=tiled)

    def swap_ctx(v):
        return lax.ppermute(v, "ctx", pair)

    def swap_dp(v, bits):
        return lax.ppermute(v, "dp", [(i, i ^ bits) for i in range(n_dp)])

    def after(v, *others):
        return lax.optimization_barrier((v,) + others)[0]

    def all_after(vs, *others):
        return list(lax.optimization_barrier(tuple(vs) + others)[: len(vs)])

    rows, width = inputs.shape
    part = rows // 2
    shard = qkv_weight.shape[1]
    cols = qkv_weight.shape[2] // 2
    units = up_weight.shape[1] // 2
    heads = cols // HD
    own_blocks = rows // BLOCK
    per = own_blocks // 2
    total_rows = 2 * rows
    extra = 4 + (-(4 * cols + 4)) % 64

    half = ((part, width), bf16)
    hbm = pl.BlockSpec(memory_space=pltpu.HBM)

    def packed(body, widths, *given):
        return call(
            body, [((shard, n), bf16) for n in widths], *given,
            scratch=[(w.shape, bf16) for w in given], copies=len(given), spec=hbm, room=60,
        )

    x_far = swap_ctx(inputs)
    w1, pack_one = packed(
        pack_first_body, (3 * cols, 4 * cols + extra), qkv_weight, norm_gains, norm_biases, out_weight.T
    )
    w1_near = [swap_dp(w1, 2 * k) for k in range(1, n_out)]
    far_one = swap_dp(pack_one, 1)
    w_up, w_down = packed(pack_second_body, (units, units), up_weight, down_weight.T)
    picks_far = swap_ctx(random_blocks)
    out_first = jnp.stack([pack_one[:, : cols + extra], far_one[:, : cols + extra]])
    out_next = swap_dp(out_first, 4)
    w1_near = all_after(w1_near, far_one, out_first)
    w1_rest = jnp.stack(w1_near)
    w1_pieces = [w1, *w1_near, far_one, swap_dp(w1_rest, 1)]
    out_pieces = [out_first, out_next]
    out_pieces.append(swap_dp(jnp.concatenate(out_pieces), 2))
    up_pieces, down_pieces = all_after([w_up[None], w_down[None]], w1_rest, out_next)
    up_pieces = [up_pieces, swap_dp(up_pieces, 4)]
    down_pieces = [down_pieces, swap_dp(down_pieces, 4)]

    picks = jnp.where(c == 0, jnp.stack([random_blocks, picks_far]), jnp.stack([picks_far, random_blocks]))
    picks = lax.dynamic_slice_in_dim(picks.reshape(2 * own_blocks, 2 * heads, 3), c * heads, heads, 1)
    blocks = jnp.arange(2 * own_blocks, dtype=jnp.int32)
    table, usable = block_table(blocks, lengths[0], picks)
    named = (table[..., None] == blocks) & usable[:, None, :, None]
    counts = jnp.sum(named.astype(f32), axis=2)
    counts = counts.reshape(2, 2, per, heads, 2, 2, per).transpose(3, 5, 4, 6, 1, 0, 2)
    bias = jnp.where(counts > 0, jnp.log(jnp.maximum(counts, 1.0)), -1e30)
    bias = bias.reshape(heads * 2 * own_blocks, 2 * own_blocks, 1)
    bias = jnp.broadcast_to(bias, bias.shape[:2] + (BLOCK,)).reshape(-1, total_rows)

    low = [((rows, width), bf16)]
    wide = [((rows, width), f32)]
    small = [((8, width), f32)]
    o, qkv, lse, x_all, w1_all = call(
        attend_body,
        [
            ((total_rows, cols), bf16), ((total_rows, 3 * cols), bf16), ((8, total_rows), f32),
            ((total_rows, width), bf16), ((width, 3 * cols), bf16),
        ],
        inputs, x_far, *w1_pieces, bias,
        scratch=[((heads * total_rows, total_rows), bf16), ((heads * total_rows, cols), bf16)],
        flops=0,
    )

    def sum_tp(mine, theirs):
        return call(add_tp_body, low, mine, both_tp(theirs))[0]

    e_far = swap_ctx(after(out_grad, o))
    mine, theirs, w_out_all, vecs = call(
        functools.partial(project_out_body, OUT_WAYS), wide + low + [((width, cols), bf16)] + small, o, *out_pieces,
        scratch=[((width, cols + extra), bf16)],
    )
    theirs, up_pieces[1], down_pieces[1] = all_after([theirs, up_pieces[1], down_pieces[1]])
    up_pieces.append(swap_dp(jnp.concatenate(up_pieces), 2))
    down_pieces.append(swap_dp(jnp.concatenate(down_pieces), 1))
    a = after(sum_tp(mine, theirs), e_far)
    a_far = swap_ctx(a)
    up_pieces.append(swap_dp(jnp.concatenate(up_pieces), 1))
    down_pieces.append(swap_dp(jnp.concatenate(down_pieces), 2))
    n1, r1, y_low = call(norm_one_body, wide + [((rows, 128), f32)] + low, x_all, a, a_far, vecs)
    flat = [((total_rows, units), bf16)]
    square = [((width, units), bf16)]
    y_all = both_tp(y_low, True)
    u, slope, w_up_all = call(ffn_body, flat * 2 + square, y_all, *up_pieces)
    theirs, w_down_all = call(functools.partial(project_body, DOWN_WAYS), low + square, u, *down_pieces)
    mine = call(part_body, wide, u, w_down_all)[0]
    m = call(add_far_body, low, mine, swap_tp(theirs))[0]
    m_far = swap_ctx(m)
    out, dz2, dm_low, grad2 = call(
        norm_two_body,
        [((part, width), bf16)] + wide + low + small,
        n1, m, m_far, out_grad, e_far, vecs,
        scratch=wide * 2,
    )

    def pairs(k, *widths):
        return [((k, shard, n), dtype) for n in widths for dtype in (f32, bf16)]

    def cut(n):
        most = n * 2 // 3 // 128 * 128
        return most, n - most

    def fold(own, got):
        return call(fold_body, pairs(own.shape[0] // 2, own.shape[2]), own, got)

    def fold_first(own, away, own2, away2):
        return call(fold_two_body, pairs(2, own.shape[2], own2.shape[2]), own, swap_dp(away, 1), own2, swap_dp(away2, 2))

    def fold_third(keep, send, bits):
        total = call(fold_last_body, [(keep.shape[1:], bf16)], keep, swap_dp(send, bits))[0]
        return total, swap_ctx(total)

    dm_all, dhid, theirs = call(
        ffn_back_body, [((total_rows, width), bf16)] + flat + low, dm_low, swap_tp(dm_low), slope, w_down_all, w_up_all
    )
    down_own, down_away = call(
        functools.partial(grad_body, (2, 1, 4)), [((n_out, shard, units), bf16)] * 2, dm_all, u, scratch=[((width, units), bf16)]
    )
    mine = call(part_body, wide, dhid, w_up_all)[0]
    d = call(add_far_body, low, after(mine, down_away), swap_tp(theirs))[0]
    d_far = swap_ctx(d)
    y_late, dhid = lax.optimization_barrier((y_all, dhid, d))[:2]
    up = call(
        functools.partial(grad_body, (1, 4, 2)), [((n_out, shard, units), bf16)] * 2, y_late, dhid, scratch=[((width, units), bf16)]
    )
    output = call(copy_body, low, both_tp(after(out, up[1]), True))[0]
    dz1, da_low = call(
        norm_one_back_body, wide + [((rows + 16, width), bf16)], dz2, d, after(d_far, up[1], output), n1, r1, vecs, grad2
    )
    last = 4 * cols + extra
    *tail, dqkv = call(
        attend_back_body,
        [((n_out, shard, n), bf16) for n in cut(last) for _ in range(2)] + [((total_rows, 3 * cols), bf16)],
        both_tp(da_low), w_out_all, qkv, o, lse, bias, x_all,
        flops=2 * 10**10,
        scratch=[
            ((total_rows, heads * total_rows), bf16),
            ((total_rows, heads * total_rows), bf16),
            ((heads * total_rows, cols), bf16),
            ((heads * total_rows, cols), bf16),
            ((width, last), bf16),
        ],
    )
    mine, theirs = call(input_body, wide + low, dqkv, w1_all)
    down_keep, down_send = fold(after(down_own, tail[0]), swap_dp(down_away, 2))
    down = fold(after(down_keep, theirs), swap_dp(down_send, 1))
    keep, send = call(fold_input_body, [((part, width), f32), half], mine, both_tp(theirs), dz1)
    up = fold(after(up[0], mine), swap_dp(up[1], 1))
    keep1, send1, keep2, send2 = fold_first(*all_after(tail[:1], send), *tail[1:])
    got1, got2 = swap_dp(send1, 2), swap_dp(send2, 1)
    dx_far = swap_ctx(send)
    keep1 = after(keep1, dx_far)
    tail = call(fold_join_body, pairs(1, last), keep1, got1, keep2, got2)
    up = fold(after(up[0], tail[0]), swap_dp(up[1], 4))
    grad_down, down_far = fold_third(*all_after(down[:1], tail[0]), down[1], 4)
    grad_up, up_far = fold_third(*up, 2)
    grad_1, far_1 = fold_third(after(tail[0], grad_down, grad_up), tail[1], 4)
    down_far = after(down_far, grad_1)
    dx = call(last_input_body, [half], keep, after(dx_far, grad_1))[0]
    input_grad = call(copy_body, low, both_tp(dx, True))[0]
    grad_1 = after(grad_1, input_grad)

    def both_ctx(g, far):
        return jnp.where(c == 0, jnp.concatenate([g, far], 1), jnp.concatenate([far, g], 1)).astype(f32)

    grad_qkv, grad_out, gains, biases = call(
        finish_body,
        [((3, shard, 2 * cols), f32), ((shard, 2 * cols), f32), ((2, shard), f32), ((2, shard), f32)],
        grad_1, far_1,
    )
    return (
        output, input_grad, grad_qkv, grad_out.T, both_ctx(grad_up, up_far), both_ctx(grad_down, down_far).T, gains, biases
    )


def solution(mesh):
    dims = dict(mesh.shape)
    fast = dims["ctx"] == 2 and dims["tp"] == 2 and dims["dp"] == 8
    step = functools.partial(rows_device, dims) if fast else per_device
    return jax.shard_map(
        step,
        mesh=mesh,
        in_specs=(
            P(("dp", "ctx"), None),
            P(None, "dp", "tp"),
            P("tp", "dp"),
            P("dp", "tp"),
            P("tp", "dp"),
            P(None, "dp"),
            P(None, "dp"),
            P("dp", None),
            P(("dp", "ctx"), "tp", None),
            P(("dp", "ctx"), None),
        ),
        out_specs=(
            P(("dp", "ctx"), None),
            P(("dp", "ctx"), None),
            P(None, "dp", "tp"),
            P("tp", "dp"),
            P("dp", "tp"),
            P("tp", "dp"),
            P(None, "dp"),
            P(None, "dp"),
        ),
        check_vma=False,
    )
```
